32 devices in a mesh: tile: 8 (over y, x, core), mode: 4 (over z).
Axes of the slice: x: 2, y: 2, z: 4, core: 2. Of those that a mesh axis runs over, the one named last changes fastest.
Arguments:
- object_field: float32 [2, 2, 2048, 384], P(None, None, 'tile'), may hold values from -4 to 4
- probe: float32 [8, 2, 256, 256], P('mode'), may hold values from -4 to 4
- measured: float32 [32, 256, 256], P('tile'), may hold values from 0 to 16
- prop_phase: float32 [256, 256], replicated, may hold values from -3.140625 to 3.140625
- counts: int32 [8], P('tile'), may hold values from 1 to 4, 16 in all
- row_offset: int32 [32], P('tile'), may hold values from 0 to 255
- col_offset: int32 [32], P('tile'), may hold values from 0 to 128
Outputs:
- object_grad: float32 [2, 2, 2048, 384], P(None, None, 'tile')
- probe_grad: float32 [8, 2, 256, 256], P('mode')
The draws below stay inside these ranges and needn't reach their ends.
Inputs may be any that keep to these rules, and one draw needn't show every extreme that they name: Slot i is live for i % 4 < counts[i // 4]; some tile has all 4 slots live.
All inputs are finite; a program needn't handle non-finite values. No bound on the sum of `counts` on one device may be relied on, other than what follows from the above.
Results may differ from the reference program's by a relative error of at most 0.0003.
Values sent between devices are 32-bit elements; how exact they have to be, the bound alone decides.
A program may use at most 128 MiB of HBM per device.

```python
import math
import jax
import jax.numpy as jnp
import numpy as np
from jax import lax

WIN = 256
MODES = 8
SLICES = 2
CAP = 4
TILE_ROWS = 256
COLS = 384
ROWS = 2048
POSITIONS = 32
N_TILE = 8


def with_ends(values, key, least, largest):
    shape = values.shape
    spot = [jax.random.randint(jax.random.fold_in(key, axis), (), 0, shape[axis]) for axis in range(len(shape))]
    values = values.at[tuple(spot)].set(least)
    longest = shape.index(max(shape))
    spot[longest] = (spot[longest] + 1) % shape[longest]
    return values.at[tuple(spot)].set(largest)


def block_scale(stream_key, extent, split, least, high):
    gain, own = 1.0, jax.random.fold_in(stream_key, 6)
    for dim, parts in split:
        heights = jnp.exp(jax.random.uniform(jax.random.fold_in(own, dim), (parts,), jnp.float32, least / len(split), high / len(split)))
        gain = gain * jnp.repeat(heights, extent[dim] // parts).reshape([-1 if axis == dim else 1 for axis in range(len(extent))])
    return gain


def split_up(number_of, total, limit, slope):
    portions = [(1 << 20) // math.isqrt(grade ** slope) + 1 for grade in range(2, number_of + 1)]
    rest, given = total - limit - (number_of - 1), [1] * (number_of - 1)
    while rest > 0:
        free = [i for i in range(number_of - 1) if given[i] < limit]
        mass, left = sum([portions[i] for i in free]), rest
        for i in free:
            extra = min(limit - given[i], max(1, left * portions[i] // mass), rest)
            given[i] = given[i] + extra
            rest = rest - extra
    return np.array([limit] + given)


def ragged_sizes(own_key, amount, total, most, lean):
    if amount == 2:
        one = jax.random.randint(own_key, (), max(1, total - most), min(most, total - 1) + 1)
        return jnp.stack([one, total - one])
    sizes = jnp.asarray(split_up(amount, total, most, lean), jnp.int32)
    pairs = (amount - 1) // 2
    giver, receiver = sizes[1:1 + 2 * pairs:2], sizes[2:2 + 2 * pairs:2]
    margin = jnp.minimum(giver - 1, most - receiver)
    moved = jax.random.randint(jax.random.fold_in(own_key, 1), (pairs,), 0, 1 << 20) % (margin + 1)
    sizes = sizes.at[1:1 + 2 * pairs:2].set(giver - moved).at[2:2 + 2 * pairs:2].set(receiver + moved)
    return sizes[jax.random.permutation(jax.random.fold_in(own_key, 2), amount)]


def scatter_about(own_key, shape, spread, most, shards=(), kind=jnp.bfloat16):
    drawn = jax.random.normal(own_key, shape, jnp.float32) * spread
    if len(shards) > 0:
        drawn = block_scale(own_key, shape, shards, -0.22, 0.18) * drawn
    return jnp.clip(drawn, min=-most, max=most).astype(kind)


def setup_inputs(seed: int = 0) -> dict:
    keys = jax.random.split(jax.random.key(seed), 8)
    return {
        "object_field": scatter_about(keys[0], (SLICES, 2, ROWS, COLS), 0.7, 4.0, ((2, 8),), jnp.float32),
        "probe": scatter_about(keys[1], (MODES, 2, WIN, WIN), 0.7, 4.0, ((0, 4),), jnp.float32),
        "measured": jnp.clip(16.0 * jax.random.uniform(keys[2], (POSITIONS, WIN, WIN), jnp.float32) ** block_scale(keys[2], (POSITIONS, WIN, WIN), ((0, 8),), -0.2, 0.2), 0.0, 16.0),
        "prop_phase": jnp.clip(jax.random.uniform(keys[3], (WIN, WIN), jnp.float32, -3.140625, 3.140625), -3.140625, 3.140625),
        "counts": ragged_sizes(keys[4], N_TILE, N_TILE * CAP // 2, CAP, 2).astype(jnp.int32),
        "row_offset": with_ends(jax.random.randint(keys[5], (POSITIONS,), 0, TILE_ROWS), jax.random.fold_in(keys[5], 1), 0, TILE_ROWS - 1).astype(jnp.int32),
        "col_offset": with_ends(jax.random.randint(keys[6], (POSITIONS,), 0, COLS - WIN + 1), jax.random.fold_in(keys[6], 1), 0, COLS - WIN).astype(jnp.int32),
    }


def forward_two(field):
    return jnp.fft.fft2(field, norm="ortho")


def inverse_two(field):
    return jnp.fft.ifft2(field, norm="ortho")


def reference(object_field, probe, measured, prop_phase, counts, row_offset, col_offset):
    layers = object_field.shape[0]
    padded = jnp.pad(object_field, ((0, 0), (0, 0), (0, WIN), (0, 0)))
    obj_wave = lax.complex(padded[:, 0], padded[:, 1])
    probe_wave = lax.complex(probe[:, 0], probe[:, 1])
    kernel = lax.complex(jnp.cos(prop_phase), jnp.sin(prop_phase))
    slot_ids = jnp.arange(N_TILE * CAP, dtype=jnp.int32)
    owners = slot_ids // CAP
    live = ((slot_ids % CAP) < counts[owners]).astype(object_field.dtype)
    rows_start = (owners * TILE_ROWS + row_offset).astype(jnp.int32)
    zero_index = jnp.zeros((), jnp.int32)

    def visit(carry, inputs):
        grad_obj, grad_probe = carry
        row_start, col_start, alive, target = inputs
        start = (zero_index, row_start.astype(jnp.int32), col_start.astype(jnp.int32))
        window = lax.dynamic_slice(obj_wave, start, (layers, WIN, WIN))
        wave = probe_wave * window[0]
        before = []
        for layer in range(1, layers):
            moved = inverse_two(kernel * forward_two(wave))
            before.append(moved)
            wave = moved * window[layer]
        far_field = forward_two(wave)
        intensity = jnp.sum(jnp.real(far_field) ** 2 + jnp.imag(far_field) ** 2, axis=0)
        weight = (intensity - target) / MODES * alive
        back = inverse_two(weight * far_field)
        pieces = [None] * layers
        for layer in range(layers - 1, 0, -1):
            pieces[layer] = jnp.sum(jnp.conj(before[layer - 1]) * back, axis=0)
            back = inverse_two(jnp.conj(kernel) * forward_two(jnp.conj(window[layer]) * back))
        pieces[0] = jnp.sum(jnp.conj(probe_wave) * back, axis=0)
        grad_probe = grad_probe + jnp.conj(window[0]) * back
        current = lax.dynamic_slice(grad_obj, start, (layers, WIN, WIN))
        grad_obj = lax.dynamic_update_slice(grad_obj, current + jnp.stack(pieces), start)
        return (grad_obj, grad_probe), None

    init = (jnp.zeros_like(obj_wave), jnp.zeros_like(probe_wave))
    (grad_obj, grad_probe), _ = lax.scan(visit, init, (rows_start, col_offset, live, measured))
    grad_obj = grad_obj[:, :N_TILE * TILE_ROWS]
    object_grad = jnp.stack([jnp.real(grad_obj), jnp.imag(grad_obj)], axis=1).astype(jnp.float32)
    probe_grad = jnp.stack([jnp.real(grad_probe), jnp.imag(grad_probe)], axis=1).astype(jnp.float32)
    return object_grad, probe_grad
```

```python
import functools
import math

import jax
import jax.numpy as jnp
import numpy as np
from jax import lax
from jax.experimental import pallas as pl
from jax.experimental.pallas import tpu as pltpu
from jax.sharding import PartitionSpec as P

F32 = jnp.float32
BF16 = jnp.bfloat16
MESH = pl.DeviceIdType.MESH
BLOCKS = 16
VMEM_SPEC = pl.BlockSpec(memory_space=pltpu.VMEM)


def shifted(block, axis, distance):
    devices = range(lax.axis_size(axis))
    route = [(i - distance, i) for i in devices if i - distance in devices]
    return lax.ppermute(block, axis, route)


def dft_constants(length):
    half = length // 2
    n, k = np.arange(half)[:, None], np.arange(half)[None, :]
    sides = []
    for side in ("left", "right"):
        for way in range(2):
            for parity in range(2):
                angle = (n * (2 * k + parity) % length) * (2.0 * math.pi / length)
                real = np.cos(angle) / math.sqrt(length)
                imag = (-np.sin(angle) if way == 0 else np.sin(angle)) / math.sqrt(length)
                if (side == "left") == (way == 0):
                    real, imag = real.T, imag.T
                if side == "left":
                    table = np.block([[real, -imag], [imag, real]])
                else:
                    table = np.block([[real, imag], [-imag, real]])
                high = table.astype(BF16)
                sides += [high, (table - high.astype(np.float64)).astype(BF16)]
    return np.stack(sides).reshape(2, 2, 2, 2, length, length)


def build_tables(dft_ref, left_ref, right_ref):
    n = dft_ref.shape[-1]
    for place, low in enumerate((0, 0, 1)):
        for way in range(2):
            for parity in range(2):
                left_ref[way, parity, :, place * n:(place + 1) * n] = dft_ref[0, way, parity, low]
                right_ref[way, parity, place * n:(place + 1) * n, :] = dft_ref[1, way, parity, low]


def split(x, axis):
    high = x.astype(BF16)
    low = (x - high.astype(F32)).astype(BF16)
    return jnp.concatenate([high, low, high], axis=axis)


def one_side(real, imag, product, axis, way):
    half = real.shape[axis] // 2
    first = lambda x: lax.slice_in_dim(x, 0, half, axis=axis)
    second = lambda x: lax.slice_in_dim(x, half, 2 * half, axis=axis)
    join = lambda x, y: jnp.concatenate([x, y], axis=axis)
    if way == 0:
        even = product(split(join(first(real) + second(real), first(imag) + second(imag)), axis), 0)
        odd = product(split(join(first(real) - second(real), first(imag) - second(imag)), axis), 1)
        return join(first(even), first(odd)), join(second(even), second(odd))
    even = product(split(join(first(real), first(imag)), axis), 0)
    odd = product(split(join(second(real), second(imag)), axis), 1)
    total, rest = even + odd, even - odd
    return join(first(total), first(rest)), join(second(total), second(rest))


def transform(real, imag, left_ref, right_ref, way):
    on_left = lambda x, parity: jnp.dot(left_ref[way, parity], x, preferred_element_type=F32)
    on_right = lambda x, parity: jnp.dot(x, right_ref[way, parity], preferred_element_type=F32)
    real, imag = one_side(real, imag, on_left, 0, way)
    return one_side(real, imag, on_right, 1, way)


def to_even_odd(fields):
    n = fields.shape[-1]
    order = np.concatenate([np.arange(0, n, 2), np.arange(1, n, 2)])
    pick = jnp.asarray(np.eye(n, dtype=np.float32)[order])
    high = lax.Precision.HIGHEST
    fields = jnp.einsum("ajk,lk->ajl", fields, pick, precision=high)
    return jnp.einsum("ij,ajl->ail", pick, fields, precision=high)


def times(a, b):
    return a[0] * b[0] - a[1] * b[1], a[0] * b[1] + a[1] * b[0]


def times_conj(a, b):
    return a[0] * b[0] + a[1] * b[1], a[0] * b[1] - a[1] * b[0]


def one_hot(shape, offset, axis):
    here = lax.broadcasted_iota(jnp.int32, shape, axis) + offset
    return jnp.where(here == lax.broadcasted_iota(jnp.int32, shape, 1 - axis), 1.0, 0.0).astype(BF16)


def cut_windows(ext_ref, window_ref, row, col):
    layers, _, rows, columns = ext_ref.shape
    width = window_ref.shape[-1]
    pick_row = one_hot((width, rows), row, 0)
    pick_col = one_hot((columns, width), col, 1)
    for layer in range(layers):
        for part in range(2):
            block = ext_ref[layer, part]
            high = block.astype(BF16)
            low = (block - high.astype(F32)).astype(BF16)
            total = None
            for piece in (high, low):
                cut = jnp.dot(pick_row, piece, preferred_element_type=F32).astype(BF16)
                cut = jnp.dot(cut, pick_col, preferred_element_type=F32)
                total = cut if total is None else total + cut
            window_ref[layer, part] = total


def forward_kernel(row_ref, col_ref, own_ref, next_ref, probe_ref, prop_ref, dft_ref,
                   before_ref, far_ref, out_ref, window_out_ref, power_ref, ext_ref, left_ref, right_ref,
                   up_ref, down_ref, send_ref, sems):
    barrier = pltpu.get_barrier_semaphore()
    line = Line(lambda k: power_ref[k], out_ref, up_ref, down_ref, send_ref, sems)
    pl.semaphore_wait(barrier, line.greet(barrier))
    slots, local_modes = before_ref.shape[:2]
    width = before_ref.shape[-1]
    build_tables(dft_ref, left_ref, right_ref)
    ext_ref[:, :, :own_ref.shape[2], :] = own_ref[...]
    ext_ref[:, :, own_ref.shape[2]:, :] = next_ref[...]
    per_slot = line.blocks // slots
    rows = width // per_slot

    def one_slot(slot, carry):
        window_ref = window_out_ref.at[slot]
        cut_windows(ext_ref, window_ref, row_ref[slot], col_ref[slot])

        def one_mode(mode, carry):
            wave = times((probe_ref[mode, 0], probe_ref[mode, 1]), (window_ref[0, 0], window_ref[0, 1]))
            spectrum = transform(*wave, left_ref, right_ref, 0)
            moved = transform(*times((prop_ref[0], prop_ref[1]), spectrum), left_ref, right_ref, 1)
            before_ref[slot, mode, 0] = moved[0]
            before_ref[slot, mode, 1] = moved[1]
            wave = times(moved, (window_ref[1, 0], window_ref[1, 1]))
            far = transform(*wave, left_ref, right_ref, 0)
            far_ref[slot, mode, 0] = far[0]
            far_ref[slot, mode, 1] = far[1]
            for part in range(per_slot):
                cut = slice(part * rows, (part + 1) * rows)
                here = far[0][cut] * far[0][cut] + far[1][cut] * far[1][cut]
                k = slot * per_slot + part

                @pl.when(mode == 0)
                def _():
                    power_ref[k] = here

                @pl.when(mode > 0)
                def _():
                    power_ref[k] += here
            return carry

        return lax.fori_loop(0, local_modes, one_mode, carry)

    lax.fori_loop(0, slots, one_slot, 0)
    for t in range(line.steps()):
        line.step(t)
    line.drain()


def backward_kernel(count_ref, row_ref, col_ref, probe_ref, prop_ref, dft_ref,
                    before_ref, far_ref, power_ref, measured_ref, window_in_ref,
                    grad_ref, rim_ref, probe_grad_ref, piece_ref, total_ref, left_ref, right_ref, *, modes):
    window_ref = window_in_ref.at[0]
    slot, mode = pl.program_id(0), pl.program_id(1)
    local_modes = pl.num_programs(1)
    alive = slot < count_ref[0]
    layers, _, tile_rows, columns = grad_ref.shape
    width = piece_ref.shape[-1]

    @pl.when((slot == 0) & (mode == 0))
    def _():
        build_tables(dft_ref, left_ref, right_ref)
        total_ref[...] = jnp.zeros_like(total_ref)
        probe_grad_ref[...] = jnp.zeros_like(probe_grad_ref)

    @pl.when(mode == 0)
    def _():
        piece_ref[...] = jnp.zeros_like(piece_ref)

    @pl.when(alive)
    def _():
        weight = (power_ref[0] - measured_ref[0]) / modes
        back = transform(weight * far_ref[0, 0, 0], weight * far_ref[0, 0, 1], left_ref, right_ref, 1)
        term = times_conj((before_ref[0, 0, 0], before_ref[0, 0, 1]), back)
        piece_ref[1, 0] += term[0]
        piece_ref[1, 1] += term[1]
        inner = transform(*times_conj((window_ref[1, 0], window_ref[1, 1]), back), left_ref, right_ref, 0)
        back = transform(*times_conj((prop_ref[0], prop_ref[1]), inner), left_ref, right_ref, 1)
        term = times_conj((probe_ref[mode, 0], probe_ref[mode, 1]), back)
        piece_ref[0, 0] += term[0]
        piece_ref[0, 1] += term[1]
        term = times_conj((window_ref[0, 0], window_ref[0, 1]), back)
        probe_grad_ref[mode, 0] += term[0]
        probe_grad_ref[mode, 1] += term[1]

    @pl.when(alive & (mode == local_modes - 1))
    def _():
        row, col = row_ref[slot], col_ref[slot]
        base = pl.multiple_of(row // 8 * 8, 8)
        extra = row - base
        for layer in range(layers):
            for part in range(2):
                block = piece_ref[layer, part]
                block = jnp.concatenate([block, jnp.zeros((width, columns - width), F32)], axis=1)
                block = pltpu.roll(block, col, 1)
                block = jnp.concatenate([block, jnp.zeros((8, columns), F32)], axis=0)
                block = pltpu.roll(block, extra, 0)
                total_ref[layer, part, pl.ds(base, width + 8), :] += block

    @pl.when((slot == pl.num_programs(0) - 1) & (mode == local_modes - 1))
    def _():
        grad_ref[...] = total_ref[:, :, :tile_rows, :]
        rim_ref[...] = total_ref[:, :, tile_rows:, :]


class Line:
    def __init__(self, own, out_ref, up_ref, down_ref, send_ref, sems):
        self.own, self.out, self.up, self.down, self.send = own, out_ref, up_ref, down_ref, send_ref
        self.sems = sems
        self.n = lax.axis_size("mode")
        self.blocks = out_ref.shape[0]
        place = lax.axis_index("mode")
        left = place < self.n // 2
        self.depth = jnp.where(left, place, self.n - 1 - place)
        self.inward = jnp.where(left, place + 1, place - 1)
        self.outward = jnp.where(left, place - 1, place + 1)
        self.middle = self.depth == self.n // 2 - 1
        self.inner = self.depth > 0

    def copy(self, source, target, sent, received, device, k):
        return pltpu.make_async_remote_copy(
            src_ref=source.at[k], dst_ref=target.at[k],
            send_sem=self.sems.at[sent, k], recv_sem=self.sems.at[received, k],
            device_id={"mode": device}, device_id_type=MESH)

    def in_up(self, k):
        return self.copy(self.send, self.up, 0, 2, self.inward, k)

    def in_across(self, k):
        return self.copy(self.send, self.down, 0, 3, self.inward, k)

    def out_down(self, k):
        return self.copy(self.out, self.down, 1, 3, self.outward, k)

    def greet(self, barrier):
        pl.semaphore_signal(barrier, inc=1, device_id={"mode": self.inward}, device_id_type=MESH)

        @pl.when(self.inner)
        def _():
            pl.semaphore_signal(barrier, inc=1, device_id={"mode": self.outward}, device_id_type=MESH)

        return jnp.where(self.inner, 2, 1)

    def gather(self, k):
        @pl.when(self.inner)
        def _():
            self.in_up(k).wait_recv()
            self.send[k] = self.own(k) + self.up[k]

        @pl.when(jnp.logical_not(self.inner))
        def _():
            self.send[k] = self.own(k)

        @pl.when(self.middle)
        def _():
            self.in_across(k).start()

        @pl.when(jnp.logical_not(self.middle))
        def _():
            self.in_up(k).start()

    def spread(self, k, middle):
        self.in_across(k).wait_recv()
        self.out[k] = self.send[k] + self.down[k] if middle else self.down[k]

        @pl.when(self.inner)
        def _():
            self.out_down(k).start()

    def step(self, t):
        if t < self.blocks:
            self.gather(t)
        if 0 <= t - 2 < self.blocks:
            @pl.when(self.middle)
            def _():
                self.spread(t - 2, True)
        late = t - self.blocks
        if 0 <= late < self.blocks:
            @pl.when(jnp.logical_not(self.middle))
            def _():
                self.spread(late, False)

    def steps(self):
        return 2 * self.blocks

    def drain(self):
        for k in range(self.blocks):
            self.in_up(k).wait_send()

        @pl.when(self.inner)
        def _():
            for k in range(self.blocks):
                self.out_down(k).wait_send()


def finish_kernel(grad_ref, rim_ref, probe_ref, out_ref, probe_out_ref,
                  up_ref, down_ref, send_ref, rim_in_ref, part_ref, got_ref, sems, rim_sems, probe_sems):
    tiles = lax.axis_size("tile")
    me = lax.axis_index("tile")
    bits = tiles.bit_length() - 1
    has_next, has_last = me < tiles - 1, me > 0

    def rim_copy(k):
        return pltpu.make_async_remote_copy(
            src_ref=rim_ref.at[k], dst_ref=rim_in_ref.at[k],
            send_sem=rim_sems.at[0, k], recv_sem=rim_sems.at[1, k],
            device_id={"tile": me + 1}, device_id_type=MESH)

    def own(k):
        return send_ref[k]

    line = Line(own, out_ref, up_ref, down_ref, send_ref, sems)

    def other(bit):
        low = lax.rem(me // (1 << bit), 2)
        return me + (1 - 2 * low) * (1 << bit)

    side = lax.rem(me, 2)

    def probe_copy(step, source, target):
        return pltpu.make_async_remote_copy(
            src_ref=source, dst_ref=target,
            send_sem=probe_sems.at[0, step], recv_sem=probe_sems.at[1, step],
            device_id={"tile": other(0 if step == bits else step)}, device_id_type=MESH)

    def exchange(step):
        if step == 0:
            return probe_copy(0, probe_ref.at[1 - side], got_ref.at[0])
        if step < bits:
            return probe_copy(step, part_ref.at[step - 1], got_ref.at[step])
        return probe_copy(step, part_ref.at[bits - 1], probe_out_ref.at[side])

    barrier = pltpu.get_barrier_semaphore()
    count = line.greet(barrier)
    for bit in range(bits):
        pl.semaphore_signal(barrier, inc=1, device_id={"tile": other(bit)}, device_id_type=MESH)

    @pl.when(has_next)
    def _():
        pl.semaphore_signal(barrier, inc=1, device_id={"tile": me + 1}, device_id_type=MESH)

    @pl.when(has_last)
    def _():
        pl.semaphore_signal(barrier, inc=1, device_id={"tile": me - 1}, device_id_type=MESH)

    pl.semaphore_wait(barrier, count + bits + has_next.astype(jnp.int32) + has_last.astype(jnp.int32))

    exchange(0).start()

    @pl.when(has_next)
    def _():
        for k in range(line.blocks):
            rim_copy(k).start()

    for t in range(line.steps()):
        if t < line.blocks:
            @pl.when(has_last)
            def _():
                rim_copy(t).wait_recv()
                send_ref[t] = grad_ref[t] + rim_in_ref[t]

            @pl.when(jnp.logical_not(has_last))
            def _():
                send_ref[t] = grad_ref[t]
        line.step(t)
        bit = 0 if t == 1 else (t - 4) // 5
        if t == 1 or (t % 5 == 4 and 0 < bit < bits):
            exchange(bit).wait_recv()
            part_ref[bit] = (probe_ref[side] if bit == 0 else part_ref[bit - 1]) + got_ref[bit]
            exchange(bit + 1).start()
    probe_out_ref[side] = part_ref[bits - 1]
    exchange(bits).wait_recv()
    for step in range(bits + 1):
        exchange(step).wait_send()
    line.drain()

    @pl.when(has_next)
    def _():
        for k in range(line.blocks):
            rim_copy(k).wait_send()


def finish(grad, rim, grad_probe):
    bits = lax.axis_size("tile").bit_length() - 1
    blocked = (BLOCKS, -1, grad.shape[-1])
    own, edge = grad.reshape(blocked), rim.reshape(blocked)
    halves = grad_probe.reshape(2, -1, grad_probe.shape[-1])
    buffer = pltpu.VMEM(own.shape, F32)
    parts = pltpu.VMEM((bits, *halves.shape[1:]), F32)
    object_grad, probe_grad = pl.pallas_call(
        finish_kernel,
        out_shape=(jax.ShapeDtypeStruct(own.shape, F32), jax.ShapeDtypeStruct(halves.shape, F32)),
        in_specs=[VMEM_SPEC] * 3,
        out_specs=(VMEM_SPEC, VMEM_SPEC),
        scratch_shapes=[buffer, buffer, buffer, buffer, parts, parts,
                        pltpu.SemaphoreType.DMA((4, BLOCKS)), pltpu.SemaphoreType.DMA((2, BLOCKS)),
                        pltpu.SemaphoreType.DMA((2, bits + 1))],
        compiler_params=pltpu.CompilerParams(collective_id=1, has_side_effects=True, vmem_limit_bytes=60 << 20),
        name="finish",
    )(own, edge, halves)
    return object_grad.reshape(grad.shape), probe_grad.reshape(grad_probe.shape)


def per_device(object_field, probe, measured, prop_phase, counts, row_offset, col_offset):
    layers, _, tile_rows, columns = object_field.shape
    width = probe.shape[-1]
    local_modes = probe.shape[0]
    modes = local_modes * lax.axis_size("mode")
    slots = row_offset.shape[0]
    next_rows = shifted(object_field, "tile", -1)
    dft = jnp.asarray(dft_constants(width))
    spectral = jnp.concatenate([jnp.cos(prop_phase)[None], jnp.sin(prop_phase)[None], measured])
    spectral = to_even_odd(spectral)
    prop, measured = spectral[:2], spectral[2:]

    per_mode = pl.BlockSpec((1, 1, 2, width, width), lambda s, m, *_: (s, m, 0, 0, 0))
    per_slot = pl.BlockSpec((1, width, width), lambda s, m, *_: (s, 0, 0))
    ext_shape = pltpu.VMEM((layers, 2, tile_rows + width, columns), F32)
    window_shape = pltpu.VMEM((layers, 2, width, width), F32)
    table_shapes = [pltpu.VMEM((2, 2, width, 3 * width), BF16), pltpu.VMEM((2, 2, 3 * width, width), BF16)]
    per_window = pl.BlockSpec((1, layers, 2, width, width), lambda s, m, *_: (s, 0, 0, 0, 0))
    field = jax.ShapeDtypeStruct((slots, local_modes, 2, width, width), F32)
    params = pltpu.CompilerParams(dimension_semantics=("arbitrary", "arbitrary"), vmem_limit_bytes=60 << 20)

    blocked = (BLOCKS, slots * width // BLOCKS, width)
    buffer = pltpu.VMEM(blocked, F32)
    smem = pl.BlockSpec(memory_space=pltpu.SMEM)
    before, far, power, windows = pl.pallas_call(
        forward_kernel,
        out_shape=(field, field, jax.ShapeDtypeStruct(blocked, F32),
                   jax.ShapeDtypeStruct((slots, layers, 2, width, width), F32)),
        in_specs=[smem, smem] + [VMEM_SPEC] * 5,
        out_specs=(VMEM_SPEC,) * 4,
        scratch_shapes=[buffer, ext_shape, *table_shapes, buffer, buffer, buffer,
                        pltpu.SemaphoreType.DMA((4, BLOCKS))],
        compiler_params=pltpu.CompilerParams(collective_id=0, has_side_effects=True, vmem_limit_bytes=60 << 20),
        name="forward",
    )(row_offset, col_offset, object_field, next_rows, probe, prop, dft)
    power = power.reshape(slots, width, width)

    whole = lambda shape: pl.BlockSpec(shape, lambda s, m, *_: (0,) * len(shape))
    grad, rim, grad_probe = pl.pallas_call(
        functools.partial(backward_kernel, modes=modes),
        out_shape=(
            jax.ShapeDtypeStruct(object_field.shape, F32),
            jax.ShapeDtypeStruct((layers, 2, width, columns), F32),
            jax.ShapeDtypeStruct(probe.shape, F32),
        ),
        grid_spec=pltpu.PrefetchScalarGridSpec(
            num_scalar_prefetch=3,
            grid=(slots, local_modes),
            in_specs=[VMEM_SPEC] * 3 + [per_mode, per_mode, per_slot, per_slot, per_window],
            out_specs=(whole(object_field.shape), whole((layers, 2, width, columns)), whole(probe.shape)),
            scratch_shapes=[window_shape, ext_shape, *table_shapes],
        ),
        compiler_params=params,
        name="backward",
    )(counts, row_offset, col_offset, probe, prop, dft, before, far, power, measured, windows)

    return finish(grad, rim, grad_probe)


def solution(mesh):
    placed = (
        P(None, None, "tile", None),
        P("mode", None, None, None),
        P("tile", None, None),
        P(),
        P("tile"),
        P("tile"),
        P("tile"),
    )
    return jax.shard_map(
        per_device,
        mesh=mesh,
        in_specs=placed,
        out_specs=(P(None, None, "tile", None), P("mode", None, None, None)),
        check_vma=False,
    )
```

```python
import functools
import math

import jax
import jax.numpy as jnp
import numpy as np
from jax import lax
from jax.experimental import pallas as pl
from jax.experimental.pallas import tpu as pltpu
from jax.sharding import PartitionSpec as P

F32 = jnp.float32
BF16 = jnp.bfloat16
MESH = pl.DeviceIdType.MESH
BLOCKS = 16
VMEM_SPEC = pl.BlockSpec(memory_space=pltpu.VMEM)


def shifted(block, axis, distance):
    devices = range(lax.axis_size(axis))
    route = [(i - distance, i) for i in devices if i - distance in devices]
    return lax.ppermute(block, axis, route)


def dft_constants(length):
    half = length // 2
    n, k = np.arange(half)[:, None], np.arange(half)[None, :]
    sides = []
    for side in ("left", "right"):
        for way in range(2):
            for parity in range(2):
                angle = (n * (2 * k + parity) % length) * (2.0 * math.pi / length)
                real = np.cos(angle) / math.sqrt(length)
                imag = (-np.sin(angle) if way == 0 else np.sin(angle)) / math.sqrt(length)
                if (side == "left") == (way == 0):
                    real, imag = real.T, imag.T
                if side == "left":
                    table = np.block([[real, -imag], [imag, real]])
                else:
                    table = np.block([[real, imag], [-imag, real]])
                high = table.astype(BF16)
                sides += [high, (table - high.astype(np.float64)).astype(BF16)]
    tables = np.stack(sides).reshape(2, 2, 2, 2, length, length)
    left, right = ([[[table[0], table[0], table[1]] for table in way] for way in side] for side in tables)
    return (np.stack([[np.concatenate(table, axis=1) for table in way] for way in left]),
            np.stack([[np.concatenate(table, axis=0) for table in way] for way in right]))


def split(x, axis):
    high = x.astype(BF16)
    low = (x - high.astype(F32)).astype(BF16)
    return jnp.concatenate([high, low, high], axis=axis)


def one_side(real, imag, product, axis, way):
    half = real.shape[axis] // 2
    first = lambda x: lax.slice_in_dim(x, 0, half, axis=axis)
    second = lambda x: lax.slice_in_dim(x, half, 2 * half, axis=axis)
    join = lambda x, y: jnp.concatenate([x, y], axis=axis)
    if way == 0:
        even = product(split(join(first(real) + second(real), first(imag) + second(imag)), axis), 0)
        odd = product(split(join(first(real) - second(real), first(imag) - second(imag)), axis), 1)
        return join(first(even), first(odd)), join(second(even), second(odd))
    even = product(split(join(first(real), first(imag)), axis), 0)
    odd = product(split(join(second(real), second(imag)), axis), 1)
    total, rest = even + odd, even - odd
    return join(first(total), first(rest)), join(second(total), second(rest))


def transform(real, imag, left_ref, right_ref, way):
    on_left = lambda x, parity: jnp.dot(left_ref[way, parity], x, preferred_element_type=F32)
    on_right = lambda x, parity: jnp.dot(x, right_ref[way, parity], preferred_element_type=F32)
    real, imag = one_side(real, imag, on_left, 0, way)
    return one_side(real, imag, on_right, 1, way)


def times(a, b):
    return a[0] * b[0] - a[1] * b[1], a[0] * b[1] + a[1] * b[0]


def times_conj(a, b):
    return a[0] * b[0] + a[1] * b[1], a[0] * b[1] - a[1] * b[0]


def one_hot(condition):
    return jnp.where(condition, 1.0, 0.0).astype(BF16)


def shift_pick(shape, offset, axis):
    here = lax.broadcasted_iota(jnp.int32, shape, axis) + offset
    return one_hot(here == lax.broadcasted_iota(jnp.int32, shape, 1 - axis))


def pieces(x, number):
    parts = []
    for _ in range(number):
        parts.append(x.astype(BF16))
        x = x - parts[-1].astype(F32)
    return parts


def select(x, pick, number):
    total = None
    for piece in pieces(x, number):
        part = jnp.dot(piece, pick, preferred_element_type=F32)
        total = part if total is None else total + part
    return total


def to_even_odd(field):
    n = field.shape[-1]
    source = lax.broadcasted_iota(jnp.int32, (n, n), 0)
    place = lax.broadcasted_iota(jnp.int32, (n, n), 1)
    half = n // 2
    pick_right = one_hot(source == jnp.where(place < half, 2 * place, 2 * place - (n - 1)))
    pick_left = one_hot(place == jnp.where(source < half, 2 * source, 2 * source - (n - 1)))
    rows = None
    for piece in pieces(field, 3):
        part = jnp.dot(pick_left, piece, preferred_element_type=F32)
        rows = part if rows is None else rows + part
    return select(rows, pick_right, 3)


class Line:
    def __init__(self, own, out_ref, up_ref, down_ref, send_ref, sems):
        self.own, self.out, self.up, self.down, self.send = own, out_ref, up_ref, down_ref, send_ref
        self.sems = sems
        self.n = lax.axis_size("mode")
        self.blocks = out_ref.shape[0]
        place = lax.axis_index("mode")
        left = place < self.n // 2
        self.depth = jnp.where(left, place, self.n - 1 - place)
        self.inward = jnp.where(left, place + 1, place - 1)
        self.outward = jnp.where(left, place - 1, place + 1)
        self.middle = self.depth == self.n // 2 - 1
        self.inner = self.depth > 0

    def copy(self, source, target, sent, received, device, k):
        return pltpu.make_async_remote_copy(
            src_ref=source.at[k], dst_ref=target.at[k],
            send_sem=self.sems.at[sent, k], recv_sem=self.sems.at[received, k],
            device_id={"mode": device}, device_id_type=MESH)

    def in_up(self, k):
        return self.copy(self.send, self.up, 0, 2, self.inward, k)

    def in_across(self, k):
        return self.copy(self.send, self.down, 0, 3, self.inward, k)

    def out_down(self, k):
        return self.copy(self.out, self.out, 1, 3, self.outward, k)

    def greet(self, barrier):
        pl.semaphore_signal(barrier, inc=1, device_id={"mode": self.inward}, device_id_type=MESH)

        @pl.when(self.inner)
        def _():
            pl.semaphore_signal(barrier, inc=1, device_id={"mode": self.outward}, device_id_type=MESH)

        return jnp.where(self.inner, 2, 1)

    def forward(self, k):
        @pl.when(self.middle)
        def _():
            self.in_across(k).start()

        @pl.when(jnp.logical_not(self.middle))
        def _():
            self.in_up(k).start()

    def gather_outer(self, k):
        @pl.when(jnp.logical_not(self.inner))
        def _():
            self.send[k] = self.own(k)
            self.forward(k)

    def gather_inner(self, k):
        @pl.when(self.inner)
        def _():
            self.in_up(k).wait_recv()
            self.send[k] = self.own(k) + self.up[k]
            self.forward(k)

    def spread_middle(self, k):
        @pl.when(self.middle)
        def _():
            self.in_across(k).wait_recv()
            self.out[k] = self.send[k] + self.down[k]

            @pl.when(self.inner)
            def _():
                self.out_down(k).start()

    def spread_outer(self, k):
        @pl.when(jnp.logical_not(self.middle))
        def _():
            self.in_across(k).wait_recv()

            @pl.when(self.inner)
            def _():
                self.out_down(k).start()

    def drain(self):
        def one(k, carry):
            self.in_up(k).wait_send()

            @pl.when(self.inner)
            def _():
                self.out_down(k).wait_send()
            return carry
        lax.fori_loop(0, self.blocks, one, 0)


def ptycho_kernel(count_ref, row_ref, col_ref, own_ref, probe_ref, phase_ref, measured_ref, left_ref, right_ref,
                  out_ref, probe_out_ref,
                  ext_ref, prop_ref, target_ref, window_ref, before_ref, far_ref, part_power_ref, power_ref,
                  power_up_ref, power_down_ref, power_send_ref, piece_ref, total_ref, probe_grad_ref,
                  up_ref, down_ref, send_ref, rim_in_ref, part_ref, got_ref,
                  halo_sems, power_sems, sems, rim_sems, probe_sems):
    tiles = lax.axis_size("tile")
    me = lax.axis_index("tile")
    bits = tiles.bit_length() - 1
    has_next, has_last = me < tiles - 1, me > 0
    slots, layers = window_ref.shape[0], window_ref.shape[1]
    local_modes = probe_ref.shape[0]
    modes = local_modes * lax.axis_size("mode")
    width = probe_ref.shape[-1]
    tile_rows, columns = own_ref.shape[2:]
    per_slot = BLOCKS // slots
    slot_rows = width // per_slot
    per_layer = BLOCKS // layers
    per_part = per_layer // 2
    block_rows = tile_rows // per_part

    def place(k):
        row = k % per_part * block_rows
        return k // per_layer, k // per_part % 2, row

    def stored(k):
        return (layers - 1 - k // per_layer) * per_layer + k % per_layer

    def halo(layer, part):
        return pltpu.make_async_remote_copy(
            src_ref=own_ref.at[layer, part, pl.ds(0, width)], dst_ref=ext_ref.at[layer, part, pl.ds(tile_rows, width)],
            send_sem=halo_sems.at[0, layer, part], recv_sem=halo_sems.at[1, layer, part],
            device_id={"tile": me - 1}, device_id_type=MESH)

    def rim_copy(k):
        layer, part, row = place(k)
        return pltpu.make_async_remote_copy(
            src_ref=total_ref.at[layer, part, pl.ds(tile_rows + row, block_rows)], dst_ref=rim_in_ref.at[k],
            send_sem=rim_sems.at[0, k], recv_sem=rim_sems.at[1, k],
            device_id={"tile": me + 1}, device_id_type=MESH)

    def other(bit):
        low = lax.rem(me // (1 << bit), 2)
        return me + (1 - 2 * low) * (1 << bit)

    side = lax.rem(me, 2)

    def probe_copy(step, source, target):
        return pltpu.make_async_remote_copy(
            src_ref=source, dst_ref=target,
            send_sem=probe_sems.at[0, step], recv_sem=probe_sems.at[1, step],
            device_id={"tile": other(0 if step == bits else step)}, device_id_type=MESH)

    def exchange(step):
        if step == 0:
            return probe_copy(0, probe_grad_ref.at[1 - side], got_ref.at[0])
        if step < bits:
            return probe_copy(step, part_ref.at[step - 1], got_ref.at[step])
        return probe_copy(step, part_ref.at[bits - 1], probe_out_ref.at[side])

    power_line = Line(lambda k: part_power_ref[k], power_ref, power_up_ref, power_down_ref, power_send_ref, power_sems)

    def own(k):
        layer, part, row = place(k)
        return total_ref[layer, part, row:row + block_rows, :]

    line = Line(own, out_ref, up_ref, down_ref, send_ref, sems)

    barrier = pltpu.get_barrier_semaphore()
    count = line.greet(barrier)
    for bit in range(bits):
        pl.semaphore_signal(barrier, inc=1, device_id={"tile": other(bit)}, device_id_type=MESH)

    @pl.when(has_next)
    def _():
        pl.semaphore_signal(barrier, inc=1, device_id={"tile": me + 1}, device_id_type=MESH)

    @pl.when(has_last)
    def _():
        pl.semaphore_signal(barrier, inc=1, device_id={"tile": me - 1}, device_id_type=MESH)

    pl.semaphore_wait(barrier, count + bits + has_next.astype(jnp.int32) + has_last.astype(jnp.int32))

    @pl.when(has_last)
    def _():
        for layer in range(layers):
            for part in range(2):
                halo(layer, part).start()

    ext_ref[:, :, :tile_rows, :] = own_ref[...]

    @pl.when(jnp.logical_not(has_next))
    def _():
        ext_ref[:, :, tile_rows:, :] = jnp.zeros((layers, 2, width, columns), F32)

    phase = to_even_odd(phase_ref[...])
    prop_ref[0] = jnp.cos(phase)
    prop_ref[1] = jnp.sin(phase)

    def order(slot, carry):
        target_ref[slot] = to_even_odd(measured_ref[slot])
        return carry
    lax.fori_loop(0, slots, order, 0)
    total_ref[...] = jnp.zeros_like(total_ref)
    probe_grad_ref[...] = jnp.zeros_like(probe_grad_ref)

    @pl.when(has_next)
    def _():
        for layer in range(layers):
            for part in range(2):
                halo(layer, part).wait_recv()

    def cut_windows(slot):
        pick_row = shift_pick((width, tile_rows + width), row_ref[slot], 0)
        pick_col = shift_pick((columns, width), col_ref[slot], 1)
        for layer in range(layers):
            for part in range(2):
                total = None
                for piece in pieces(ext_ref[layer, part], 2):
                    cut = jnp.dot(pick_row, piece, preferred_element_type=F32).astype(BF16)
                    cut = jnp.dot(cut, pick_col, preferred_element_type=F32)
                    total = cut if total is None else total + cut
                window_ref[slot, layer, part] = total

    def put_back(slot, layer):
        pick_row = shift_pick((tile_rows + width, width), row_ref[slot], 1)
        pick_col = shift_pick((width, columns), col_ref[slot], 0)
        for part in range(2):
            total = total_ref[layer, part]
            for piece in pieces(piece_ref[part], 2):
                cut = jnp.dot(piece, pick_col, preferred_element_type=F32).astype(BF16)
                total = total + jnp.dot(pick_row, cut, preferred_element_type=F32)
            total_ref[layer, part] = total

    lag_gather, lag_middle, lag_outer = 5, 8, 11

    def within(k, blocks, action):
        if isinstance(k, int):
            if 0 <= k < blocks:
                action(k)
        else:
            @pl.when((k >= 0) & (k < blocks))
            def _():
                action(k)

    def power_hook(q):
        within(q - lag_gather, BLOCKS, power_line.gather_inner)
        within(q - lag_middle, BLOCKS, power_line.spread_middle)
        within(q - lag_outer, BLOCKS, power_line.spread_outer)

    def forward_slot(slot, carry):
        cut_windows(slot)

        def forward_mode(mode, carry):
            q = (slot * local_modes + mode) * (per_slot // local_modes)
            wave = times((probe_ref[mode, 0], probe_ref[mode, 1]), (window_ref[slot, 0, 0], window_ref[slot, 0, 1]))
            spectrum = transform(*wave, left_ref, right_ref, 0)
            hooks = per_slot // local_modes
            for h in range(hooks // 2):
                power_hook(q + h)
            moved = transform(*times((prop_ref[0], prop_ref[1]), spectrum), left_ref, right_ref, 1)
            before_ref[slot, mode, 0] = moved[0]
            before_ref[slot, mode, 1] = moved[1]
            for h in range(hooks // 2, hooks):
                power_hook(q + h)
            wave = times(moved, (window_ref[slot, 1, 0], window_ref[slot, 1, 1]))
            far = transform(*wave, left_ref, right_ref, 0)
            far_ref[slot, mode, 0] = far[0]
            far_ref[slot, mode, 1] = far[1]
            for part in range(per_slot):
                cut = slice(part * slot_rows, (part + 1) * slot_rows)
                here = far[0][cut] * far[0][cut] + far[1][cut] * far[1][cut]
                k = slot * per_slot + part

                @pl.when(mode == 0)
                def _():
                    part_power_ref[k] = here

                @pl.when(mode > 0)
                def _():
                    part_power_ref[k] += here
            return carry

        lax.fori_loop(0, local_modes, forward_mode, carry)
        for part in range(per_slot):
            power_line.gather_outer(slot * per_slot + part)
        return carry

    lax.fori_loop(0, slots, forward_slot, 0)
    hooks = [BLOCKS]

    def next_power_hook():
        power_hook(hooks[0])
        hooks[0] += 1

    def first_back(slot, hook):
        live = jnp.where(jnp.full((width, width), count_ref[0], jnp.int32) > slot, 1.0 / modes, 0.0)
        power = power_ref[slot * per_slot:(slot + 1) * per_slot].reshape(width, width)
        target_ref[slot] = (power - target_ref[slot]) * live
        for mode in range(local_modes):
            weight = target_ref[slot]
            back = transform(weight * far_ref[slot, mode, 0], weight * far_ref[slot, mode, 1], left_ref, right_ref, 1)
            term = times_conj((before_ref[slot, mode, 0], before_ref[slot, mode, 1]), back)
            for part in range(2):
                far_ref[slot, mode, part] = back[part]
                if mode == 0:
                    piece_ref[part] = term[part]
                else:
                    piece_ref[part] += term[part]
            hook()
        put_back(slot, 1)

    def second_back(slot, hook):
        for mode in range(local_modes):
            back = far_ref[slot, mode, 0], far_ref[slot, mode, 1]
            inner = transform(*times_conj((window_ref[slot, 1, 0], window_ref[slot, 1, 1]), back), left_ref, right_ref, 0)
            hook()
            back = transform(*times_conj((prop_ref[0], prop_ref[1]), inner), left_ref, right_ref, 1)
            term = times_conj((probe_ref[mode, 0], probe_ref[mode, 1]), back)
            grad = times_conj((window_ref[slot, 0, 0], window_ref[slot, 0, 1]), back)
            for part in range(2):
                if mode == 0:
                    piece_ref[part] = term[part]
                else:
                    piece_ref[part] += term[part]
                flat = mode * 2 + part
                first = flat % local_modes * width
                probe_grad_ref[flat // local_modes, first:first + width, :] += grad[part]
            hook()
        put_back(slot, 0)

    def ready(slot):
        while hooks[0] <= (slot + 1) * per_slot - 1 + lag_outer:
            next_power_hook()

    early = min(2, slots - 1)
    for slot in range(slots - 1):
        ready(slot)
        first_back(slot, next_power_hook)
        if slot == 0 and early > 0:
            second_back(0, next_power_hook)
    for slot in range(1, early):
        second_back(slot, next_power_hook)
    ready(slots - 1)
    first_back(slots - 1, next_power_hook)
    while hooks[0] < BLOCKS + lag_outer:
        next_power_hook()

    def send_rim(layer):
        @pl.when(has_next)
        def _():
            for k in range(layer * per_layer, (layer + 1) * per_layer):
                rim_copy(k).start()

    def add_rim(k):
        @pl.when(has_last)
        def _():
            rim_copy(k).wait_recv()
            layer, part, row = place(k)
            total_ref[layer, part, row:row + block_rows, :] += rim_in_ref[k]

    def line_hook(h):
        if 0 <= h - 2 < BLOCKS:
            add_rim(stored(h - 2))
            line.gather_outer(stored(h - 2))
        if 0 <= h - 4 < BLOCKS:
            line.gather_inner(stored(h - 4))
        if 0 <= h - 7 < BLOCKS:
            line.spread_middle(stored(h - 7))
        if 0 <= h - 10 < BLOCKS:
            line.spread_outer(stored(h - 10))

    hooks = [0]

    def next_line_hook():
        if hooks[0] < per_layer:
            line_hook(hooks[0])
            hooks[0] += 1

    for layer in range(layers - 1, 0, -1):
        send_rim(layer)
    for slot in range(early, slots):
        second_back(slot, next_line_hook)
    send_rim(0)
    exchange(0).start()
    for h in range(hooks[0], BLOCKS + 10):
        line_hook(h)
        late = h - per_layer
        bit = late // 5
        if late % 5 == 1 and 0 <= bit < bits:
            exchange(bit).wait_recv()
            part_ref[bit] = (probe_grad_ref[side] if bit == 0 else part_ref[bit - 1]) + got_ref[bit]
            exchange(bit + 1).start()
    probe_out_ref[side] = part_ref[bits - 1]
    exchange(bits).wait_recv()
    for step in range(bits + 1):
        exchange(step).wait_send()
    power_line.drain()
    line.drain()

    @pl.when(has_next)
    def _():
        for k in range(BLOCKS):
            rim_copy(k).wait_send()

    @pl.when(has_last)
    def _():
        for layer in range(layers):
            for part in range(2):
                halo(layer, part).wait_send()


def per_device(object_field, probe, measured, prop_phase, counts, row_offset, col_offset):
    layers, _, tile_rows, columns = object_field.shape
    width = probe.shape[-1]
    local_modes = probe.shape[0]
    slots = row_offset.shape[0]
    bits = lax.axis_size("tile").bit_length() - 1
    left, right = (jnp.asarray(table) for table in dft_constants(width))
    smem = pl.BlockSpec(memory_space=pltpu.SMEM)
    field = pltpu.VMEM((slots, local_modes, 2, width, width), F32)
    power = pltpu.VMEM((BLOCKS, slots * width // BLOCKS, width), F32)
    own_blocks = (BLOCKS, layers * 2 * tile_rows // BLOCKS, columns)
    block = pltpu.VMEM(own_blocks, F32)
    ext = pltpu.VMEM((layers, 2, tile_rows + width, columns), F32)
    halves = (2, local_modes * width, width)
    parts = pltpu.VMEM((bits, *halves[1:]), F32)
    dma = pltpu.SemaphoreType.DMA
    object_grad, probe_grad = pl.pallas_call(
        ptycho_kernel,
        out_shape=(jax.ShapeDtypeStruct(own_blocks, F32), jax.ShapeDtypeStruct(halves, F32)),
        in_specs=[smem] * 3 + [VMEM_SPEC] * 6,
        out_specs=(VMEM_SPEC, VMEM_SPEC),
        scratch_shapes=[
            ext, pltpu.VMEM((2, width, width), F32), pltpu.VMEM((slots, width, width), F32),
            pltpu.VMEM((slots, layers, 2, width, width), F32), field, field, power, power,
            power, power, power, pltpu.VMEM((2, width, width), F32),
            ext, pltpu.VMEM(halves, F32),
            block, block, block, block, parts, parts,
            dma((2, layers, 2)), dma((4, BLOCKS)), dma((4, BLOCKS)), dma((2, BLOCKS)), dma((2, bits + 1))],
        compiler_params=pltpu.CompilerParams(collective_id=0, has_side_effects=True, vmem_limit_bytes=62 << 20),
        name="ptycho",
    )(counts, row_offset, col_offset, object_field, probe, prop_phase, measured, left, right)
    return object_grad.reshape(object_field.shape), probe_grad.reshape(probe.shape)


def solution(mesh):
    placed = (
        P(None, None, "tile", None),
        P("mode", None, None, None),
        P("tile", None, None),
        P(),
        P("tile"),
        P("tile"),
        P("tile"),
    )
    return jax.shard_map(
        per_device,
        mesh=mesh,
        in_specs=placed,
        out_specs=(P(None, None, "tile", None), P("mode", None, None, None)),
        check_vma=False,
    )
```

```python
import functools
import math

import jax
import jax.numpy as jnp
import numpy as np
from jax import lax
from jax.experimental import pallas as pl
from jax.experimental.pallas import tpu as pltpu
from jax.sharding import PartitionSpec as P

F32 = jnp.float32
BF16 = jnp.bfloat16
MESH = pl.DeviceIdType.MESH
BLOCKS = 16
VMEM_SPEC = pl.BlockSpec(memory_space=pltpu.VMEM)


def shifted(block, axis, distance):
    devices = range(lax.axis_size(axis))
    route = [(i - distance, i) for i in devices if i - distance in devices]
    return lax.ppermute(block, axis, route)


def dft_constants(length):
    half = length // 2
    n, k = np.arange(half)[:, None], np.arange(half)[None, :]
    sides = []
    for side in ("left", "right"):
        for way in range(2):
            for parity in range(2):
                angle = (n * (2 * k + parity) % length) * (2.0 * math.pi / length)
                real = np.cos(angle) / math.sqrt(length)
                imag = (-np.sin(angle) if way == 0 else np.sin(angle)) / math.sqrt(length)
                if (side == "left") == (way == 0):
                    real, imag = real.T, imag.T
                if side == "left":
                    table = np.block([[real, -imag], [imag, real]])
                else:
                    table = np.block([[real, imag], [-imag, real]])
                high = table.astype(BF16)
                sides += [high, (table - high.astype(np.float64)).astype(BF16)]
    tables = np.stack(sides).reshape(2, 2, 2, 2, length, length)
    left, right = ([[[table[0], table[0], table[1]] for table in way] for way in side] for side in tables)
    return (np.stack([[np.concatenate(table, axis=1) for table in way] for way in left]),
            np.stack([[np.concatenate(table, axis=0) for table in way] for way in right]))


def split(x, axis):
    high = x.astype(BF16)
    low = (x - high.astype(F32)).astype(BF16)
    return jnp.concatenate([high, low, high], axis=axis)


def one_side(fields, product, axis, way):
    size = fields[0][0].shape[axis]
    half = size // 2
    first = lambda x: lax.slice_in_dim(x, 0, half, axis=axis)
    second = lambda x: lax.slice_in_dim(x, half, size, axis=axis)
    join = lambda x, y: jnp.concatenate([x, y], axis=axis)
    beside = lambda blocks: jnp.concatenate(blocks, axis=1 - axis)
    if way == 0:
        even = [join(first(x) + second(x), first(y) + second(y)) for x, y in fields]
        odd = [join(first(x) - second(x), first(y) - second(y)) for x, y in fields]
    else:
        even = [join(first(x), first(y)) for x, y in fields]
        odd = [join(second(x), second(y)) for x, y in fields]
    even = product(split(beside(even), axis), 0)
    odd = product(split(beside(odd), axis), 1)
    if way == 1:
        even, odd = even + odd, even - odd
    results = []
    for i in range(len(fields)):
        cut = lambda x: lax.slice_in_dim(x, i * size, (i + 1) * size, axis=1 - axis)
        results.append((join(first(cut(even)), first(cut(odd))), join(second(cut(even)), second(cut(odd)))))
    return results


def transform(fields, left_ref, right_ref, way):
    on_left = lambda x, parity: jnp.dot(left_ref[way, parity], x, preferred_element_type=F32)
    on_right = lambda x, parity: jnp.dot(x, right_ref[way, parity], preferred_element_type=F32)
    return one_side(one_side(fields, on_left, 0, way), on_right, 1, way)


def times(a, b):
    return a[0] * b[0] - a[1] * b[1], a[0] * b[1] + a[1] * b[0]


def times_conj(a, b):
    return a[0] * b[0] + a[1] * b[1], a[0] * b[1] - a[1] * b[0]


def one_hot(condition):
    return jnp.where(condition, 1.0, 0.0).astype(BF16)


def shift_pick(shape, offset, axis):
    here = lax.broadcasted_iota(jnp.int32, shape, axis) + offset
    return one_hot(here == lax.broadcasted_iota(jnp.int32, shape, 1 - axis))


def pieces(x, number):
    parts = []
    for _ in range(number):
        parts.append(x.astype(BF16))
        x = x - parts[-1].astype(F32)
    return parts


def select(x, pick, number):
    total = None
    for piece in pieces(x, number):
        part = jnp.dot(piece, pick, preferred_element_type=F32)
        total = part if total is None else total + part
    return total


def to_even_odd(field):
    n = field.shape[-1]
    source = lax.broadcasted_iota(jnp.int32, (n, n), 0)
    place = lax.broadcasted_iota(jnp.int32, (n, n), 1)
    half = n // 2
    pick_right = one_hot(source == jnp.where(place < half, 2 * place, 2 * place - (n - 1)))
    pick_left = one_hot(place == jnp.where(source < half, 2 * source, 2 * source - (n - 1)))
    rows = None
    for piece in pieces(field, 3):
        part = jnp.dot(pick_left, piece, preferred_element_type=F32)
        rows = part if rows is None else rows + part
    return select(rows, pick_right, 3)


class Line:
    def __init__(self, own, out_ref, up_ref, down_ref, send_ref, sems):
        self.own, self.out, self.up, self.down, self.send = own, out_ref, up_ref, down_ref, send_ref
        self.sems = sems
        self.n = lax.axis_size("mode")
        self.blocks = out_ref.shape[0]
        place = lax.axis_index("mode")
        left = place < self.n // 2
        self.depth = jnp.where(left, place, self.n - 1 - place)
        self.inward = jnp.where(left, place + 1, place - 1)
        self.outward = jnp.where(left, place - 1, place + 1)
        self.middle = self.depth == self.n // 2 - 1
        self.inner = self.depth > 0

    def copy(self, source, target, sent, received, device, k):
        return pltpu.make_async_remote_copy(
            src_ref=source.at[k], dst_ref=target.at[k],
            send_sem=self.sems.at[sent, k], recv_sem=self.sems.at[received, k],
            device_id={"mode": device}, device_id_type=MESH)

    def in_up(self, k):
        return self.copy(self.send, self.up, 0, 2, self.inward, k)

    def in_across(self, k):
        return self.copy(self.send, self.down, 0, 3, self.inward, k)

    def out_down(self, k):
        return self.copy(self.out, self.out, 1, 3, self.outward, k)

    def greet(self, barrier):
        pl.semaphore_signal(barrier, inc=1, device_id={"mode": self.inward}, device_id_type=MESH)

        @pl.when(self.inner)
        def _():
            pl.semaphore_signal(barrier, inc=1, device_id={"mode": self.outward}, device_id_type=MESH)

        return jnp.where(self.inner, 2, 1)

    def forward(self, k):
        @pl.when(self.middle)
        def _():
            self.in_across(k).start()

        @pl.when(jnp.logical_not(self.middle))
        def _():
            self.in_up(k).start()

    def gather_outer(self, k):
        @pl.when(jnp.logical_not(self.inner))
        def _():
            self.send[k] = self.own(k)
            self.forward(k)

    def gather_inner(self, k):
        @pl.when(self.inner)
        def _():
            self.in_up(k).wait_recv()
            self.send[k] = self.own(k) + self.up[k]
            self.forward(k)

    def spread_middle(self, k):
        @pl.when(self.middle)
        def _():
            self.in_across(k).wait_recv()
            self.out[k] = self.send[k] + self.down[k]

            @pl.when(self.inner)
            def _():
                self.out_down(k).start()

    def spread_outer(self, k):
        @pl.when(jnp.logical_not(self.middle))
        def _():
            self.in_across(k).wait_recv()

            @pl.when(self.inner)
            def _():
                self.out_down(k).start()

    def drain(self):
        def one(k, carry):
            self.in_up(k).wait_send()

            @pl.when(self.inner)
            def _():
                self.out_down(k).wait_send()
            return carry
        lax.fori_loop(0, self.blocks, one, 0)


def ptycho_kernel(count_ref, row_ref, col_ref, own_ref, probe_in_ref, phase_in_ref, measured_in_ref, left_in_ref, right_in_ref,
                  out_ref, probe_out_ref,
                  probe_ref, phase_ref, measured_ref, left_ref, right_ref, ext_ref, prop_ref, target_ref, window_ref, before_ref, far_ref, part_power_ref, power_ref,
                  power_up_ref, power_down_ref, power_send_ref, piece_ref, total_ref, probe_grad_ref,
                  up_ref, down_ref, send_ref, rim_in_ref, part_ref, got_ref,
                  fetch_sems, halo_sems, power_sems, sems, rim_sems, probe_sems):
    tiles = lax.axis_size("tile")
    me = lax.axis_index("tile")
    bits = tiles.bit_length() - 1
    has_next, has_last = me < tiles - 1, me > 0
    slots, layers = window_ref.shape[0], window_ref.shape[1]
    local_modes = probe_ref.shape[0]
    modes = local_modes * lax.axis_size("mode")
    width = probe_ref.shape[-1]
    tile_rows, columns = own_ref.shape[2:]
    per_slot = BLOCKS // slots
    slot_rows = width // per_slot
    per_layer = BLOCKS // layers
    per_part = per_layer // 2
    block_rows = tile_rows // per_part

    def place(k):
        row = k % per_part * block_rows
        return k // per_layer, k // per_part % 2, row

    def stored(k):
        return (layers - 1 - k // per_layer) * per_layer + k % per_layer

    plane = lax.axis_index("mode")
    odd = lax.rem(plane, 2)
    partner = plane + 1 - 2 * odd
    near = lax.rem(me, 2)
    half_rows = width // 2

    def region(layer, part, half):
        return ext_ref.at[layer, part, pl.ds(pl.multiple_of(tile_rows + half * half_rows, 8), half_rows)]

    def halo(layer, part, half):
        first = pl.multiple_of(half * half_rows, 8)
        return pltpu.make_async_remote_copy(
            src_ref=own_ref.at[layer, part, pl.ds(first, half_rows)], dst_ref=region(layer, part, half),
            send_sem=halo_sems.at[0, layer, part, half], recv_sem=halo_sems.at[1, layer, part, half],
            device_id={"tile": me - 1}, device_id_type=MESH)

    def hand_over(layer, part, half):
        return pltpu.make_async_remote_copy(
            src_ref=region(layer, part, half), dst_ref=region(layer, part, half),
            send_sem=halo_sems.at[2, layer, part, half], recv_sem=halo_sems.at[1, layer, part, half],
            device_id={"mode": partner}, device_id_type=MESH)

    def each_half(layer, action):
        for part in range(2):
            for half in range(2):
                action(layer, part, half)

    def start_halo():
        for layer in range(layers):
            @pl.when(has_last & (near == 1))
            def _():
                each_half(layer, lambda *which: halo(*which).start())

            @pl.when(has_last & (near == 0))
            def _():
                for part in range(2):
                    halo(layer, part, odd).start()

    def pass_halo(layer):
        @pl.when(has_next & (near == 1))
        def _():
            for part in range(2):
                halo(layer, part, odd).wait_recv()
                hand_over(layer, part, odd).start()

    def take_halo(layer):
        @pl.when(has_next & (near == 0))
        def _():
            each_half(layer, lambda *which: halo(*which).wait_recv())

        @pl.when(has_next & (near == 1))
        def _():
            for part in range(2):
                halo(layer, part, 1 - odd).wait_recv()

    def end_halo():
        for layer in range(layers):
            @pl.when(has_last & (near == 1))
            def _():
                each_half(layer, lambda *which: halo(*which).wait_send())

            @pl.when(has_last & (near == 0))
            def _():
                for part in range(2):
                    halo(layer, part, odd).wait_send()

            @pl.when(has_next & (near == 1))
            def _():
                for part in range(2):
                    hand_over(layer, part, odd).wait_send()

    def finish_halo():
        for layer in range(1, layers):
            take_halo(layer)
            cut_window(0, layer)

    def rim_copy(k):
        layer, part, row = place(k)
        return pltpu.make_async_remote_copy(
            src_ref=total_ref.at[layer, part, pl.ds(tile_rows + row, block_rows)], dst_ref=rim_in_ref.at[k],
            send_sem=rim_sems.at[0, k], recv_sem=rim_sems.at[1, k],
            device_id={"tile": me + 1}, device_id_type=MESH)

    def other(bit):
        low = lax.rem(me // (1 << bit), 2)
        return me + (1 - 2 * low) * (1 << bit)

    side = lax.rem(me, 2)

    def probe_copy(step, source, target):
        return pltpu.make_async_remote_copy(
            src_ref=source, dst_ref=target,
            send_sem=probe_sems.at[0, step], recv_sem=probe_sems.at[1, step],
            device_id={"tile": other(0 if step == bits else step)}, device_id_type=MESH)

    def exchange(step):
        if step == 0:
            return probe_copy(0, probe_grad_ref.at[1 - side], got_ref.at[0])
        if step < bits:
            return probe_copy(step, part_ref.at[step - 1], got_ref.at[step])
        return probe_copy(step, part_ref.at[bits - 1], probe_out_ref.at[side])

    power_line = Line(lambda k: part_power_ref[k], power_ref, power_up_ref, power_down_ref, power_send_ref, power_sems)

    def own(k):
        layer, part, row = place(k)
        return total_ref[layer, part, row:row + block_rows, :]

    line = Line(own, out_ref, up_ref, down_ref, send_ref, sems)

    def fetch(number):
        source, target = ((phase_in_ref, phase_ref), (measured_in_ref, measured_ref), (own_ref, ext_ref.at[:, :, pl.ds(0, tile_rows)]),
                          (left_in_ref, left_ref), (right_in_ref, right_ref), (probe_in_ref, probe_ref))[number]
        return pltpu.make_async_copy(source, target, fetch_sems.at[number])

    for number in range(6):
        fetch(number).start()
    barrier = pltpu.get_barrier_semaphore()
    count = line.greet(barrier)
    for bit in range(bits):
        pl.semaphore_signal(barrier, inc=1, device_id={"tile": other(bit)}, device_id_type=MESH)

    @pl.when(has_next)
    def _():
        pl.semaphore_signal(barrier, inc=1, device_id={"tile": me + 1}, device_id_type=MESH)

    @pl.when(has_last)
    def _():
        pl.semaphore_signal(barrier, inc=1, device_id={"tile": me - 1}, device_id_type=MESH)

    pl.semaphore_wait(barrier, count + bits + has_next.astype(jnp.int32) + has_last.astype(jnp.int32))

    start_halo()

    @pl.when(jnp.logical_not(has_next))
    def _():
        ext_ref[:, :, tile_rows:, :] = jnp.zeros((layers, 2, width, columns), F32)

    total_ref[...] = jnp.zeros_like(total_ref)
    probe_grad_ref[...] = jnp.zeros_like(probe_grad_ref)
    fetch(0).wait()
    phase = to_even_odd(phase_ref[...])
    prop_ref[0] = jnp.cos(phase)
    prop_ref[1] = jnp.sin(phase)
    fetch(1).wait()

    def order(slot, carry):
        target_ref[slot] = to_even_odd(measured_ref[slot])
        return carry
    lax.fori_loop(0, slots, order, 0)
    for number in range(2, 6):
        fetch(number).wait()

    def chosen(amount, bit, yes, no):
        return jnp.where(jnp.full(yes.shape, amount & bit, jnp.int32) > 0, yes, no)

    steps = [1 << level for level in reversed(range(3, (tile_rows - 1).bit_length()))]

    def cut_window(slot, layer):
        row = row_ref[slot]
        pick = shift_pick((columns, width), col_ref[slot], 1)
        for part in range(2):
            block = ext_ref[layer, part]
            for step in steps:
                size = block.shape[0] - step
                block = chosen(row, step, block[step:], block[:size])
            size = block.shape[0]
            for step in (4, 2, 1):
                block = chosen(row, step, pltpu.roll(block, size - step, 0), block)
            window_ref[slot, layer, part] = select(block[:width], pick, 2)

    def put_back(slot, layer):
        row = row_ref[slot]
        pick = shift_pick((width, columns), col_ref[slot], 0)
        for part in range(2):
            block = jnp.concatenate([select(piece_ref[part], pick, 2), jnp.zeros((8, columns), F32)], axis=0)
            for step in (1, 2, 4):
                block = chosen(row, step, pltpu.roll(block, step, 0), block)
            for step in reversed(steps):
                space = jnp.zeros((step, columns), F32)
                block = chosen(row, step, jnp.concatenate([space, block], axis=0), jnp.concatenate([block, space], axis=0))
            total_ref[layer, part] += block

    lag_gather, lag_middle, lag_outer = 5, 8, 11

    def within(k, blocks, action):
        if isinstance(k, int):
            if 0 <= k < blocks:
                action(k)
        else:
            @pl.when((k >= 0) & (k < blocks))
            def _():
                action(k)

    def power_hook(q):
        within(q - lag_gather, BLOCKS, power_line.gather_inner)
        within(q - lag_middle, BLOCKS, power_line.spread_middle)
        within(q - lag_outer, BLOCKS, power_line.spread_outer)

    pair = lambda ref, *place: (ref[(*place, 0)], ref[(*place, 1)])
    each = range(local_modes)
    prop = lambda: pair(prop_ref)

    def forward_slot(slot, carry):
        @pl.when(slot > 0)
        def _():
            for layer in range(layers):
                cut_window(slot, layer)

        waves = [times(pair(probe_ref, mode), pair(window_ref, slot, 0)) for mode in each]
        spectra = transform(waves, left_ref, right_ref, 0)

        @pl.when(slot == 0)
        def _():
            for layer in range(1, layers):
                pass_halo(layer)

        q = slot * per_slot
        for h in range(per_slot // 2):
            power_hook(q + h)
        moved = transform([times(prop(), field) for field in spectra], left_ref, right_ref, 1)
        for mode in each:
            for part in range(2):
                before_ref[slot, mode, part] = moved[mode][part]

        @pl.when(slot == 0)
        def _():
            finish_halo()

        for h in range(per_slot // 2, per_slot):
            power_hook(q + h)
        waves = [times(pair(before_ref, slot, mode), pair(window_ref, slot, 1)) for mode in each]
        far = transform(waves, left_ref, right_ref, 0)
        power = None
        for mode in each:
            for part in range(2):
                far_ref[slot, mode, part] = far[mode][part]
                here = far[mode][part] * far[mode][part]
                power = here if power is None else power + here
        for part in range(per_slot):
            part_power_ref[slot * per_slot + part] = power[part * slot_rows:(part + 1) * slot_rows]
        for part in range(per_slot):
            power_line.gather_outer(slot * per_slot + part)
        return carry

    pass_halo(0)
    take_halo(0)
    cut_window(0, 0)
    lax.fori_loop(0, slots, forward_slot, 0)
    hooks = [BLOCKS]

    def next_power_hook():
        power_hook(hooks[0])
        hooks[0] += 1

    def add_up(fields):
        for part in range(2):
            total = fields[0][part]
            for field in fields[1:]:
                total = total + field[part]
            piece_ref[part] = total

    def first_back(slot, hook):
        live = jnp.where(jnp.full((width, width), count_ref[0], jnp.int32) > slot, 1.0 / modes, 0.0)
        power = power_ref[slot * per_slot:(slot + 1) * per_slot].reshape(width, width)
        weight = (power - target_ref[slot]) * live
        waves = [(weight * far_ref[slot, mode, 0], weight * far_ref[slot, mode, 1]) for mode in each]
        back = transform(waves, left_ref, right_ref, 1)
        add_up([times_conj(pair(before_ref, slot, mode), back[mode]) for mode in each])
        for mode in each:
            for part in range(2):
                far_ref[slot, mode, part] = back[mode][part]
        for _ in range(per_slot // 2):
            hook()
        put_back(slot, 1)

    def second_back(slot, hook):
        waves = [times_conj(pair(window_ref, slot, 1), pair(far_ref, slot, mode)) for mode in each]
        inner = transform(waves, left_ref, right_ref, 0)
        for _ in range(per_slot // 2):
            hook()
        back = transform([times_conj(prop(), field) for field in inner], left_ref, right_ref, 1)
        add_up([times_conj(pair(probe_ref, mode), back[mode]) for mode in each])
        for mode in each:
            grad = times_conj(pair(window_ref, slot, 0), back[mode])
            for part in range(2):
                flat = mode * 2 + part
                first = flat % local_modes * width
                probe_grad_ref[flat // local_modes, first:first + width, :] += grad[part]
        for _ in range(per_slot // 2):
            hook()
        put_back(slot, 0)

    def ready(slot):
        while hooks[0] <= (slot + 1) * per_slot - 1 + lag_outer:
            next_power_hook()

    early = min(2, slots - 1)
    for slot in range(slots - 1):
        ready(slot)
        first_back(slot, next_power_hook)
        if slot == 0 and early > 0:
            second_back(0, next_power_hook)
    for slot in range(1, early):
        second_back(slot, next_power_hook)
    ready(slots - 1)
    first_back(slots - 1, next_power_hook)
    while hooks[0] < BLOCKS + lag_outer:
        next_power_hook()

    def send_rim(layer):
        @pl.when(has_next)
        def _():
            for k in range(layer * per_layer, (layer + 1) * per_layer):
                rim_copy(k).start()

    def add_rim(k):
        @pl.when(has_last)
        def _():
            rim_copy(k).wait_recv()
            layer, part, row = place(k)
            total_ref[layer, part, row:row + block_rows, :] += rim_in_ref[k]

    def line_hook(h):
        if 0 <= h - 2 < BLOCKS:
            add_rim(stored(h - 2))
            line.gather_outer(stored(h - 2))
        if 0 <= h - 4 < BLOCKS:
            line.gather_inner(stored(h - 4))
        if 0 <= h - 7 < BLOCKS:
            line.spread_middle(stored(h - 7))
        if 0 <= h - 10 < BLOCKS:
            line.spread_outer(stored(h - 10))

    hooks = [0]

    def next_line_hook():
        if hooks[0] < per_layer:
            line_hook(hooks[0])
            hooks[0] += 1

    for layer in range(layers - 1, 0, -1):
        send_rim(layer)
    for slot in range(early, slots):
        second_back(slot, next_line_hook)
    send_rim(0)
    exchange(0).start()
    for h in range(hooks[0], BLOCKS + 10):
        line_hook(h)
        late = h - per_layer
        bit = late // 5
        if late % 5 == 1 and 0 <= bit < bits:
            exchange(bit).wait_recv()
            part_ref[bit] = (probe_grad_ref[side] if bit == 0 else part_ref[bit - 1]) + got_ref[bit]
            exchange(bit + 1).start()
    probe_out_ref[side] = part_ref[bits - 1]
    exchange(bits).wait_recv()
    for step in range(bits + 1):
        exchange(step).wait_send()
    power_line.drain()
    line.drain()

    @pl.when(has_next)
    def _():
        for k in range(BLOCKS):
            rim_copy(k).wait_send()

    end_halo()


def per_device(object_field, probe, measured, prop_phase, counts, row_offset, col_offset):
    layers, _, tile_rows, columns = object_field.shape
    width = probe.shape[-1]
    local_modes = probe.shape[0]
    slots = row_offset.shape[0]
    bits = lax.axis_size("tile").bit_length() - 1
    left, right = (jnp.asarray(table) for table in dft_constants(width))
    smem = pl.BlockSpec(memory_space=pltpu.SMEM)
    field = pltpu.VMEM((slots, local_modes, 2, width, width), F32)
    power = pltpu.VMEM((BLOCKS, slots * width // BLOCKS, width), F32)
    own_blocks = (BLOCKS, layers * 2 * tile_rows // BLOCKS, columns)
    block = pltpu.VMEM(own_blocks, F32)
    ext = pltpu.VMEM((layers, 2, tile_rows + width, columns), F32)
    halves = (2, local_modes * width, width)
    parts = pltpu.VMEM((bits, *halves[1:]), F32)
    dma = pltpu.SemaphoreType.DMA
    object_grad, probe_grad = pl.pallas_call(
        ptycho_kernel,
        out_shape=(jax.ShapeDtypeStruct(own_blocks, F32), jax.ShapeDtypeStruct(halves, F32)),
        in_specs=[smem] * 3 + [pl.BlockSpec(memory_space=pl.ANY)] * 6,
        out_specs=(VMEM_SPEC, VMEM_SPEC),
        scratch_shapes=[
            pltpu.VMEM(probe.shape, F32), pltpu.VMEM((width, width), F32), pltpu.VMEM(measured.shape, F32),
            pltpu.VMEM(left.shape, BF16), pltpu.VMEM(right.shape, BF16),
            ext, pltpu.VMEM((2, width, width), F32), pltpu.VMEM((slots, width, width), F32),
            pltpu.VMEM((slots, layers, 2, width, width), F32), field, field, power, power,
            power, power, power, pltpu.VMEM((2, width, width), F32),
            ext, pltpu.VMEM(halves, F32),
            block, block, block, block, parts, parts,
            dma((6,)), dma((3, layers, 2, 2)), dma((4, BLOCKS)), dma((4, BLOCKS)), dma((2, BLOCKS)), dma((2, bits + 1))],
        compiler_params=pltpu.CompilerParams(collective_id=0, has_side_effects=True, vmem_limit_bytes=62 << 20),
        name="ptycho",
    )(counts, row_offset, col_offset, object_field, probe, prop_phase, measured, left, right)
    return object_grad.reshape(object_field.shape), probe_grad.reshape(probe.shape)


def solution(mesh):
    placed = (
        P(None, None, "tile", None),
        P("mode", None, None, None),
        P("tile", None, None),
        P(),
        P("tile"),
        P("tile"),
        P("tile"),
    )
    return jax.shard_map(
        per_device,
        mesh=mesh,
        in_specs=placed,
        out_specs=(P(None, None, "tile", None), P("mode", None, None, None)),
        check_vma=False,
    )
```

```python
import functools
import math

import jax
import jax.numpy as jnp
import numpy as np
from jax import lax
from jax.experimental import pallas as pl
from jax.experimental.pallas import tpu as pltpu
from jax.sharding import PartitionSpec as P

F32 = jnp.float32
BF16 = jnp.bfloat16
MESH = pl.DeviceIdType.MESH
BLOCKS = 16
LINE_BLOCKS = 32
PIECES = 2
VMEM_SPEC = pl.BlockSpec(memory_space=pltpu.VMEM)


def shifted(block, axis, distance):
    devices = range(lax.axis_size(axis))
    route = [(i - distance, i) for i in devices if i - distance in devices]
    return lax.ppermute(block, axis, route)


def dft_constants(length):
    half = length // 2
    n, k = np.arange(half)[:, None], np.arange(half)[None, :]
    sides = []
    for side in ("left", "right"):
        for way in range(2):
            for parity in range(2):
                angle = (n * (2 * k + parity) % length) * (2.0 * math.pi / length)
                real = np.cos(angle) / math.sqrt(length)
                imag = (-np.sin(angle) if way == 0 else np.sin(angle)) / math.sqrt(length)
                if (side == "left") == (way == 0):
                    real, imag = real.T, imag.T
                if side == "left":
                    table = np.block([[real, -imag], [imag, real]])
                else:
                    table = np.block([[real, imag], [-imag, real]])
                high = table.astype(BF16)
                sides += [high, (table - high.astype(np.float64)).astype(BF16)]
    tables = np.stack(sides).reshape(2, 2, 2, 2, length, length)
    left, right = ([[[table[0], table[0], table[1]] for table in way] for way in side] for side in tables)
    return (np.stack([[np.concatenate(table, axis=1) for table in way] for way in left]),
            np.stack([[np.concatenate(table, axis=0) for table in way] for way in right]))


def split(x, axis):
    high = x.astype(BF16)
    low = (x - high.astype(F32)).astype(BF16)
    return jnp.concatenate([high, low, high], axis=axis)


def one_side(fields, product, axis, way):
    size = fields[0][0].shape[axis]
    half = size // 2
    first = lambda x: lax.slice_in_dim(x, 0, half, axis=axis)
    second = lambda x: lax.slice_in_dim(x, half, size, axis=axis)
    join = lambda x, y: jnp.concatenate([x, y], axis=axis)
    beside = lambda blocks: jnp.concatenate(blocks, axis=1 - axis)
    if way == 0:
        even = [join(first(x) + second(x), first(y) + second(y)) for x, y in fields]
        odd = [join(first(x) - second(x), first(y) - second(y)) for x, y in fields]
    else:
        even = [join(first(x), first(y)) for x, y in fields]
        odd = [join(second(x), second(y)) for x, y in fields]
    even = product(split(beside(even), axis), 0)
    odd = product(split(beside(odd), axis), 1)
    if way == 1:
        even, odd = even + odd, even - odd
    results = []
    for i in range(len(fields)):
        cut = lambda x: lax.slice_in_dim(x, i * size, (i + 1) * size, axis=1 - axis)
        results.append((join(first(cut(even)), first(cut(odd))), join(second(cut(even)), second(cut(odd)))))
    return results


def transform(fields, left_ref, right_ref, way):
    on_left = lambda x, parity: jnp.dot(left_ref[way, parity], x, preferred_element_type=F32)
    on_right = lambda x, parity: jnp.dot(x, right_ref[way, parity], preferred_element_type=F32)
    return one_side(one_side(fields, on_left, 0, way), on_right, 1, way)


def times(a, b):
    return a[0] * b[0] - a[1] * b[1], a[0] * b[1] + a[1] * b[0]


def times_conj(a, b):
    return a[0] * b[0] + a[1] * b[1], a[0] * b[1] - a[1] * b[0]


def one_hot(condition):
    return jnp.where(condition, 1.0, 0.0).astype(BF16)


def shift_pick(shape, offset, axis):
    here = lax.broadcasted_iota(jnp.int32, shape, axis) + offset
    return one_hot(here == lax.broadcasted_iota(jnp.int32, shape, 1 - axis))


def pieces(x, number):
    parts = []
    for _ in range(number):
        parts.append(x.astype(BF16))
        x = x - parts[-1].astype(F32)
    return parts


def select(x, pick, number):
    total = None
    for piece in pieces(x, number):
        part = jnp.dot(piece, pick, preferred_element_type=F32)
        total = part if total is None else total + part
    return total


def to_even_odd(field):
    n = field.shape[-1]
    source = lax.broadcasted_iota(jnp.int32, (n, n), 0)
    place = lax.broadcasted_iota(jnp.int32, (n, n), 1)
    half = n // 2
    pick_right = one_hot(source == jnp.where(place < half, 2 * place, 2 * place - (n - 1)))
    pick_left = one_hot(place == jnp.where(source < half, 2 * source, 2 * source - (n - 1)))
    rows = None
    for piece in pieces(field, 3):
        part = jnp.dot(pick_left, piece, preferred_element_type=F32)
        rows = part if rows is None else rows + part
    return select(rows, pick_right, 3)


class Line:
    def __init__(self, own, out_ref, up_ref, down_ref, send_ref, sems):
        self.own, self.out, self.up, self.down, self.send = own, out_ref, up_ref, down_ref, send_ref
        self.sems = sems
        self.n = lax.axis_size("mode")
        self.blocks = out_ref.shape[0]
        place = lax.axis_index("mode")
        left = place < self.n // 2
        self.depth = jnp.where(left, place, self.n - 1 - place)
        self.inward = jnp.where(left, place + 1, place - 1)
        self.outward = jnp.where(left, place - 1, place + 1)
        self.middle = self.depth == self.n // 2 - 1
        self.inner = self.depth > 0

    def copy(self, source, target, sent, received, device, k):
        return pltpu.make_async_remote_copy(
            src_ref=source.at[k], dst_ref=target.at[k],
            send_sem=self.sems.at[sent, k], recv_sem=self.sems.at[received, k],
            device_id={"mode": device}, device_id_type=MESH)

    def in_up(self, k):
        return self.copy(self.send, self.up, 0, 2, self.inward, k)

    def in_across(self, k):
        return self.copy(self.send, self.down, 0, 3, self.inward, k)

    def out_down(self, k):
        return self.copy(self.out, self.out, 1, 3, self.outward, k)

    def greet(self, barrier):
        pl.semaphore_signal(barrier, inc=1, device_id={"mode": self.inward}, device_id_type=MESH)

        @pl.when(self.inner)
        def _():
            pl.semaphore_signal(barrier, inc=1, device_id={"mode": self.outward}, device_id_type=MESH)

        return jnp.where(self.inner, 2, 1)

    def forward(self, k):
        @pl.when(self.middle)
        def _():
            self.in_across(k).start()

        @pl.when(jnp.logical_not(self.middle))
        def _():
            self.in_up(k).start()

    def gather_outer(self, k):
        @pl.when(jnp.logical_not(self.inner))
        def _():
            self.send[k] = self.own(k)
            self.forward(k)

    def gather_inner(self, k):
        @pl.when(self.inner)
        def _():
            self.in_up(k).wait_recv()
            self.send[k] = self.own(k) + self.up[k]
            self.forward(k)

    def spread_middle(self, k):
        @pl.when(self.middle)
        def _():
            self.in_across(k).wait_recv()
            self.out[k] = self.send[k] + self.down[k]

            @pl.when(self.inner)
            def _():
                self.out_down(k).start()

    def spread_outer(self, k):
        @pl.when(jnp.logical_not(self.middle))
        def _():
            self.in_across(k).wait_recv()

            @pl.when(self.inner)
            def _():
                self.out_down(k).start()

    def drain(self):
        def one(k, carry):
            self.in_up(k).wait_send()

            @pl.when(self.inner)
            def _():
                self.out_down(k).wait_send()
            return carry
        lax.fori_loop(0, self.blocks, one, 0)


def ptycho_kernel(count_ref, row_ref, col_ref, own_ref, probe_in_ref, phase_in_ref, measured_in_ref, left_in_ref, right_in_ref,
                  out_ref, probe_out_ref,
                  probe_ref, phase_ref, measured_ref, left_ref, right_ref, ext_ref, prop_ref, target_ref, window_ref, before_ref, far_ref, part_power_ref, power_ref,
                  power_up_ref, power_down_ref, power_send_ref, piece_ref, total_ref, probe_grad_ref,
                  up_ref, down_ref, send_ref, rim_in_ref, part_ref, got_ref,
                  fetch_sems, halo_sems, power_sems, sems, rim_sems, probe_sems):
    tiles = lax.axis_size("tile")
    me = lax.axis_index("tile")
    bits = tiles.bit_length() - 1
    has_next, has_last = me < tiles - 1, me > 0
    slots, layers = window_ref.shape[0], window_ref.shape[1]
    local_modes = probe_ref.shape[0]
    modes = local_modes * lax.axis_size("mode")
    width = probe_ref.shape[-1]
    tile_rows, columns = own_ref.shape[2:]
    per_slot = BLOCKS // slots
    slot_rows = width // per_slot
    per_layer = BLOCKS // layers
    per_part = per_layer // 2
    block_rows = tile_rows // per_part

    def place(k):
        row = k % per_part * block_rows
        return k // per_layer, k // per_part % 2, row

    def stored(k):
        return (layers - 1 - k // per_layer) * per_layer + k % per_layer

    plane = lax.axis_index("mode")
    odd = lax.rem(plane, 2)
    partner = plane + 1 - 2 * odd
    near = lax.rem(me, 2)
    half_rows = width // 2

    def region(layer, part, half):
        return ext_ref.at[layer, part, pl.ds(pl.multiple_of(tile_rows + half * half_rows, 8), half_rows)]

    def halo(layer, part, half):
        first = pl.multiple_of(half * half_rows, 8)
        return pltpu.make_async_remote_copy(
            src_ref=own_ref.at[layer, part, pl.ds(first, half_rows)], dst_ref=region(layer, part, half),
            send_sem=halo_sems.at[0, layer, part, half], recv_sem=halo_sems.at[1, layer, part, half],
            device_id={"tile": me - 1}, device_id_type=MESH)

    def hand_over(layer, part, half):
        return pltpu.make_async_remote_copy(
            src_ref=region(layer, part, half), dst_ref=region(layer, part, half),
            send_sem=halo_sems.at[2, layer, part, half], recv_sem=halo_sems.at[1, layer, part, half],
            device_id={"mode": partner}, device_id_type=MESH)

    def each_half(layer, action):
        for part in range(2):
            for half in range(2):
                action(layer, part, half)

    def start_halo():
        for layer in range(layers):
            @pl.when(has_last & (near == 1))
            def _():
                each_half(layer, lambda *which: halo(*which).start())

            @pl.when(has_last & (near == 0))
            def _():
                for part in range(2):
                    halo(layer, part, odd).start()

    def pass_halo(layer):
        @pl.when(has_next & (near == 1))
        def _():
            for part in range(2):
                halo(layer, part, odd).wait_recv()
                hand_over(layer, part, odd).start()

    def take_halo(layer):
        @pl.when(has_next & (near == 0))
        def _():
            each_half(layer, lambda *which: halo(*which).wait_recv())

        @pl.when(has_next & (near == 1))
        def _():
            for part in range(2):
                halo(layer, part, 1 - odd).wait_recv()

    def end_halo():
        for layer in range(layers):
            @pl.when(has_last & (near == 1))
            def _():
                each_half(layer, lambda *which: halo(*which).wait_send())

            @pl.when(has_last & (near == 0))
            def _():
                for part in range(2):
                    halo(layer, part, odd).wait_send()

            @pl.when(has_next & (near == 1))
            def _():
                for part in range(2):
                    hand_over(layer, part, odd).wait_send()

    def finish_halo():
        for layer in range(1, layers):
            take_halo(layer)
            cut_window(0, layer)

    def rim_copy(k):
        layer, part, row = place(k)
        return pltpu.make_async_remote_copy(
            src_ref=total_ref.at[layer, part, pl.ds(tile_rows + row, block_rows)], dst_ref=rim_in_ref.at[k],
            send_sem=rim_sems.at[0, k], recv_sem=rim_sems.at[1, k],
            device_id={"tile": me + 1}, device_id_type=MESH)

    def other(bit):
        low = lax.rem(me // (1 << bit), 2)
        return me + (1 - 2 * low) * (1 << bit)

    side = lax.rem(me, 2)

    def probe_copy(step, source, target):
        return pltpu.make_async_remote_copy(
            src_ref=source, dst_ref=target,
            send_sem=probe_sems.at[0, step], recv_sem=probe_sems.at[1, step],
            device_id={"tile": other(0 if step == bits else step)}, device_id_type=MESH)

    def exchange(step):
        if step == 0:
            return probe_copy(0, probe_grad_ref.at[1 - side], got_ref.at[0])
        if step < bits:
            return probe_copy(step, part_ref.at[step - 1], got_ref.at[step])
        return probe_copy(step, part_ref.at[bits - 1], probe_out_ref.at[side])

    power_line = Line(lambda k: part_power_ref[k], power_ref, power_up_ref, power_down_ref, power_send_ref, power_sems)

    def own(k):
        layer, part, row = place(k)
        return total_ref[layer, part, row:row + block_rows, :]

    line = Line(own, out_ref, up_ref, down_ref, send_ref, sems)

    def fetch(number):
        source, target = ((phase_in_ref, phase_ref), (measured_in_ref, measured_ref), (own_ref, ext_ref.at[:, :, pl.ds(0, tile_rows)]),
                          (left_in_ref, left_ref), (right_in_ref, right_ref), (probe_in_ref, probe_ref))[number]
        return pltpu.make_async_copy(source, target, fetch_sems.at[number])

    for number in range(6):
        fetch(number).start()
    barrier = pltpu.get_barrier_semaphore()
    count = line.greet(barrier)
    for bit in range(bits):
        pl.semaphore_signal(barrier, inc=1, device_id={"tile": other(bit)}, device_id_type=MESH)

    @pl.when(has_next)
    def _():
        pl.semaphore_signal(barrier, inc=1, device_id={"tile": me + 1}, device_id_type=MESH)

    @pl.when(has_last)
    def _():
        pl.semaphore_signal(barrier, inc=1, device_id={"tile": me - 1}, device_id_type=MESH)

    pl.semaphore_wait(barrier, count + bits + has_next.astype(jnp.int32) + has_last.astype(jnp.int32))

    start_halo()

    @pl.when(jnp.logical_not(has_next))
    def _():
        ext_ref[:, :, tile_rows:, :] = jnp.zeros((layers, 2, width, columns), F32)

    total_ref[...] = jnp.zeros_like(total_ref)
    probe_grad_ref[...] = jnp.zeros_like(probe_grad_ref)
    fetch(0).wait()
    phase = to_even_odd(phase_ref[...])
    prop_ref[0] = jnp.cos(phase)
    prop_ref[1] = jnp.sin(phase)
    fetch(1).wait()

    def order(slot, carry):
        target_ref[slot] = to_even_odd(measured_ref[slot])
        return carry
    lax.fori_loop(0, slots, order, 0)
    for number in range(2, 6):
        fetch(number).wait()

    def chosen(amount, bit, yes, no):
        return jnp.where(jnp.full(yes.shape, amount & bit, jnp.int32) > 0, yes, no)

    steps = [1 << level for level in reversed(range(3, (tile_rows - 1).bit_length()))]

    def cut_window(slot, layer):
        row = row_ref[slot]
        pick = shift_pick((columns, width), col_ref[slot], 1)
        for part in range(2):
            block = ext_ref[layer, part]
            for step in steps:
                size = block.shape[0] - step
                block = chosen(row, step, block[step:], block[:size])
            size = block.shape[0]
            for step in (4, 2, 1):
                block = chosen(row, step, pltpu.roll(block, size - step, 0), block)
            window_ref[slot, layer, part] = select(block[:width], pick, 2)

    def put_back(slot, layer):
        row = row_ref[slot]
        pick = shift_pick((width, columns), col_ref[slot], 0)
        for part in range(2):
            block = jnp.concatenate([select(piece_ref[part], pick, 2), jnp.zeros((8, columns), F32)], axis=0)
            for step in (1, 2, 4):
                block = chosen(row, step, pltpu.roll(block, step, 0), block)
            for step in reversed(steps):
                space = jnp.zeros((step, columns), F32)
                block = chosen(row, step, jnp.concatenate([space, block], axis=0), jnp.concatenate([block, space], axis=0))
            total_ref[layer, part] += block

    lag_gather, lag_middle, lag_outer = 5, 8, 11

    def within(k, blocks, action):
        if isinstance(k, int):
            if 0 <= k < blocks:
                action(k)
        else:
            @pl.when((k >= 0) & (k < blocks))
            def _():
                action(k)

    def power_hook(q):
        within(q - lag_gather, BLOCKS, power_line.gather_inner)
        within(q - lag_middle, BLOCKS, power_line.spread_middle)
        within(q - lag_outer, BLOCKS, power_line.spread_outer)

    pair = lambda ref, *place: (ref[(*place, 0)], ref[(*place, 1)])
    each = range(local_modes)
    prop = lambda: pair(prop_ref)

    def forward_slot(slot, carry):
        @pl.when(slot > 0)
        def _():
            for layer in range(layers):
                cut_window(slot, layer)

        waves = [times(pair(probe_ref, mode), pair(window_ref, slot, 0)) for mode in each]
        spectra = transform(waves, left_ref, right_ref, 0)

        @pl.when(slot == 0)
        def _():
            for layer in range(1, layers):
                pass_halo(layer)

        q = slot * per_slot
        for h in range(per_slot // 2):
            power_hook(q + h)
        moved = transform([times(prop(), field) for field in spectra], left_ref, right_ref, 1)
        for mode in each:
            for part in range(2):
                before_ref[slot, mode, part] = moved[mode][part]

        @pl.when(slot == 0)
        def _():
            finish_halo()

        for h in range(per_slot // 2, per_slot):
            power_hook(q + h)
        waves = [times(pair(before_ref, slot, mode), pair(window_ref, slot, 1)) for mode in each]
        far = transform(waves, left_ref, right_ref, 0)
        power = None
        for mode in each:
            for part in range(2):
                far_ref[slot, mode, part] = far[mode][part]
                here = far[mode][part] * far[mode][part]
                power = here if power is None else power + here
        for part in range(per_slot):
            part_power_ref[slot * per_slot + part] = power[part * slot_rows:(part + 1) * slot_rows]
        for part in range(per_slot):
            power_line.gather_outer(slot * per_slot + part)
        return carry

    pass_halo(0)
    take_halo(0)
    cut_window(0, 0)
    lax.fori_loop(0, slots, forward_slot, 0)
    hooks = [BLOCKS]

    def next_power_hook():
        power_hook(hooks[0])
        hooks[0] += 1

    def add_up(fields):
        for part in range(2):
            total = fields[0][part]
            for field in fields[1:]:
                total = total + field[part]
            piece_ref[part] = total

    def first_back(slot, hook):
        live = jnp.where(jnp.full((width, width), count_ref[0], jnp.int32) > slot, 1.0 / modes, 0.0)
        power = power_ref[slot * per_slot:(slot + 1) * per_slot].reshape(width, width)
        weight = (power - target_ref[slot]) * live
        waves = [(weight * far_ref[slot, mode, 0], weight * far_ref[slot, mode, 1]) for mode in each]
        back = transform(waves, left_ref, right_ref, 1)
        add_up([times_conj(pair(before_ref, slot, mode), back[mode]) for mode in each])
        for mode in each:
            for part in range(2):
                far_ref[slot, mode, part] = back[mode][part]
        for _ in range(per_slot // 2):
            hook()
        put_back(slot, 1)

    def second_back(slot, hook):
        waves = [times_conj(pair(window_ref, slot, 1), pair(far_ref, slot, mode)) for mode in each]
        inner = transform(waves, left_ref, right_ref, 0)
        for _ in range(per_slot // 2):
            hook()
        back = transform([times_conj(prop(), field) for field in inner], left_ref, right_ref, 1)
        add_up([times_conj(pair(probe_ref, mode), back[mode]) for mode in each])
        for mode in each:
            grad = times_conj(pair(window_ref, slot, 0), back[mode])
            for part in range(2):
                flat = mode * 2 + part
                first = flat % local_modes * width
                probe_grad_ref[flat // local_modes, first:first + width, :] += grad[part]
        for _ in range(per_slot // 2):
            hook()
        put_back(slot, 0)

    def ready(slot):
        while hooks[0] <= (slot + 1) * per_slot - 1 + lag_outer:
            next_power_hook()

    early = min(2, slots - 1)
    for slot in range(slots - 1):
        ready(slot)
        first_back(slot, next_power_hook)
        if slot == 0 and early > 0:
            second_back(0, next_power_hook)
    for slot in range(1, early):
        second_back(slot, next_power_hook)
    ready(slots - 1)
    first_back(slots - 1, next_power_hook)
    while hooks[0] < BLOCKS + lag_outer:
        next_power_hook()

    def send_rim(layer):
        @pl.when(has_next)
        def _():
            for k in range(layer * per_layer, (layer + 1) * per_layer):
                rim_copy(k).start()

    def add_rim(k):
        @pl.when(has_last)
        def _():
            rim_copy(k).wait_recv()
            layer, part, row = place(k)
            total_ref[layer, part, row:row + block_rows, :] += rim_in_ref[k]

    def line_hook(h):
        if 0 <= h - 2 < BLOCKS:
            add_rim(stored(h - 2))
            line.gather_outer(stored(h - 2))
        if 0 <= h - 4 < BLOCKS:
            line.gather_inner(stored(h - 4))
        if 0 <= h - 7 < BLOCKS:
            line.spread_middle(stored(h - 7))
        if 0 <= h - 10 < BLOCKS:
            line.spread_outer(stored(h - 10))

    hooks = [0]

    def next_line_hook():
        if hooks[0] < per_layer:
            line_hook(hooks[0])
            hooks[0] += 1

    for layer in range(layers - 1, 0, -1):
        send_rim(layer)
    for slot in range(early, slots):
        second_back(slot, next_line_hook)
    send_rim(0)
    exchange(0).start()
    for h in range(hooks[0], BLOCKS + 10):
        line_hook(h)
        late = h - per_layer
        bit = late // 5
        if late % 5 == 1 and 0 <= bit < bits:
            exchange(bit).wait_recv()
            part_ref[bit] = (probe_grad_ref[side] if bit == 0 else part_ref[bit - 1]) + got_ref[bit]
            exchange(bit + 1).start()
    probe_out_ref[side] = part_ref[bits - 1]
    exchange(bits).wait_recv()
    for step in range(bits + 1):
        exchange(step).wait_send()
    power_line.drain()
    line.drain()

    @pl.when(has_next)
    def _():
        for k in range(BLOCKS):
            rim_copy(k).wait_send()

    end_halo()


def slot_kernel(count_ref, row_ref, col_ref, own_ref, probe_ref, phase_in_ref, measured_in_ref, left_in_ref, right_in_ref,
                out_ref, probe_out_ref,
                modes_ref, phase_ref, measured_ref, left_ref, right_ref, ext_ref, prop_ref, target_ref, window_ref,
                before_ref, far_ref, power_ref, piece_ref, total_ref, grad_ref,
                core_in_ref, core_sum_ref, first_in_ref, first_sum_ref, second_in_ref, second_sum_ref, plane_in_ref, plane_out_ref,
                up_ref, down_ref, send_ref, rim_in_ref,
                fetch_sems, halo_sems, sems, rim_sems, share_sems, core_sems, first_sems, second_sems, plane_sems, spread_sems):
    tiles = lax.axis_size("tile")
    me = lax.axis_index("tile")
    bits = tiles.bit_length() - 1
    has_next, has_last = me < tiles - 1, me > 0
    layers = window_ref.shape[0]
    modes, width = modes_ref.shape[0], modes_ref.shape[-1]
    local_modes = probe_ref.shape[0]
    tile_rows, columns = own_ref.shape[2:]
    per_layer = LINE_BLOCKS // layers
    per_part = per_layer // 2
    half = width // 2

    def stored(k):
        return (layers - 1 - k // per_layer) * per_layer + k % per_layer

    plane = lax.axis_index("mode")
    odd = lax.rem(plane, 2)
    partner = plane + 1 - 2 * odd
    near = lax.rem(me, 2)
    piece_rows = width // (2 * PIECES)

    def rows_of(half, piece):
        return pl.multiple_of((half * PIECES + piece) * piece_rows, 8)

    def region(layer, part, half, piece):
        return ext_ref.at[layer, part, pl.ds(tile_rows + rows_of(half, piece), piece_rows)]

    def halo(layer, part, half, piece):
        return pltpu.make_async_remote_copy(
            src_ref=own_ref.at[layer, part, pl.ds(rows_of(half, piece), piece_rows)],
            dst_ref=region(layer, part, half, piece),
            send_sem=halo_sems.at[0, layer, part, half, piece], recv_sem=halo_sems.at[1, layer, part, half, piece],
            device_id={"tile": me - 1}, device_id_type=MESH)

    def hand_over(layer, part, half, piece):
        return pltpu.make_async_remote_copy(
            src_ref=region(layer, part, half, piece), dst_ref=region(layer, part, half, piece),
            send_sem=halo_sems.at[2, layer, part, half, piece], recv_sem=halo_sems.at[1, layer, part, half, piece],
            device_id={"mode": partner}, device_id_type=MESH)

    def each_piece(layer, halves, action):
        for part in range(2):
            for piece in range(PIECES):
                for half in halves:
                    action(layer, part, half, piece)

    def start_halo():
        for layer in range(layers):
            @pl.when(has_last & (near == 1))
            def _():
                each_piece(layer, (0, 1), lambda *which: halo(*which).start())

            @pl.when(has_last & (near == 0))
            def _():
                each_piece(layer, (odd,), lambda *which: halo(*which).start())

    def pass_halo(layer):
        def one(*which):
            halo(*which).wait_recv()
            hand_over(*which).start()

        @pl.when(has_next & (near == 1))
        def _():
            each_piece(layer, (odd,), one)

    def take_halo(layer):
        @pl.when(has_next & (near == 0))
        def _():
            each_piece(layer, (0, 1), lambda *which: halo(*which).wait_recv())

        @pl.when(has_next & (near == 1))
        def _():
            each_piece(layer, (1 - odd,), lambda *which: halo(*which).wait_recv())

    def end_halo():
        for layer in range(layers):
            @pl.when(has_last & (near == 1))
            def _():
                each_piece(layer, (0, 1), lambda *which: halo(*which).wait_send())

            @pl.when(has_last & (near == 0))
            def _():
                each_piece(layer, (odd,), lambda *which: halo(*which).wait_send())

            @pl.when(has_next & (near == 1))
            def _():
                each_piece(layer, (odd,), lambda *which: hand_over(*which).wait_send())

    def rim_copy(k):
        return pltpu.make_async_remote_copy(
            src_ref=total_ref.at[k // per_part, per_part + k % per_part], dst_ref=rim_in_ref.at[k],
            send_sem=rim_sems.at[0, k], recv_sem=rim_sems.at[1, k],
            device_id={"tile": me + 1}, device_id_type=MESH)

    def other(stride):
        return me + (1 - 2 * lax.rem(me // stride, 2)) * stride

    core, bit_x, bit_y = lax.rem(me, 2), lax.rem(me // 2, 2), lax.rem(me // 4, 2)
    mate, side_x, side_y = other(1), other(2), other(4)
    inner = (plane > 0) & (plane < 3)
    outer = jnp.logical_not(inner)
    across = 3 - plane
    twin = partner
    far_inner = jnp.where(inner, across, 3 - partner)
    far_outer = jnp.where(inner, 3 - partner, across)

    def own(k):
        return total_ref[k // per_part, k % per_part]

    line = Line(own, out_ref, up_ref, down_ref, send_ref, sems)

    def remote(source, target, sent, received, **device):
        return pltpu.make_async_remote_copy(
            src_ref=source, dst_ref=target, send_sem=sent, recv_sem=received,
            device_id=device, device_id_type=MESH)

    def share(p, parity, sent, received, **device):
        region = modes_ref.at[local_modes * p + parity, core]
        return remote(region, region, share_sems.at[0, sent, p], share_sems.at[1, received, p], **device)

    def share_own(to):
        region = modes_ref.at[local_modes * plane + bit_y, core]
        return remote(probe_ref.at[bit_y, core], region, share_sems.at[0, 0 if to is twin else 1, plane],
                      share_sems.at[1, 0, plane], mode=to)

    to_twin = lambda p: share(p, bit_y, 0, 0, mode=twin)
    to_across = lambda p: share(p, bit_y, 1, 0, mode=across)
    to_mate = lambda p: share(p, bit_y, 2, 2, tile=mate)
    to_side = lambda p: share(p, bit_y, 3, 1, tile=side_y)
    rest_to_mate = lambda p: share(p, 1 - bit_y, 4, 3, tile=mate)

    def from_mate(p, parity, kind):
        region = modes_ref.at[local_modes * p + parity, 1 - core]
        return remote(region, region, share_sems.at[0, 2, p], share_sems.at[1, kind, p], tile=mate)

    def spread_piece(p):
        to_mate(p).start()
        to_side(p).start()

    def serve_twin():
        to_twin(twin).wait_recv()

        @pl.when(inner)
        def _():
            to_across(twin).start()
        spread_piece(twin)

    def serve_far(p):
        to_twin(p).wait_recv()

        @pl.when(inner)
        def _():
            to_twin(p).start()
        spread_piece(p)

    def serve_side(p):
        share(p, 1 - bit_y, 3, 1, tile=side_y).wait_recv()
        rest_to_mate(p).start()

    def have(p):
        from_mate(p, bit_y, 2).wait_recv()
        from_mate(p, 1 - bit_y, 3).wait_recv()

    def end_share():
        share_own(twin).wait_send()

        @pl.when(inner)
        def _():
            share_own(across).wait_send()
            to_across(twin).wait_send()
            to_twin(far_inner).wait_send()
            to_twin(far_outer).wait_send()
        for p in (twin, far_inner, far_outer):
            to_mate(p).wait_send()
            to_side(p).wait_send()
            rest_to_mate(p).wait_send()

    def fetch(number):
        source, target = ((phase_in_ref, phase_ref), (measured_in_ref.at[plane], measured_ref),
                          (own_ref, ext_ref.at[:, :, pl.ds(0, tile_rows)]),
                          (left_in_ref, left_ref), (right_in_ref, right_ref),
                          (probe_ref, modes_ref.at[pl.ds(plane * local_modes, local_modes)]))[number]
        return pltpu.make_async_copy(source, target, fetch_sems.at[number])

    for number in range(6):
        fetch(number).start()
    barrier = pltpu.get_barrier_semaphore()
    count = line.greet(barrier)
    for stride in (1, 2, 4):
        pl.semaphore_signal(barrier, inc=1, device_id={"tile": other(stride)}, device_id_type=MESH)

    @pl.when(has_next)
    def _():
        pl.semaphore_signal(barrier, inc=1, device_id={"tile": me + 1}, device_id_type=MESH)

    @pl.when(has_last)
    def _():
        pl.semaphore_signal(barrier, inc=1, device_id={"tile": me - 1}, device_id_type=MESH)

    pl.semaphore_wait(barrier, count + bits + has_next.astype(jnp.int32) + has_last.astype(jnp.int32))

    start_halo()
    share_own(twin).start()

    @pl.when(inner)
    def _():
        share_own(across).start()

    @pl.when(jnp.logical_not(has_next))
    def _():
        ext_ref[:, :, tile_rows:, :] = jnp.zeros((layers, 2, width, columns), F32)

    fetch(0).wait()
    phase = to_even_odd(phase_ref[...])
    prop_ref[0] = jnp.cos(phase)
    prop_ref[1] = jnp.sin(phase)
    fetch(1).wait()
    target_ref[...] = to_even_odd(measured_ref[...])
    for number in range(2, 6):
        fetch(number).wait()

    def chosen(amount, bit, yes, no):
        return jnp.where(jnp.full(yes.shape, amount & bit, jnp.int32) > 0, yes, no)

    steps = [1 << level for level in reversed(range(3, (tile_rows - 1).bit_length()))]
    pair = lambda ref, *place: (ref[(*place, 0)], ref[(*place, 1)])
    prop = lambda: pair(prop_ref)

    def cut_window(layer):
        row = row_ref[plane]
        pick = shift_pick((columns, width), col_ref[plane], 1)
        for part in range(2):
            block = ext_ref[layer, part]
            for step in steps:
                size = block.shape[0] - step
                block = chosen(row, step, block[step:], block[:size])
            size = block.shape[0]
            for step in (4, 2, 1):
                block = chosen(row, step, pltpu.roll(block, size - step, 0), block)
            window_ref[layer, part] = select(block[:width], pick, 2)

    def put_back(layer):
        row = row_ref[plane]
        pick = shift_pick((width, columns), col_ref[plane], 0)
        for part in range(2):
            block = jnp.concatenate([select(piece_ref[part], pick, 2), jnp.zeros((8, columns), F32)], axis=0)
            for step in (1, 2, 4):
                block = chosen(row, step, pltpu.roll(block, step, 0), block)
            for step in reversed(steps):
                space = jnp.zeros((step, columns), F32)
                block = chosen(row, step, jnp.concatenate([space, block], axis=0), jnp.concatenate([block, space], axis=0))
            total_ref[layer * 2 + part] = block.reshape(total_ref.shape[1:])

    near_planes, far_planes = (plane, twin), (far_inner, far_outer)
    members = lambda planes: [local_modes * p + i for p in planes for i in range(local_modes)]

    def forward(planes, after_first, after_second, first):
        batch = members(planes)
        waves = [times(pair(modes_ref, m), pair(window_ref, 0)) for m in batch]
        spectra = transform(waves, left_ref, right_ref, 0)
        after_first()
        moved = transform([times(prop(), field) for field in spectra], left_ref, right_ref, 1)
        for m, field in zip(batch, moved):
            for part in range(2):
                before_ref[m, part] = field[part]
        after_second()
        waves = [times(pair(before_ref, m), pair(window_ref, 1)) for m in batch]
        far = transform(waves, left_ref, right_ref, 0)
        power = None if first else power_ref[...]
        for m, field in zip(batch, far):
            for part in range(2):
                far_ref[m, part] = field[part]
                here = field[part] * field[part]
                power = here if power is None else power + here
        power_ref[...] = power

    def add_up(fields, first):
        for part in range(2):
            total = fields[0][part] if first else piece_ref[part] + fields[0][part]
            for field in fields[1:]:
                total = total + field[part]
            piece_ref[part] = total

    def first_back(planes, first):
        batch = members(planes)
        weight = power_ref[...]
        waves = [(weight * far_ref[m, 0], weight * far_ref[m, 1]) for m in batch]
        back = transform(waves, left_ref, right_ref, 1)
        add_up([times_conj(pair(before_ref, m), field) for m, field in zip(batch, back)], first)
        for m, field in zip(batch, back):
            for part in range(2):
                far_ref[m, part] = field[part]

    def second_back(planes, first, between):
        batch = members(planes)
        waves = [times_conj(pair(window_ref, 1), pair(far_ref, m)) for m in batch]
        inner_fields = transform(waves, left_ref, right_ref, 0)
        between()
        back = transform([times_conj(prop(), field) for field in inner_fields], left_ref, right_ref, 1)
        add_up([times_conj(pair(modes_ref, m), field) for m, field in zip(batch, back)], first)
        for m, field in zip(batch, back):
            grad = times_conj(pair(window_ref, 0), field)
            for part in range(2):
                grad_ref[m, part] = grad[part]

    serve_twin()
    pass_halo(0)
    take_halo(0)

    @pl.when(inner)
    def _():
        serve_far(far_inner)
    cut_window(0)
    serve_side(twin)
    for layer in range(1, layers):
        pass_halo(layer)
    have(twin)

    def after_first():
        @pl.when(outer)
        def _():
            serve_far(far_inner)
        for layer in range(1, layers):
            take_halo(layer)
            cut_window(layer)

    def after_second():
        @pl.when(inner)
        def _():
            serve_far(far_outer)
        serve_side(far_inner)

    forward(near_planes, after_first, after_second, True)

    @pl.when(outer)
    def _():
        serve_far(far_outer)
    serve_side(far_outer)
    have(far_inner)
    have(far_outer)
    forward(far_planes, lambda: None, lambda: None, False)

    live = jnp.where(jnp.full((width, width), count_ref[0], jnp.int32) > plane, 1.0 / modes, 0.0)
    power_ref[...] = (power_ref[...] - target_ref[...]) * live
    first_back(near_planes, True)
    first_back(far_planes, False)
    put_back(1)

    def send_rim(layer):
        @pl.when(has_next)
        def _():
            def one(k, carry):
                rim_copy(layer * per_layer + k).start()
                return carry
            lax.fori_loop(0, per_layer, one, 0)

    def add_rim(k):
        @pl.when(has_last)
        def _():
            rim_copy(k).wait_recv()
            total_ref[k // per_part, k % per_part] += rim_in_ref[k]

    def gather_outer(k):
        add_rim(stored(k))
        line.gather_outer(stored(k))

    line_lags = ((1, gather_outer), (4, lambda k: line.gather_inner(stored(k))),
                 (8, lambda k: line.spread_middle(stored(k))), (12, lambda k: line.spread_outer(stored(k))))
    end = LINE_BLOCKS + 12
    hooks = [0]

    def line_hooks(number):
        def one(h, carry):
            for lag, action in line_lags:
                @pl.when((h >= lag) & (h < lag + LINE_BLOCKS))
                def _():
                    action(h - lag)
            return carry
        number = min(number, end - hooks[0])
        lax.fori_loop(hooks[0], hooks[0] + number, one, 0)
        hooks[0] += number

    def core_copy(m):
        return remote(grad_ref.at[m, 1 - core], core_in_ref.at[m], core_sems.at[0, m], core_sems.at[1, m], tile=mate)

    def first_copy(p):
        return remote(core_sum_ref.at[local_modes * p + 1 - bit_y], first_in_ref.at[p],
                      first_sems.at[0, p], first_sems.at[1, p], tile=side_y)

    def rows_x(which):
        return pl.ds(pl.multiple_of(which * half, 8), half)

    def second_copy(p):
        return remote(first_sum_ref.at[p, rows_x(1 - bit_x)], second_in_ref.at[p],
                      second_sems.at[0, p], second_sems.at[1, p], tile=side_x)

    def send_core(planes):
        for m in members(planes):
            core_copy(m).start()

    def take_core(planes):
        for m in members(planes):
            core_copy(m).wait_recv()
            core_sum_ref[m] = grad_ref[m, core] + core_in_ref[m]
        for p in planes:
            first_copy(p).start()

    def take_first(planes):
        for p in planes:
            first_copy(p).wait_recv()
            first_sum_ref[p] = core_sum_ref[local_modes * p + bit_y] + first_in_ref[p]
            second_copy(p).start()

    def take_second(planes):
        for p in planes:
            second_copy(p).wait_recv()
            second_sum_ref[p] = first_sum_ref[p, rows_x(bit_x)] + second_in_ref[p]

    def plane_copy(slot, source, **device):
        return remote(source, plane_in_ref.at[slot], plane_sems.at[0, slot], plane_sems.at[1, slot], **device)

    inward = lambda slot, p: plane_copy(slot, second_sum_ref.at[p], mode=twin)
    cross = lambda slot: plane_copy(3 + slot, plane_out_ref.at[slot], mode=across)
    outward = lambda: plane_copy(5, plane_out_ref.at[2], mode=twin)

    def send_inward():
        @pl.when(outer)
        def _():
            inward(0, far_inner).start()
            inward(1, far_outer).start()

    def send_twin():
        @pl.when(outer)
        def _():
            inward(2, twin).start()

    def send_cross():
        @pl.when(inner)
        def _():
            for slot, p in enumerate((far_inner, far_outer)):
                inward(slot, p).wait_recv()
                plane_out_ref[slot] = second_sum_ref[p] + plane_in_ref[slot]
                cross(slot).start()

    final = probe_out_ref.at[bit_y, core, rows_x(bit_x)]

    def take_cross():
        @pl.when(inner)
        def _():
            cross(1).wait_recv()
            plane_out_ref[2] = second_sum_ref[twin] + plane_in_ref[4]
            outward().start()
            cross(0).wait_recv()
            inward(2, plane).wait_recv()
            final[...] = second_sum_ref[plane] + plane_in_ref[2] + plane_in_ref[3]

    def take_outward():
        @pl.when(outer)
        def _():
            outward().wait_recv()
            final[...] = second_sum_ref[plane] + plane_in_ref[5]

    def spread_x(which):
        region = probe_out_ref.at[bit_y, core, rows_x(which)]
        return remote(region, region, spread_sems.at[0, 0], spread_sems.at[1, 0], tile=side_x)

    def spread_y(which):
        region = probe_out_ref.at[which, core]
        return remote(region, region, spread_sems.at[0, 1], spread_sems.at[1, 1], tile=side_y)

    def spread_core(parity, which):
        region = probe_out_ref.at[parity, which]
        return remote(region, region, spread_sems.at[0, 2 + parity], spread_sems.at[1, 2 + parity], tile=mate)

    for layer in range(layers - 1, 0, -1):
        send_rim(layer)
    second_back(far_planes, True, lambda: line_hooks(3))
    send_core(far_planes)
    line_hooks(3)

    def between():
        take_core(far_planes)
        line_hooks(4)

    second_back(near_planes, False, between)
    send_core(near_planes)
    put_back(0)
    send_rim(0)
    take_core(near_planes)
    line_hooks(4)
    take_first(far_planes)
    line_hooks(3)
    take_second(far_planes)
    send_inward()
    line_hooks(2)
    take_first(near_planes)
    line_hooks(3)
    take_second(near_planes)
    send_twin()
    line_hooks(2)
    send_cross()
    line_hooks(6)
    take_cross()
    line_hooks(4)
    take_outward()
    spread_x(bit_x).start()
    line_hooks(3)
    spread_x(1 - bit_x).wait_recv()
    spread_y(bit_y).start()
    line_hooks(4)
    spread_y(1 - bit_y).wait_recv()
    for parity in range(2):
        spread_core(parity, core).start()
    line_hooks(end)
    for parity in range(2):
        spread_core(parity, 1 - core).wait_recv()

    end_halo()
    end_share()
    line.drain()
    for m in members((plane, twin, far_inner, far_outer)):
        core_copy(m).wait_send()
    for p in (plane, twin, far_inner, far_outer):
        first_copy(p).wait_send()
        second_copy(p).wait_send()

    @pl.when(outer)
    def _():
        inward(0, far_inner).wait_send()
        inward(1, far_outer).wait_send()
        inward(2, twin).wait_send()

    @pl.when(inner)
    def _():
        cross(0).wait_send()
        cross(1).wait_send()
        outward().wait_send()
    spread_x(bit_x).wait_send()
    spread_y(bit_y).wait_send()
    for parity in range(2):
        spread_core(parity, core).wait_send()

    @pl.when(has_next)
    def _():
        def sent(k, carry):
            rim_copy(k).wait_send()
            return carry
        lax.fori_loop(0, LINE_BLOCKS, sent, 0)


def by_slot(object_field, probe, measured, prop_phase, counts, row_offset, col_offset):
    layers, _, tile_rows, columns = object_field.shape
    width = probe.shape[-1]
    planes = lax.axis_size("mode")
    modes = probe.shape[0] * planes
    left, right = (jnp.asarray(table) for table in dft_constants(width))
    smem = pl.BlockSpec(memory_space=pltpu.SMEM)
    vmem = lambda *shape: pltpu.VMEM(shape, F32)
    dma = lambda *shape: pltpu.SemaphoreType.DMA(shape)
    own_blocks = (LINE_BLOCKS, layers * 2 * tile_rows // LINE_BLOCKS, columns)
    block = vmem(*own_blocks)
    field = vmem(modes, 2, width, width)
    image = (width, width)
    piece = (width // 2, width)
    object_grad, probe_grad = pl.pallas_call(
        slot_kernel,
        out_shape=(jax.ShapeDtypeStruct(own_blocks, F32), jax.ShapeDtypeStruct(probe.shape, F32)),
        in_specs=[smem] * 3 + [pl.BlockSpec(memory_space=pl.ANY)] * 6,
        out_specs=(VMEM_SPEC, VMEM_SPEC),
        scratch_shapes=[
            field, vmem(*image), vmem(*image), pltpu.VMEM(left.shape, BF16), pltpu.VMEM(right.shape, BF16),
            vmem(layers, 2, tile_rows + width, columns), vmem(2, *image), vmem(*image), vmem(layers, 2, *image),
            field, field, vmem(*image), vmem(2, *image),
            vmem(layers * 2, (tile_rows + width) // own_blocks[1], *own_blocks[1:]), field,
            vmem(modes, *image), vmem(modes, *image), vmem(planes, *image), vmem(planes, *image),
            vmem(planes, *piece), vmem(planes, *piece), vmem(6, *piece), vmem(3, *piece),
            block, block, block, block,
            dma(6), dma(3, layers, 2, 2, PIECES), dma(4, LINE_BLOCKS), dma(2, LINE_BLOCKS), dma(2, 5, planes),
            dma(2, modes), dma(2, planes), dma(2, planes), dma(2, 6), dma(2, 4)],
        compiler_params=pltpu.CompilerParams(collective_id=0, has_side_effects=True, vmem_limit_bytes=62 << 20),
        name="by_slot",
    )(counts, row_offset, col_offset, object_field, probe, prop_phase, measured, left, right)
    return object_grad.reshape(object_field.shape), probe_grad


def per_device(object_field, probe, measured, *rest):
    fits = (lax.axis_size("mode") == measured.shape[0] == 4 and lax.axis_size("tile") == 8 and probe.shape[0] == 2)
    return (by_slot if fits else by_mode)(object_field, probe, measured, *rest)


def by_mode(object_field, probe, measured, prop_phase, counts, row_offset, col_offset):
    layers, _, tile_rows, columns = object_field.shape
    width = probe.shape[-1]
    local_modes = probe.shape[0]
    slots = row_offset.shape[0]
    bits = lax.axis_size("tile").bit_length() - 1
    left, right = (jnp.asarray(table) for table in dft_constants(width))
    smem = pl.BlockSpec(memory_space=pltpu.SMEM)
    field = pltpu.VMEM((slots, local_modes, 2, width, width), F32)
    power = pltpu.VMEM((BLOCKS, slots * width // BLOCKS, width), F32)
    own_blocks = (BLOCKS, layers * 2 * tile_rows // BLOCKS, columns)
    block = pltpu.VMEM(own_blocks, F32)
    ext = pltpu.VMEM((layers, 2, tile_rows + width, columns), F32)
    halves = (2, local_modes * width, width)
    parts = pltpu.VMEM((bits, *halves[1:]), F32)
    dma = pltpu.SemaphoreType.DMA
    object_grad, probe_grad = pl.pallas_call(
        ptycho_kernel,
        out_shape=(jax.ShapeDtypeStruct(own_blocks, F32), jax.ShapeDtypeStruct(halves, F32)),
        in_specs=[smem] * 3 + [pl.BlockSpec(memory_space=pl.ANY)] * 6,
        out_specs=(VMEM_SPEC, VMEM_SPEC),
        scratch_shapes=[
            pltpu.VMEM(probe.shape, F32), pltpu.VMEM((width, width), F32), pltpu.VMEM(measured.shape, F32),
            pltpu.VMEM(left.shape, BF16), pltpu.VMEM(right.shape, BF16),
            ext, pltpu.VMEM((2, width, width), F32), pltpu.VMEM((slots, width, width), F32),
            pltpu.VMEM((slots, layers, 2, width, width), F32), field, field, power, power,
            power, power, power, pltpu.VMEM((2, width, width), F32),
            ext, pltpu.VMEM(halves, F32),
            block, block, block, block, parts, parts,
            dma((6,)), dma((3, layers, 2, 2)), dma((4, BLOCKS)), dma((4, BLOCKS)), dma((2, BLOCKS)), dma((2, bits + 1))],
        compiler_params=pltpu.CompilerParams(collective_id=0, has_side_effects=True, vmem_limit_bytes=62 << 20),
        name="ptycho",
    )(counts, row_offset, col_offset, object_field, probe, prop_phase, measured, left, right)
    return object_grad.reshape(object_field.shape), probe_grad.reshape(probe.shape)


def solution(mesh):
    placed = (
        P(None, None, "tile", None),
        P("mode", None, None, None),
        P("tile", None, None),
        P(),
        P("tile"),
        P("tile"),
        P("tile"),
    )
    return jax.shard_map(
        per_device,
        mesh=mesh,
        in_specs=placed,
        out_specs=(P(None, None, "tile", None), P("mode", None, None, None)),
        check_vma=False,
    )
```

```python
import functools
import math

import jax
import jax.numpy as jnp
import numpy as np
from jax import lax
from jax.experimental import pallas as pl
from jax.experimental.pallas import tpu as pltpu
from jax.sharding import PartitionSpec as P

F32 = jnp.float32
BF16 = jnp.bfloat16
MESH = pl.DeviceIdType.MESH
BLOCKS = 16
LINE_BLOCKS = 32
PIECES = 2
VMEM_SPEC = pl.BlockSpec(memory_space=pltpu.VMEM)


def shifted(block, axis, distance):
    devices = range(lax.axis_size(axis))
    route = [(i - distance, i) for i in devices if i - distance in devices]
    return lax.ppermute(block, axis, route)


def dft_constants(length):
    half = length // 2
    n, k = np.arange(half)[:, None], np.arange(half)[None, :]
    sides = []
    for side in ("left", "right"):
        for way in range(2):
            for parity in range(2):
                angle = (n * (2 * k + parity) % length) * (2.0 * math.pi / length)
                real = np.cos(angle) / math.sqrt(length)
                imag = (-np.sin(angle) if way == 0 else np.sin(angle)) / math.sqrt(length)
                if (side == "left") == (way == 0):
                    real, imag = real.T, imag.T
                if side == "left":
                    table = np.block([[real, -imag], [imag, real]])
                else:
                    table = np.block([[real, imag], [-imag, real]])
                high = table.astype(BF16)
                sides += [high, (table - high.astype(np.float64)).astype(BF16)]
    tables = np.stack(sides).reshape(2, 2, 2, 2, length, length)
    left, right = ([[[table[0], table[0], table[1]] for table in way] for way in side] for side in tables)
    return (np.stack([[np.concatenate(table, axis=1) for table in way] for way in left]),
            np.stack([[np.concatenate(table, axis=0) for table in way] for way in right]))


def split(x, axis):
    high = x.astype(BF16)
    low = (x - high.astype(F32)).astype(BF16)
    return jnp.concatenate([high, low, high], axis=axis)


def one_side(fields, product, axis, way):
    size = fields[0][0].shape[axis]
    half = size // 2
    first = lambda x: lax.slice_in_dim(x, 0, half, axis=axis)
    second = lambda x: lax.slice_in_dim(x, half, size, axis=axis)
    join = lambda x, y: jnp.concatenate([x, y], axis=axis)
    beside = lambda blocks: jnp.concatenate(blocks, axis=1 - axis)
    if way == 0:
        even = [join(first(x) + second(x), first(y) + second(y)) for x, y in fields]
        odd = [join(first(x) - second(x), first(y) - second(y)) for x, y in fields]
    else:
        even = [join(first(x), first(y)) for x, y in fields]
        odd = [join(second(x), second(y)) for x, y in fields]
    even = product(split(beside(even), axis), 0)
    odd = product(split(beside(odd), axis), 1)
    if way == 1:
        even, odd = even + odd, even - odd
    results = []
    for i in range(len(fields)):
        cut = lambda x: lax.slice_in_dim(x, i * size, (i + 1) * size, axis=1 - axis)
        results.append((join(first(cut(even)), first(cut(odd))), join(second(cut(even)), second(cut(odd)))))
    return results


def transform(fields, left_ref, right_ref, way):
    on_left = lambda x, parity: jnp.dot(left_ref[way, parity], x, preferred_element_type=F32)
    on_right = lambda x, parity: jnp.dot(x, right_ref[way, parity], preferred_element_type=F32)
    return one_side(one_side(fields, on_left, 0, way), on_right, 1, way)


def times(a, b):
    return a[0] * b[0] - a[1] * b[1], a[0] * b[1] + a[1] * b[0]


def times_conj(a, b):
    return a[0] * b[0] + a[1] * b[1], a[0] * b[1] - a[1] * b[0]


def one_hot(condition):
    return jnp.where(condition, 1.0, 0.0).astype(BF16)


def shift_pick(shape, offset, axis):
    here = lax.broadcasted_iota(jnp.int32, shape, axis) + offset
    return one_hot(here == lax.broadcasted_iota(jnp.int32, shape, 1 - axis))


def pieces(x, number):
    parts = []
    for _ in range(number):
        parts.append(x.astype(BF16))
        x = x - parts[-1].astype(F32)
    return parts


def select(x, pick, number):
    total = None
    for piece in pieces(x, number):
        part = jnp.dot(piece, pick, preferred_element_type=F32)
        total = part if total is None else total + part
    return total


def to_even_odd(field):
    n = field.shape[-1]
    source = lax.broadcasted_iota(jnp.int32, (n, n), 0)
    place = lax.broadcasted_iota(jnp.int32, (n, n), 1)
    half = n // 2
    pick_right = one_hot(source == jnp.where(place < half, 2 * place, 2 * place - (n - 1)))
    pick_left = one_hot(place == jnp.where(source < half, 2 * source, 2 * source - (n - 1)))
    rows = None
    for piece in pieces(field, 3):
        part = jnp.dot(pick_left, piece, preferred_element_type=F32)
        rows = part if rows is None else rows + part
    return select(rows, pick_right, 3)


class Line:
    def __init__(self, own, out_ref, up_ref, down_ref, send_ref, sems):
        self.own, self.out, self.up, self.down, self.send = own, out_ref, up_ref, down_ref, send_ref
        self.sems = sems
        self.n = lax.axis_size("mode")
        self.blocks = out_ref.shape[0]
        place = lax.axis_index("mode")
        left = place < self.n // 2
        self.depth = jnp.where(left, place, self.n - 1 - place)
        self.inward = jnp.where(left, place + 1, place - 1)
        self.outward = jnp.where(left, place - 1, place + 1)
        self.middle = self.depth == self.n // 2 - 1
        self.inner = self.depth > 0

    def copy(self, source, target, sent, received, device, k):
        return pltpu.make_async_remote_copy(
            src_ref=source.at[k], dst_ref=target.at[k],
            send_sem=self.sems.at[sent, k], recv_sem=self.sems.at[received, k],
            device_id={"mode": device}, device_id_type=MESH)

    def in_up(self, k):
        return self.copy(self.send, self.up, 0, 2, self.inward, k)

    def in_across(self, k):
        return self.copy(self.send, self.down, 0, 3, self.inward, k)

    def out_down(self, k):
        return self.copy(self.out, self.out, 1, 3, self.outward, k)

    def greet(self, barrier):
        pl.semaphore_signal(barrier, inc=1, device_id={"mode": self.inward}, device_id_type=MESH)

        @pl.when(self.inner)
        def _():
            pl.semaphore_signal(barrier, inc=1, device_id={"mode": self.outward}, device_id_type=MESH)

        return jnp.where(self.inner, 2, 1)

    def forward(self, k):
        @pl.when(self.middle)
        def _():
            self.in_across(k).start()

        @pl.when(jnp.logical_not(self.middle))
        def _():
            self.in_up(k).start()

    def gather_outer(self, k):
        @pl.when(jnp.logical_not(self.inner))
        def _():
            self.send[k] = self.own(k)
            self.forward(k)

    def gather_inner(self, k):
        @pl.when(self.inner)
        def _():
            self.in_up(k).wait_recv()
            self.send[k] = self.own(k) + self.up[k]
            self.forward(k)

    def spread_middle(self, k):
        @pl.when(self.middle)
        def _():
            self.in_across(k).wait_recv()
            self.out[k] = self.send[k] + self.down[k]

            @pl.when(self.inner)
            def _():
                self.out_down(k).start()

    def spread_outer(self, k):
        @pl.when(jnp.logical_not(self.middle))
        def _():
            self.in_across(k).wait_recv()

            @pl.when(self.inner)
            def _():
                self.out_down(k).start()

    def drain(self):
        def one(k, carry):
            self.in_up(k).wait_send()

            @pl.when(self.inner)
            def _():
                self.out_down(k).wait_send()
            return carry
        lax.fori_loop(0, self.blocks, one, 0)


def ptycho_kernel(count_ref, row_ref, col_ref, own_ref, probe_in_ref, phase_in_ref, measured_in_ref, left_in_ref, right_in_ref,
                  out_ref, probe_out_ref,
                  probe_ref, phase_ref, measured_ref, left_ref, right_ref, ext_ref, prop_ref, target_ref, window_ref, before_ref, far_ref, part_power_ref, power_ref,
                  power_up_ref, power_down_ref, power_send_ref, piece_ref, total_ref, probe_grad_ref,
                  up_ref, down_ref, send_ref, rim_in_ref, part_ref, got_ref,
                  fetch_sems, halo_sems, power_sems, sems, rim_sems, probe_sems):
    tiles = lax.axis_size("tile")
    me = lax.axis_index("tile")
    bits = tiles.bit_length() - 1
    has_next, has_last = me < tiles - 1, me > 0
    slots, layers = window_ref.shape[0], window_ref.shape[1]
    local_modes = probe_ref.shape[0]
    modes = local_modes * lax.axis_size("mode")
    width = probe_ref.shape[-1]
    tile_rows, columns = own_ref.shape[2:]
    per_slot = BLOCKS // slots
    slot_rows = width // per_slot
    per_layer = LINE_BLOCKS // layers
    per_part = per_layer // 2

    def stored(k):
        return (layers - 1 - k // per_layer) * per_layer + k % per_layer

    plane = lax.axis_index("mode")
    odd = lax.rem(plane, 2)
    partner = plane + 1 - 2 * odd
    near = lax.rem(me, 2)
    piece_rows = width // (2 * PIECES)

    def rows_of(half, piece):
        return pl.multiple_of((half * PIECES + piece) * piece_rows, 8)

    def region(layer, part, half, piece):
        return ext_ref.at[layer, part, pl.ds(tile_rows + rows_of(half, piece), piece_rows)]

    def halo(layer, part, half, piece):
        return pltpu.make_async_remote_copy(
            src_ref=own_ref.at[layer, part, pl.ds(rows_of(half, piece), piece_rows)],
            dst_ref=region(layer, part, half, piece),
            send_sem=halo_sems.at[0, layer, part, half, piece], recv_sem=halo_sems.at[1, layer, part, half, piece],
            device_id={"tile": me - 1}, device_id_type=MESH)

    def hand_over(layer, part, half, piece):
        return pltpu.make_async_remote_copy(
            src_ref=region(layer, part, half, piece), dst_ref=region(layer, part, half, piece),
            send_sem=halo_sems.at[2, layer, part, half, piece], recv_sem=halo_sems.at[1, layer, part, half, piece],
            device_id={"mode": partner}, device_id_type=MESH)

    def each_piece(layer, halves, action):
        for part in range(2):
            for piece in range(PIECES):
                for half in halves:
                    action(layer, part, half, piece)

    def start_halo():
        for layer in range(layers):
            @pl.when(has_last & (near == 1))
            def _():
                each_piece(layer, (0, 1), lambda *which: halo(*which).start())

            @pl.when(has_last & (near == 0))
            def _():
                each_piece(layer, (odd,), lambda *which: halo(*which).start())

    def pass_halo(layer):
        def one(*which):
            halo(*which).wait_recv()
            hand_over(*which).start()

        @pl.when(has_next & (near == 1))
        def _():
            each_piece(layer, (odd,), one)

    def take_halo(layer):
        @pl.when(has_next & (near == 0))
        def _():
            each_piece(layer, (0, 1), lambda *which: halo(*which).wait_recv())

        @pl.when(has_next & (near == 1))
        def _():
            each_piece(layer, (1 - odd,), lambda *which: halo(*which).wait_recv())

    def end_halo():
        for layer in range(layers):
            @pl.when(has_last & (near == 1))
            def _():
                each_piece(layer, (0, 1), lambda *which: halo(*which).wait_send())

            @pl.when(has_last & (near == 0))
            def _():
                each_piece(layer, (odd,), lambda *which: halo(*which).wait_send())

            @pl.when(has_next & (near == 1))
            def _():
                each_piece(layer, (odd,), lambda *which: hand_over(*which).wait_send())

    def finish_halo():
        for layer in range(1, layers):
            take_halo(layer)
            cut_window(0, layer)

    def rim_copy(k):
        return pltpu.make_async_remote_copy(
            src_ref=total_ref.at[k // per_part, per_part + k % per_part], dst_ref=rim_in_ref.at[k],
            send_sem=rim_sems.at[0, k], recv_sem=rim_sems.at[1, k],
            device_id={"tile": me + 1}, device_id_type=MESH)

    def other(step):
        bit = step and bits - step
        low = lax.rem(me // (1 << bit), 2)
        return me + (1 - 2 * low) * (1 << bit)

    side = lax.rem(me, 2)

    def probe_copy(step, source, target):
        return pltpu.make_async_remote_copy(
            src_ref=source, dst_ref=target,
            send_sem=probe_sems.at[0, step], recv_sem=probe_sems.at[1, step],
            device_id={"tile": other(0 if step == bits else step)}, device_id_type=MESH)

    def exchange(step):
        if step == 0:
            return probe_copy(0, probe_grad_ref.at[1 - side], got_ref.at[0])
        if step < bits:
            return probe_copy(step, part_ref.at[step - 1], got_ref.at[step])
        return probe_copy(step, part_ref.at[bits - 1], probe_out_ref.at[side])

    power_line = Line(lambda k: part_power_ref[k], power_ref, power_up_ref, power_down_ref, power_send_ref, power_sems)

    def own(k):
        return total_ref[k // per_part, k % per_part]

    line = Line(own, out_ref, up_ref, down_ref, send_ref, sems)

    def fetch(number):
        source, target = ((phase_in_ref, phase_ref), (measured_in_ref, measured_ref), (own_ref, ext_ref.at[:, :, pl.ds(0, tile_rows)]),
                          (left_in_ref, left_ref), (right_in_ref, right_ref), (probe_in_ref, probe_ref))[number]
        return pltpu.make_async_copy(source, target, fetch_sems.at[number])

    for number in range(6):
        fetch(number).start()
    barrier = pltpu.get_barrier_semaphore()
    count = line.greet(barrier)
    for bit in range(bits):
        pl.semaphore_signal(barrier, inc=1, device_id={"tile": other(bit)}, device_id_type=MESH)

    @pl.when(has_next)
    def _():
        pl.semaphore_signal(barrier, inc=1, device_id={"tile": me + 1}, device_id_type=MESH)

    @pl.when(has_last)
    def _():
        pl.semaphore_signal(barrier, inc=1, device_id={"tile": me - 1}, device_id_type=MESH)

    pl.semaphore_wait(barrier, count + bits + has_next.astype(jnp.int32) + has_last.astype(jnp.int32))

    start_halo()

    @pl.when(jnp.logical_not(has_next))
    def _():
        ext_ref[:, :, tile_rows:, :] = jnp.zeros((layers, 2, width, columns), F32)

    total_ref[...] = jnp.zeros_like(total_ref)
    probe_grad_ref[...] = jnp.zeros_like(probe_grad_ref)
    fetch(0).wait()
    phase = to_even_odd(phase_ref[...])
    prop_ref[0] = jnp.cos(phase)
    prop_ref[1] = jnp.sin(phase)
    fetch(1).wait()

    def order(slot, carry):
        target_ref[slot] = to_even_odd(measured_ref[slot])
        return carry
    lax.fori_loop(0, slots, order, 0)
    for number in range(2, 6):
        fetch(number).wait()

    def chosen(amount, bit, yes, no):
        return jnp.where(jnp.full(yes.shape, amount & bit, jnp.int32) > 0, yes, no)

    steps = [1 << level for level in reversed(range(3, (tile_rows - 1).bit_length()))]

    def cut_window(slot, layer):
        row = row_ref[slot]
        pick = shift_pick((columns, width), col_ref[slot], 1)
        for part in range(2):
            block = select(ext_ref[layer, part], pick, 2)
            for step in steps:
                size = block.shape[0] - step
                block = chosen(row, step, block[step:], block[:size])
            size = block.shape[0]
            for step in (4, 2, 1):
                block = chosen(row, step, pltpu.roll(block, size - step, 0), block)
            window_ref[slot, layer, part] = block[:width]

    def put_back(slot, layer):
        row = row_ref[slot]
        pick = shift_pick((width, columns), col_ref[slot], 0)
        for part in range(2):
            block = jnp.concatenate([select(piece_ref[part], pick, 2), jnp.zeros((8, columns), F32)], axis=0)
            for step in (1, 2, 4):
                block = chosen(row, step, pltpu.roll(block, step, 0), block)
            for step in reversed(steps):
                space = jnp.zeros((step, columns), F32)
                block = chosen(row, step, jnp.concatenate([space, block], axis=0), jnp.concatenate([block, space], axis=0))
            total_ref[layer * 2 + part] += block.reshape(total_ref.shape[1:])

    lag_gather, lag_middle, lag_outer = 6, 10, 12

    def within(k, blocks, action):
        if isinstance(k, int):
            if 0 <= k < blocks:
                action(k)
        else:
            @pl.when((k >= 0) & (k < blocks))
            def _():
                action(k)

    def power_hook(q):
        within(q - lag_gather, BLOCKS, power_line.gather_inner)
        within(q - lag_middle, BLOCKS, power_line.spread_middle)
        within(q - lag_outer, BLOCKS, power_line.spread_outer)

    pair = lambda ref, *place: (ref[(*place, 0)], ref[(*place, 1)])
    each = range(local_modes)
    prop = lambda: pair(prop_ref)

    def forward_slot(slot, carry):
        @pl.when(slot > 0)
        def _():
            for layer in range(layers):
                cut_window(slot, layer)

        waves = [times(pair(probe_ref, mode), pair(window_ref, slot, 0)) for mode in each]
        spectra = transform(waves, left_ref, right_ref, 0)

        @pl.when(slot == 0)
        def _():
            for layer in range(1, layers):
                pass_halo(layer)

        q = slot * per_slot
        for h in range(per_slot // 2):
            power_hook(q + h)
        moved = transform([times(prop(), field) for field in spectra], left_ref, right_ref, 1)
        for mode in each:
            for part in range(2):
                before_ref[slot, mode, part] = moved[mode][part]

        @pl.when(slot == 0)
        def _():
            finish_halo()

        for h in range(per_slot // 2, per_slot):
            power_hook(q + h)
        waves = [times(pair(before_ref, slot, mode), pair(window_ref, slot, 1)) for mode in each]
        far = transform(waves, left_ref, right_ref, 0)
        power = None
        for mode in each:
            for part in range(2):
                far_ref[slot, mode, part] = far[mode][part]
                here = far[mode][part] * far[mode][part]
                power = here if power is None else power + here
        for part in range(per_slot):
            part_power_ref[slot * per_slot + part] = power[part * slot_rows:(part + 1) * slot_rows]
        for part in range(per_slot):
            power_line.gather_outer(slot * per_slot + part)
        return carry

    pass_halo(0)
    take_halo(0)
    cut_window(0, 0)
    lax.fori_loop(0, slots, forward_slot, 0)
    hooks = [BLOCKS]

    def next_power_hook():
        power_hook(hooks[0])
        hooks[0] += 1

    def add_up(fields):
        for part in range(2):
            total = fields[0][part]
            for field in fields[1:]:
                total = total + field[part]
            piece_ref[part] = total

    def first_back(slot, hook):
        live = jnp.where(jnp.full((width, width), count_ref[0], jnp.int32) > slot, 1.0 / modes, 0.0)
        power = power_ref[slot * per_slot:(slot + 1) * per_slot].reshape(width, width)
        weight = (power - target_ref[slot]) * live
        waves = [(weight * far_ref[slot, mode, 0], weight * far_ref[slot, mode, 1]) for mode in each]
        back = transform(waves, left_ref, right_ref, 1)
        add_up([times_conj(pair(before_ref, slot, mode), back[mode]) for mode in each])
        for mode in each:
            for part in range(2):
                far_ref[slot, mode, part] = back[mode][part]
        for _ in range(per_slot // 2):
            hook()
        put_back(slot, 1)

    def second_back(slot, hook):
        waves = [times_conj(pair(window_ref, slot, 1), pair(far_ref, slot, mode)) for mode in each]
        inner = transform(waves, left_ref, right_ref, 0)
        for _ in range(per_slot // 2):
            hook()
        back = transform([times_conj(prop(), field) for field in inner], left_ref, right_ref, 1)
        add_up([times_conj(pair(probe_ref, mode), back[mode]) for mode in each])
        for mode in each:
            grad = times_conj(pair(window_ref, slot, 0), back[mode])
            for part in range(2):
                flat = mode * 2 + part
                first = flat % local_modes * width
                probe_grad_ref[flat // local_modes, first:first + width, :] += grad[part]
        for _ in range(per_slot // 2):
            hook()
        put_back(slot, 0)

    def ready(slot):
        while hooks[0] <= (slot + 1) * per_slot - 1 + lag_outer:
            next_power_hook()

    no_hook = lambda: None
    for slot in range(slots - 1):
        ready(slot)
        first_back(slot, no_hook)
    while hooks[0] < BLOCKS + lag_middle:
        next_power_hook()
    early = min(1, slots - 1)
    for slot in range(early):
        second_back(slot, no_hook)
    ready(slots - 1)
    first_back(slots - 1, no_hook)
    while hooks[0] < BLOCKS + lag_outer:
        next_power_hook()

    def send_rim(layer):
        @pl.when(has_next)
        def _():
            def one(k, carry):
                rim_copy(layer * per_layer + k).start()
                return carry
            lax.fori_loop(0, per_layer, one, 0)

    def add_rim(k):
        @pl.when(has_last)
        def _():
            rim_copy(k).wait_recv()
            total_ref[k // per_part, k % per_part] += rim_in_ref[k]

    def gather_outer(k):
        add_rim(stored(k))
        line.gather_outer(stored(k))

    line_lags = ((1, gather_outer), (4, lambda k: line.gather_inner(stored(k))),
                 (8, lambda k: line.spread_middle(stored(k))), (12, lambda k: line.spread_outer(stored(k))))
    end = LINE_BLOCKS + 12

    def line_hook(h):
        for lag, action in line_lags:
            within(h - lag, LINE_BLOCKS, action)

    hooks = [0]

    def next_line_hook():
        if hooks[0] < per_layer:
            line_hook(hooks[0])
            hooks[0] += 1

    def line_hooks(number):
        number = min(number, end - hooks[0])

        def one(i, carry):
            line_hook(i)
            return carry
        lax.fori_loop(hooks[0], hooks[0] + number, one, 0)
        hooks[0] += number

    def reduce_probe(bit):
        exchange(bit).wait_recv()
        part_ref[bit] = (probe_grad_ref[side] if bit == 0 else part_ref[bit - 1]) + got_ref[bit]
        exchange(bit + 1).start()

    for layer in range(layers - 1, 0, -1):
        send_rim(layer)
    for slot in range(early, slots):
        second_back(slot, next_line_hook)
    exchange(0).start()
    send_rim(0)
    line_hooks(2)
    reduce_probe(0)
    for bit in range(1, bits):
        line_hooks((end - 6 - hooks[0]) // (bits - bit))
        reduce_probe(bit)
    line_hooks(end)
    probe_out_ref[side] = part_ref[bits - 1]
    exchange(bits).wait_recv()
    for step in range(bits + 1):
        exchange(step).wait_send()
    power_line.drain()
    line.drain()

    @pl.when(has_next)
    def _():
        def sent(k, carry):
            rim_copy(k).wait_send()
            return carry
        lax.fori_loop(0, LINE_BLOCKS, sent, 0)

    end_halo()


def per_device(object_field, probe, measured, prop_phase, counts, row_offset, col_offset):
    layers, _, tile_rows, columns = object_field.shape
    width = probe.shape[-1]
    local_modes = probe.shape[0]
    slots = row_offset.shape[0]
    bits = lax.axis_size("tile").bit_length() - 1
    left, right = (jnp.asarray(table) for table in dft_constants(width))
    smem = pl.BlockSpec(memory_space=pltpu.SMEM)
    field = pltpu.VMEM((slots, local_modes, 2, width, width), F32)
    power = pltpu.VMEM((BLOCKS, slots * width // BLOCKS, width), F32)
    own_blocks = (LINE_BLOCKS, layers * 2 * tile_rows // LINE_BLOCKS, columns)
    block = pltpu.VMEM(own_blocks, F32)
    ext = pltpu.VMEM((layers, 2, tile_rows + width, columns), F32)
    halves = (2, local_modes * width, width)
    parts = pltpu.VMEM((bits, *halves[1:]), F32)
    dma = pltpu.SemaphoreType.DMA
    object_grad, probe_grad = pl.pallas_call(
        ptycho_kernel,
        out_shape=(jax.ShapeDtypeStruct(own_blocks, F32), jax.ShapeDtypeStruct(halves, F32)),
        in_specs=[smem] * 3 + [pl.BlockSpec(memory_space=pl.ANY)] * 6,
        out_specs=(VMEM_SPEC, VMEM_SPEC),
        scratch_shapes=[
            pltpu.VMEM(probe.shape, F32), pltpu.VMEM((width, width), F32), pltpu.VMEM(measured.shape, F32),
            pltpu.VMEM(left.shape, BF16), pltpu.VMEM(right.shape, BF16),
            ext, pltpu.VMEM((2, width, width), F32), pltpu.VMEM((slots, width, width), F32),
            pltpu.VMEM((slots, layers, 2, width, width), F32), field, field, power, power,
            power, power, power, pltpu.VMEM((2, width, width), F32),
            pltpu.VMEM((layers * 2, (tile_rows + width) // own_blocks[1], *own_blocks[1:]), F32), pltpu.VMEM(halves, F32),
            block, block, block, block, parts, parts,
            dma((6,)), dma((3, layers, 2, 2, PIECES)), dma((4, BLOCKS)), dma((4, LINE_BLOCKS)), dma((2, LINE_BLOCKS)), dma((2, bits + 1))],
        compiler_params=pltpu.CompilerParams(collective_id=0, has_side_effects=True, vmem_limit_bytes=62 << 20),
        name="ptycho",
    )(counts, row_offset, col_offset, object_field, probe, prop_phase, measured, left, right)
    return object_grad.reshape(object_field.shape), probe_grad.reshape(probe.shape)


def solution(mesh):
    placed = (
        P(None, None, "tile", None),
        P("mode", None, None, None),
        P("tile", None, None),
        P(),
        P("tile"),
        P("tile"),
        P("tile"),
    )
    return jax.shard_map(
        per_device,
        mesh=mesh,
        in_specs=placed,
        out_specs=(P(None, None, "tile", None), P("mode", None, None, None)),
        check_vma=False,
    )
```

```python
import functools
import math

import jax
import jax.numpy as jnp
import numpy as np
from jax import lax
from jax.experimental import pallas as pl
from jax.experimental.pallas import tpu as pltpu
from jax.sharding import PartitionSpec as P

F32 = jnp.float32
BF16 = jnp.bfloat16
MESH = pl.DeviceIdType.MESH
BLOCKS = 16
LINE_BLOCKS = 32
PIECES = 2
VMEM_SPEC = pl.BlockSpec(memory_space=pltpu.VMEM)


def shifted(block, axis, distance):
    devices = range(lax.axis_size(axis))
    route = [(i - distance, i) for i in devices if i - distance in devices]
    return lax.ppermute(block, axis, route)


def dft_constants(length):
    half = length // 2
    n, k = np.arange(half)[:, None], np.arange(half)[None, :]
    sides = []
    for side in ("left", "right"):
        for way in range(2):
            for parity in range(2):
                angle = (n * (2 * k + parity) % length) * (2.0 * math.pi / length)
                real = np.cos(angle) / math.sqrt(length)
                imag = (-np.sin(angle) if way == 0 else np.sin(angle)) / math.sqrt(length)
                if (side == "left") == (way == 0):
                    real, imag = real.T, imag.T
                if side == "left":
                    table = np.block([[real, -imag], [imag, real]])
                else:
                    table = np.block([[real, imag], [-imag, real]])
                high = table.astype(BF16)
                sides += [high, (table - high.astype(np.float64)).astype(BF16)]
    tables = np.stack(sides).reshape(2, 2, 2, 2, length, length)
    left, right = ([[[table[0], table[0], table[1]] for table in way] for way in side] for side in tables)
    return (np.stack([[np.concatenate(table, axis=1) for table in way] for way in left]),
            np.stack([[np.concatenate(table, axis=0) for table in way] for way in right]))


def split(x, axis):
    high = x.astype(BF16)
    low = (x - high.astype(F32)).astype(BF16)
    return jnp.concatenate([high, low, high], axis=axis)


def one_side(fields, product, axis, way):
    size = fields[0][0].shape[axis]
    half = size // 2
    first = lambda x: lax.slice_in_dim(x, 0, half, axis=axis)
    second = lambda x: lax.slice_in_dim(x, half, size, axis=axis)
    join = lambda x, y: jnp.concatenate([x, y], axis=axis)
    beside = lambda blocks: jnp.concatenate(blocks, axis=1 - axis)
    if way == 0:
        even = [join(first(x) + second(x), first(y) + second(y)) for x, y in fields]
        odd = [join(first(x) - second(x), first(y) - second(y)) for x, y in fields]
    else:
        even = [join(first(x), first(y)) for x, y in fields]
        odd = [join(second(x), second(y)) for x, y in fields]
    even = product(split(beside(even), axis), 0)
    odd = product(split(beside(odd), axis), 1)
    if way == 1:
        even, odd = even + odd, even - odd
    results = []
    for i in range(len(fields)):
        cut = lambda x: lax.slice_in_dim(x, i * size, (i + 1) * size, axis=1 - axis)
        results.append((join(first(cut(even)), first(cut(odd))), join(second(cut(even)), second(cut(odd)))))
    return results


def transform(fields, left_ref, right_ref, way):
    on_left = lambda x, parity: jnp.dot(left_ref[way, parity], x, preferred_element_type=F32)
    on_right = lambda x, parity: jnp.dot(x, right_ref[way, parity], preferred_element_type=F32)
    return one_side(one_side(fields, on_left, 0, way), on_right, 1, way)


def times(a, b):
    return a[0] * b[0] - a[1] * b[1], a[0] * b[1] + a[1] * b[0]


def times_conj(a, b):
    return a[0] * b[0] + a[1] * b[1], a[0] * b[1] - a[1] * b[0]


def one_hot(condition):
    return jnp.where(condition, 1.0, 0.0).astype(BF16)


def shift_pick(shape, offset, axis):
    here = lax.broadcasted_iota(jnp.int32, shape, axis) + offset
    return one_hot(here == lax.broadcasted_iota(jnp.int32, shape, 1 - axis))


def pieces(x, number):
    parts = []
    for _ in range(number):
        parts.append(x.astype(BF16))
        x = x - parts[-1].astype(F32)
    return parts


def select(x, pick, number):
    total = None
    for piece in pieces(x, number):
        part = jnp.dot(piece, pick, preferred_element_type=F32)
        total = part if total is None else total + part
    return total


def to_even_odd(field):
    n = field.shape[-1]
    source = lax.broadcasted_iota(jnp.int32, (n, n), 0)
    place = lax.broadcasted_iota(jnp.int32, (n, n), 1)
    half = n // 2
    pick_right = one_hot(source == jnp.where(place < half, 2 * place, 2 * place - (n - 1)))
    pick_left = one_hot(place == jnp.where(source < half, 2 * source, 2 * source - (n - 1)))
    rows = None
    for piece in pieces(field, 3):
        part = jnp.dot(pick_left, piece, preferred_element_type=F32)
        rows = part if rows is None else rows + part
    return select(rows, pick_right, 3)


class Line:
    def __init__(self, own, out_ref, up_ref, down_ref, send_ref, sems):
        self.own, self.out, self.up, self.down, self.send = own, out_ref, up_ref, down_ref, send_ref
        self.sems = sems
        self.n = lax.axis_size("mode")
        self.blocks = out_ref.shape[0]
        place = lax.axis_index("mode")
        left = place < self.n // 2
        self.depth = jnp.where(left, place, self.n - 1 - place)
        self.inward = jnp.where(left, place + 1, place - 1)
        self.outward = jnp.where(left, place - 1, place + 1)
        self.middle = self.depth == self.n // 2 - 1
        self.inner = self.depth > 0

    def copy(self, source, target, sent, received, device, k):
        return pltpu.make_async_remote_copy(
            src_ref=source.at[k], dst_ref=target.at[k],
            send_sem=self.sems.at[sent, k], recv_sem=self.sems.at[received, k],
            device_id={"mode": device}, device_id_type=MESH)

    def in_up(self, k):
        return self.copy(self.send, self.up, 0, 2, self.inward, k)

    def in_across(self, k):
        return self.copy(self.send, self.down, 0, 3, self.inward, k)

    def out_down(self, k):
        return self.copy(self.out, self.out, 1, 3, self.outward, k)

    def greet(self, barrier):
        pl.semaphore_signal(barrier, inc=1, device_id={"mode": self.inward}, device_id_type=MESH)

        @pl.when(self.inner)
        def _():
            pl.semaphore_signal(barrier, inc=1, device_id={"mode": self.outward}, device_id_type=MESH)

        return jnp.where(self.inner, 2, 1)

    def forward(self, k):
        @pl.when(self.middle)
        def _():
            self.in_across(k).start()

        @pl.when(jnp.logical_not(self.middle))
        def _():
            self.in_up(k).start()

    def gather_outer(self, k):
        @pl.when(jnp.logical_not(self.inner))
        def _():
            self.send[k] = self.own(k)
            self.forward(k)

    def gather_inner(self, k):
        @pl.when(self.inner)
        def _():
            self.in_up(k).wait_recv()
            self.send[k] = self.own(k) + self.up[k]
            self.forward(k)

    def spread_middle(self, k):
        @pl.when(self.middle)
        def _():
            self.in_across(k).wait_recv()
            self.out[k] = self.send[k] + self.down[k]

            @pl.when(self.inner)
            def _():
                self.out_down(k).start()

    def spread_outer(self, k):
        @pl.when(jnp.logical_not(self.middle))
        def _():
            self.in_across(k).wait_recv()

            @pl.when(self.inner)
            def _():
                self.out_down(k).start()

    def drain(self):
        def one(k, carry):
            self.in_up(k).wait_send()

            @pl.when(self.inner)
            def _():
                self.out_down(k).wait_send()
            return carry
        lax.fori_loop(0, self.blocks, one, 0)


def ptycho_kernel(count_ref, row_ref, col_ref, own_ref, probe_in_ref, phase_in_ref, measured_in_ref, left_in_ref, right_in_ref,
                  out_ref, probe_out_ref,
                  probe_ref, phase_ref, measured_ref, left_ref, right_ref, ext_ref, prop_ref, target_ref, window_ref, before_ref, far_ref, part_power_ref, power_ref,
                  power_up_ref, power_down_ref, power_send_ref, piece_ref, total_ref, probe_grad_ref,
                  up_ref, down_ref, send_ref, rim_in_ref, part_ref, got_ref,
                  fetch_sems, halo_sems, power_sems, sems, rim_sems, probe_sems):
    tiles = lax.axis_size("tile")
    me = lax.axis_index("tile")
    bits = tiles.bit_length() - 1
    has_next, has_last = me < tiles - 1, me > 0
    slots, layers = window_ref.shape[0], window_ref.shape[1]
    local_modes = probe_ref.shape[0]
    modes = local_modes * lax.axis_size("mode")
    width = probe_ref.shape[-1]
    tile_rows, columns = own_ref.shape[2:]
    per_slot = BLOCKS // slots
    slot_rows = width // per_slot
    per_layer = LINE_BLOCKS // layers
    per_part = per_layer // 2

    def stored(k):
        return (layers - 1 - k // per_layer) * per_layer + k % per_layer

    plane = lax.axis_index("mode")
    odd = lax.rem(plane, 2)
    partner = plane + 1 - 2 * odd
    near = lax.rem(me, 2)
    piece_rows = width // (2 * PIECES)

    def rows_of(half, piece):
        return pl.multiple_of((half * PIECES + piece) * piece_rows, 8)

    def region(layer, part, half, piece):
        return ext_ref.at[layer, part, pl.ds(tile_rows + rows_of(half, piece), piece_rows)]

    def halo(layer, part, half, piece):
        return pltpu.make_async_remote_copy(
            src_ref=own_ref.at[layer, part, pl.ds(rows_of(half, piece), piece_rows)],
            dst_ref=region(layer, part, half, piece),
            send_sem=halo_sems.at[0, layer, part, half, piece], recv_sem=halo_sems.at[1, layer, part, half, piece],
            device_id={"tile": me - 1}, device_id_type=MESH)

    def hand_over(layer, part, half, piece):
        return pltpu.make_async_remote_copy(
            src_ref=region(layer, part, half, piece), dst_ref=region(layer, part, half, piece),
            send_sem=halo_sems.at[2, layer, part, half, piece], recv_sem=halo_sems.at[1, layer, part, half, piece],
            device_id={"mode": partner}, device_id_type=MESH)

    def each_piece(layer, halves, action):
        for part in range(2):
            for piece in range(PIECES):
                for half in halves:
                    action(layer, part, half, piece)

    def start_halo():
        for layer in range(layers):
            @pl.when(has_last & (near == 1))
            def _():
                each_piece(layer, (0, 1), lambda *which: halo(*which).start())

            @pl.when(has_last & (near == 0))
            def _():
                each_piece(layer, (odd,), lambda *which: halo(*which).start())

    def pass_halo(layer):
        def one(*which):
            halo(*which).wait_recv()
            hand_over(*which).start()

        @pl.when(has_next & (near == 1))
        def _():
            each_piece(layer, (odd,), one)

    def take_halo(layer):
        @pl.when(has_next & (near == 0))
        def _():
            each_piece(layer, (0, 1), lambda *which: halo(*which).wait_recv())

        @pl.when(has_next & (near == 1))
        def _():
            each_piece(layer, (1 - odd,), lambda *which: halo(*which).wait_recv())

    def end_halo():
        for layer in range(layers):
            @pl.when(has_last & (near == 1))
            def _():
                each_piece(layer, (0, 1), lambda *which: halo(*which).wait_send())

            @pl.when(has_last & (near == 0))
            def _():
                each_piece(layer, (odd,), lambda *which: halo(*which).wait_send())

            @pl.when(has_next & (near == 1))
            def _():
                each_piece(layer, (odd,), lambda *which: hand_over(*which).wait_send())

    def finish_halo():
        for layer in range(1, layers):
            take_halo(layer)
            cut_window(0, layer)

    def rim_copy(k):
        return pltpu.make_async_remote_copy(
            src_ref=total_ref.at[k // per_part, per_part + k % per_part], dst_ref=rim_in_ref.at[k],
            send_sem=rim_sems.at[0, k], recv_sem=rim_sems.at[1, k],
            device_id={"tile": me + 1}, device_id_type=MESH)

    def other(step):
        bit = step and bits - step
        low = lax.rem(me // (1 << bit), 2)
        return me + (1 - 2 * low) * (1 << bit)

    side = lax.rem(me, 2)

    def probe_copy(step, source, target):
        return pltpu.make_async_remote_copy(
            src_ref=source, dst_ref=target,
            send_sem=probe_sems.at[0, step], recv_sem=probe_sems.at[1, step],
            device_id={"tile": other(0 if step == bits else step)}, device_id_type=MESH)

    def exchange(step):
        if step == 0:
            return probe_copy(0, probe_grad_ref.at[1 - side], got_ref.at[0])
        if step < bits:
            return probe_copy(step, part_ref.at[step - 1], got_ref.at[step])
        return probe_copy(step, part_ref.at[bits - 1], probe_out_ref.at[side])

    power_line = Line(lambda k: part_power_ref[k], power_ref, power_up_ref, power_down_ref, power_send_ref, power_sems)

    def own(k):
        return total_ref[k // per_part, k % per_part]

    line = Line(own, out_ref, up_ref, down_ref, send_ref, sems)

    def fetch(number):
        source, target = ((phase_in_ref, phase_ref), (measured_in_ref, measured_ref), (own_ref, ext_ref.at[:, :, pl.ds(0, tile_rows)]),
                          (left_in_ref, left_ref), (right_in_ref, right_ref), (probe_in_ref, probe_ref))[number]
        return pltpu.make_async_copy(source, target, fetch_sems.at[number])

    for number in range(6):
        fetch(number).start()
    barrier = pltpu.get_barrier_semaphore()
    count = line.greet(barrier)
    for bit in range(bits):
        pl.semaphore_signal(barrier, inc=1, device_id={"tile": other(bit)}, device_id_type=MESH)

    @pl.when(has_next)
    def _():
        pl.semaphore_signal(barrier, inc=1, device_id={"tile": me + 1}, device_id_type=MESH)

    @pl.when(has_last)
    def _():
        pl.semaphore_signal(barrier, inc=1, device_id={"tile": me - 1}, device_id_type=MESH)

    pl.semaphore_wait(barrier, count + bits + has_next.astype(jnp.int32) + has_last.astype(jnp.int32))

    start_halo()

    @pl.when(jnp.logical_not(has_next))
    def _():
        ext_ref[:, :, tile_rows:, :] = jnp.zeros((layers, 2, width, columns), F32)

    total_ref[...] = jnp.zeros_like(total_ref)
    probe_grad_ref[...] = jnp.zeros_like(probe_grad_ref)
    fetch(0).wait()
    phase = to_even_odd(phase_ref[...])
    prop_ref[0] = jnp.cos(phase)
    prop_ref[1] = jnp.sin(phase)
    fetch(1).wait()

    def order(slot, carry):
        target_ref[slot] = to_even_odd(measured_ref[slot])
        return carry
    lax.fori_loop(0, slots, order, 0)
    for number in range(2, 6):
        fetch(number).wait()

    def chosen(amount, bit, yes, no):
        return jnp.where(jnp.full(yes.shape, amount & bit, jnp.int32) > 0, yes, no)

    steps = [1 << level for level in reversed(range(3, (tile_rows - 1).bit_length()))]

    def cut_window(slot, layer):
        row = row_ref[slot]
        pick = shift_pick((columns, width), col_ref[slot], 1)
        for part in range(2):
            block = select(ext_ref[layer, part], pick, 2)
            for step in steps:
                size = block.shape[0] - step
                block = chosen(row, step, block[step:], block[:size])
            size = block.shape[0]
            for step in (4, 2, 1):
                block = chosen(row, step, pltpu.roll(block, size - step, 0), block)
            window_ref[slot, layer, part] = block[:width]

    def put_back(slot, layer):
        row = row_ref[slot]
        pick = shift_pick((width, columns), col_ref[slot], 0)
        for part in range(2):
            block = jnp.concatenate([select(piece_ref[part], pick, 2), jnp.zeros((8, columns), F32)], axis=0)
            for step in (1, 2, 4):
                block = chosen(row, step, pltpu.roll(block, step, 0), block)
            for step in reversed(steps):
                space = jnp.zeros((step, columns), F32)
                block = chosen(row, step, jnp.concatenate([space, block], axis=0), jnp.concatenate([block, space], axis=0))
            total_ref[layer * 2 + part] += block.reshape(total_ref.shape[1:])

    lag_gather, lag_middle, lag_outer = 6, 10, 12

    def within(k, blocks, action):
        if isinstance(k, int):
            if 0 <= k < blocks:
                action(k)
        else:
            @pl.when((k >= 0) & (k < blocks))
            def _():
                action(k)

    def power_hook(q):
        within(q - lag_gather, BLOCKS, power_line.gather_inner)
        within(q - lag_middle, BLOCKS, power_line.spread_middle)
        within(q - lag_outer, BLOCKS, power_line.spread_outer)

    pair = lambda ref, *place: (ref[(*place, 0)], ref[(*place, 1)])
    each = range(local_modes)
    prop = lambda: pair(prop_ref)

    def forward_slot(slot, carry):
        @pl.when(slot > 0)
        def _():
            for layer in range(layers):
                cut_window(slot, layer)

        waves = [times(pair(probe_ref, mode), pair(window_ref, slot, 0)) for mode in each]
        spectra = transform(waves, left_ref, right_ref, 0)

        @pl.when(slot == 0)
        def _():
            for layer in range(1, layers):
                pass_halo(layer)

        q = slot * per_slot
        for h in range(per_slot // 2):
            power_hook(q + h)
        moved = transform([times(prop(), field) for field in spectra], left_ref, right_ref, 1)
        for mode in each:
            for part in range(2):
                before_ref[slot, mode, part] = moved[mode][part]

        @pl.when(slot == 0)
        def _():
            finish_halo()

        for h in range(per_slot // 2, per_slot):
            power_hook(q + h)
        waves = [times(pair(before_ref, slot, mode), pair(window_ref, slot, 1)) for mode in each]
        far = transform(waves, left_ref, right_ref, 0)
        power = None
        for mode in each:
            for part in range(2):
                far_ref[slot, mode, part] = far[mode][part]
                here = far[mode][part] * far[mode][part]
                power = here if power is None else power + here
        for part in range(per_slot):
            part_power_ref[slot * per_slot + part] = power[part * slot_rows:(part + 1) * slot_rows]
        for part in range(per_slot):
            power_line.gather_outer(slot * per_slot + part)
        return carry

    pass_halo(0)
    take_halo(0)
    cut_window(0, 0)
    lax.fori_loop(0, slots, forward_slot, 0)
    hooks = [BLOCKS]

    def next_power_hook():
        power_hook(hooks[0])
        hooks[0] += 1

    def add_up(fields):
        for part in range(2):
            total = fields[0][part]
            for field in fields[1:]:
                total = total + field[part]
            piece_ref[part] = total

    def first_back(slot, hook):
        live = jnp.where(jnp.full((width, width), count_ref[0], jnp.int32) > slot, 1.0 / modes, 0.0)
        power = power_ref[slot * per_slot:(slot + 1) * per_slot].reshape(width, width)
        weight = (power - target_ref[slot]) * live
        waves = [(weight * far_ref[slot, mode, 0], weight * far_ref[slot, mode, 1]) for mode in each]
        back = transform(waves, left_ref, right_ref, 1)
        add_up([times_conj(pair(before_ref, slot, mode), back[mode]) for mode in each])
        for mode in each:
            for part in range(2):
                far_ref[slot, mode, part] = back[mode][part]
        for _ in range(per_slot // 2):
            hook()
        put_back(slot, 1)

    def second_back(slot, hook):
        waves = [times_conj(pair(window_ref, slot, 1), pair(far_ref, slot, mode)) for mode in each]
        inner = transform(waves, left_ref, right_ref, 0)
        for _ in range(per_slot - 1):
            hook()
        back = transform([times_conj(prop(), field) for field in inner], left_ref, right_ref, 1)
        add_up([times_conj(pair(probe_ref, mode), back[mode]) for mode in each])
        for mode in each:
            grad = times_conj(pair(window_ref, slot, 0), back[mode])
            for part in range(2):
                flat = mode * 2 + part
                first = flat % local_modes * width
                probe_grad_ref[flat // local_modes, first:first + width, :] += grad[part]
        for _ in range(per_slot - 1):
            hook()
        put_back(slot, 0)

    def ready(slot):
        while hooks[0] <= (slot + 1) * per_slot - 1 + lag_outer:
            next_power_hook()

    no_hook = lambda: None
    for slot in range(slots - 1):
        ready(slot)
        first_back(slot, no_hook)
    while hooks[0] < BLOCKS + lag_middle:
        next_power_hook()
    early = min(1, slots - 1)
    for slot in range(early):
        second_back(slot, no_hook)
    ready(slots - 1)
    first_back(slots - 1, no_hook)
    while hooks[0] < BLOCKS + lag_outer:
        next_power_hook()

    def send_rim(layer):
        @pl.when(has_next)
        def _():
            def one(k, carry):
                rim_copy(layer * per_layer + k).start()
                return carry
            lax.fori_loop(0, per_layer, one, 0)

    def add_rim(k):
        @pl.when(has_last)
        def _():
            rim_copy(k).wait_recv()
            total_ref[k // per_part, k % per_part] += rim_in_ref[k]

    def gather_outer(k):
        add_rim(stored(k))
        line.gather_outer(stored(k))

    line_lags = ((1, gather_outer), (7, lambda k: line.gather_inner(stored(k))),
                 (13, lambda k: line.spread_middle(stored(k))), (18, lambda k: line.spread_outer(stored(k))))
    end = LINE_BLOCKS + 18

    def line_hook(h):
        for lag, action in line_lags:
            within(h - lag, LINE_BLOCKS, action)

    hooks = [0]

    def next_line_hook():
        if hooks[0] < per_layer:
            line_hook(hooks[0])
            hooks[0] += 1

    def line_hooks(number):
        number = min(number, end - hooks[0])

        def one(i, carry):
            line_hook(i)
            return carry
        lax.fori_loop(hooks[0], hooks[0] + number, one, 0)
        hooks[0] += number

    def reduce_probe(bit):
        exchange(bit).wait_recv()
        part_ref[bit] = (probe_grad_ref[side] if bit == 0 else part_ref[bit - 1]) + got_ref[bit]
        exchange(bit + 1).start()

    for layer in range(layers - 1, 0, -1):
        send_rim(layer)
    for slot in range(early, slots):
        second_back(slot, next_line_hook)
    exchange(0).start()
    send_rim(0)
    line_hooks(2)
    reduce_probe(0)
    for bit in range(1, bits):
        line_hooks((end - 6 - hooks[0]) // (bits - bit))
        reduce_probe(bit)
    line_hooks(end)
    probe_out_ref[side] = part_ref[bits - 1]
    exchange(bits).wait_recv()
    for step in range(bits + 1):
        exchange(step).wait_send()
    power_line.drain()
    line.drain()

    @pl.when(has_next)
    def _():
        def sent(k, carry):
            rim_copy(k).wait_send()
            return carry
        lax.fori_loop(0, LINE_BLOCKS, sent, 0)

    end_halo()


def per_device(object_field, probe, measured, prop_phase, counts, row_offset, col_offset):
    layers, _, tile_rows, columns = object_field.shape
    width = probe.shape[-1]
    local_modes = probe.shape[0]
    slots = row_offset.shape[0]
    bits = lax.axis_size("tile").bit_length() - 1
    left, right = (jnp.asarray(table) for table in dft_constants(width))
    smem = pl.BlockSpec(memory_space=pltpu.SMEM)
    field = pltpu.VMEM((slots, local_modes, 2, width, width), F32)
    power = pltpu.VMEM((BLOCKS, slots * width // BLOCKS, width), F32)
    own_blocks = (LINE_BLOCKS, layers * 2 * tile_rows // LINE_BLOCKS, columns)
    block = pltpu.VMEM(own_blocks, F32)
    ext = pltpu.VMEM((layers, 2, tile_rows + width, columns), F32)
    halves = (2, local_modes * width, width)
    parts = pltpu.VMEM((bits, *halves[1:]), F32)
    dma = pltpu.SemaphoreType.DMA
    object_grad, probe_grad = pl.pallas_call(
        ptycho_kernel,
        out_shape=(jax.ShapeDtypeStruct(own_blocks, F32), jax.ShapeDtypeStruct(halves, F32)),
        in_specs=[smem] * 3 + [pl.BlockSpec(memory_space=pl.ANY)] * 6,
        out_specs=(VMEM_SPEC, VMEM_SPEC),
        scratch_shapes=[
            pltpu.VMEM(probe.shape, F32), pltpu.VMEM((width, width), F32), pltpu.VMEM(measured.shape, F32),
            pltpu.VMEM(left.shape, BF16), pltpu.VMEM(right.shape, BF16),
            ext, pltpu.VMEM((2, width, width), F32), pltpu.VMEM((slots, width, width), F32),
            pltpu.VMEM((slots, layers, 2, width, width), F32), field, field, power, power,
            power, power, power, pltpu.VMEM((2, width, width), F32),
            pltpu.VMEM((layers * 2, (tile_rows + width) // own_blocks[1], *own_blocks[1:]), F32), pltpu.VMEM(halves, F32),
            block, block, block, block, parts, parts,
            dma((6,)), dma((3, layers, 2, 2, PIECES)), dma((4, BLOCKS)), dma((4, LINE_BLOCKS)), dma((2, LINE_BLOCKS)), dma((2, bits + 1))],
        compiler_params=pltpu.CompilerParams(collective_id=0, has_side_effects=True, vmem_limit_bytes=62 << 20),
        name="ptycho",
    )(counts, row_offset, col_offset, object_field, probe, prop_phase, measured, left, right)
    return object_grad.reshape(object_field.shape), probe_grad.reshape(probe.shape)


def solution(mesh):
    placed = (
        P(None, None, "tile", None),
        P("mode", None, None, None),
        P("tile", None, None),
        P(),
        P("tile"),
        P("tile"),
        P("tile"),
    )
    return jax.shard_map(
        per_device,
        mesh=mesh,
        in_specs=placed,
        out_specs=(P(None, None, "tile", None), P("mode", None, None, None)),
        check_vma=False,
    )
```

```python
import functools
import math

import jax
import jax.numpy as jnp
import numpy as np
from jax import lax
from jax.experimental import pallas as pl
from jax.experimental.pallas import tpu as pltpu
from jax.sharding import PartitionSpec as P

F32 = jnp.float32
BF16 = jnp.bfloat16
MESH = pl.DeviceIdType.MESH
BLOCKS = 16
LINE_BLOCKS = 32
PIECES = 2
VMEM_SPEC = pl.BlockSpec(memory_space=pltpu.VMEM)


def shifted(block, axis, distance):
    devices = range(lax.axis_size(axis))
    route = [(i - distance, i) for i in devices if i - distance in devices]
    return lax.ppermute(block, axis, route)


def dft_constants(length):
    half = length // 2
    n, k = np.arange(half)[:, None], np.arange(half)[None, :]
    sides = []
    for side in ("left", "right"):
        for way in range(2):
            for parity in range(2):
                angle = (n * (2 * k + parity) % length) * (2.0 * math.pi / length)
                real = np.cos(angle) / math.sqrt(length)
                imag = (-np.sin(angle) if way == 0 else np.sin(angle)) / math.sqrt(length)
                if (side == "left") == (way == 0):
                    real, imag = real.T, imag.T
                if side == "left":
                    table = np.block([[real, -imag], [imag, real]])
                else:
                    table = np.block([[real, imag], [-imag, real]])
                high = table.astype(BF16)
                sides += [high, (table - high.astype(np.float64)).astype(BF16)]
    tables = np.stack(sides).reshape(2, 2, 2, 2, length, length)
    left, right = ([[[table[0], table[0], table[1]] for table in way] for way in side] for side in tables)
    return (np.stack([[np.concatenate(table, axis=1) for table in way] for way in left]),
            np.stack([[np.concatenate(table, axis=0) for table in way] for way in right]))


def split(x, axis):
    high = x.astype(BF16)
    low = (x - high.astype(F32)).astype(BF16)
    return jnp.concatenate([high, low, high], axis=axis)


def one_side(fields, product, axis, way):
    size = fields[0][0].shape[axis]
    half = size // 2
    first = lambda x: lax.slice_in_dim(x, 0, half, axis=axis)
    second = lambda x: lax.slice_in_dim(x, half, size, axis=axis)
    join = lambda x, y: jnp.concatenate([x, y], axis=axis)
    beside = lambda blocks: jnp.concatenate(blocks, axis=1 - axis)
    if way == 0:
        even = [join(first(x) + second(x), first(y) + second(y)) for x, y in fields]
        odd = [join(first(x) - second(x), first(y) - second(y)) for x, y in fields]
    else:
        even = [join(first(x), first(y)) for x, y in fields]
        odd = [join(second(x), second(y)) for x, y in fields]
    even = product(split(beside(even), axis), 0)
    odd = product(split(beside(odd), axis), 1)
    if way == 1:
        even, odd = even + odd, even - odd
    results = []
    for i in range(len(fields)):
        cut = lambda x: lax.slice_in_dim(x, i * size, (i + 1) * size, axis=1 - axis)
        results.append((join(first(cut(even)), first(cut(odd))), join(second(cut(even)), second(cut(odd)))))
    return results


def transform(fields, left_ref, right_ref, way):
    on_left = lambda x, parity: jnp.dot(left_ref[way, parity], x, preferred_element_type=F32)
    on_right = lambda x, parity: jnp.dot(x, right_ref[way, parity], preferred_element_type=F32)
    return one_side(one_side(fields, on_left, 0, way), on_right, 1, way)


def times(a, b):
    return a[0] * b[0] - a[1] * b[1], a[0] * b[1] + a[1] * b[0]


def times_conj(a, b):
    return a[0] * b[0] + a[1] * b[1], a[0] * b[1] - a[1] * b[0]


def one_hot(condition):
    return jnp.where(condition, 1.0, 0.0).astype(BF16)


def shift_pick(shape, offset, axis):
    here = lax.broadcasted_iota(jnp.int32, shape, axis) + offset
    return one_hot(here == lax.broadcasted_iota(jnp.int32, shape, 1 - axis))


def pieces(x, number):
    parts = []
    for _ in range(number):
        parts.append(x.astype(BF16))
        x = x - parts[-1].astype(F32)
    return parts


def select(x, pick, number):
    total = None
    for piece in pieces(x, number):
        part = jnp.dot(piece, pick, preferred_element_type=F32)
        total = part if total is None else total + part
    return total


def to_even_odd(field):
    n = field.shape[-1]
    source = lax.broadcasted_iota(jnp.int32, (n, n), 0)
    place = lax.broadcasted_iota(jnp.int32, (n, n), 1)
    half = n // 2
    pick_right = one_hot(source == jnp.where(place < half, 2 * place, 2 * place - (n - 1)))
    pick_left = one_hot(place == jnp.where(source < half, 2 * source, 2 * source - (n - 1)))
    rows = None
    for piece in pieces(field, 3):
        part = jnp.dot(pick_left, piece, preferred_element_type=F32)
        rows = part if rows is None else rows + part
    return select(rows, pick_right, 3)


class Line:
    def __init__(self, own, out_ref, up_ref, down_ref, send_ref, sems):
        self.own, self.out, self.up, self.down, self.send = own, out_ref, up_ref, down_ref, send_ref
        self.sems = sems
        self.n = lax.axis_size("mode")
        self.blocks = out_ref.shape[0]
        place = lax.axis_index("mode")
        left = place < self.n // 2
        self.depth = jnp.where(left, place, self.n - 1 - place)
        self.inward = jnp.where(left, place + 1, place - 1)
        self.outward = jnp.where(left, place - 1, place + 1)
        self.middle = self.depth == self.n // 2 - 1
        self.inner = self.depth > 0

    def copy(self, source, target, sent, received, device, k):
        return pltpu.make_async_remote_copy(
            src_ref=source.at[k], dst_ref=target.at[k],
            send_sem=self.sems.at[sent, k], recv_sem=self.sems.at[received, k],
            device_id={"mode": device}, device_id_type=MESH)

    def in_up(self, k):
        return self.copy(self.send, self.up, 0, 2, self.inward, k)

    def in_across(self, k):
        return self.copy(self.send, self.down, 0, 3, self.inward, k)

    def out_down(self, k):
        return self.copy(self.out, self.out, 1, 3, self.outward, k)

    def greet(self, barrier):
        pl.semaphore_signal(barrier, inc=1, device_id={"mode": self.inward}, device_id_type=MESH)

        @pl.when(self.inner)
        def _():
            pl.semaphore_signal(barrier, inc=1, device_id={"mode": self.outward}, device_id_type=MESH)

        return jnp.where(self.inner, 2, 1)

    def forward(self, k):
        @pl.when(self.middle)
        def _():
            self.in_across(k).start()

        @pl.when(jnp.logical_not(self.middle))
        def _():
            self.in_up(k).start()

    def gather_outer(self, k):
        @pl.when(jnp.logical_not(self.inner))
        def _():
            self.send[k] = self.own(k)
            self.forward(k)

    def gather_inner(self, k):
        @pl.when(self.inner)
        def _():
            self.in_up(k).wait_recv()
            self.send[k] = self.own(k) + self.up[k]
            self.forward(k)

    def spread_middle(self, k):
        @pl.when(self.middle)
        def _():
            self.in_across(k).wait_recv()
            self.out[k] = self.send[k] + self.down[k]

            @pl.when(self.inner)
            def _():
                self.out_down(k).start()

    def spread_outer(self, k):
        @pl.when(jnp.logical_not(self.middle))
        def _():
            self.in_across(k).wait_recv()

            @pl.when(self.inner)
            def _():
                self.out_down(k).start()

    def drain(self):
        def one(k, carry):
            self.in_up(k).wait_send()

            @pl.when(self.inner)
            def _():
                self.out_down(k).wait_send()
            return carry
        lax.fori_loop(0, self.blocks, one, 0)


def ptycho_kernel(count_ref, row_ref, col_ref, own_ref, probe_in_ref, phase_in_ref, measured_in_ref, left_in_ref, right_in_ref,
                  out_ref, probe_out_ref,
                  probe_ref, phase_ref, measured_ref, left_ref, right_ref, ext_ref, prop_ref, target_ref, window_ref, before_ref, far_ref, part_power_ref, power_ref,
                  power_up_ref, power_down_ref, power_send_ref, piece_ref, total_ref, probe_grad_ref,
                  up_ref, down_ref, send_ref, rim_in_ref, part_ref, got_ref,
                  fetch_sems, halo_sems, power_sems, sems, rim_sems, probe_sems):
    tiles = lax.axis_size("tile")
    me = lax.axis_index("tile")
    bits = tiles.bit_length() - 1
    has_next, has_last = me < tiles - 1, me > 0
    slots, layers = window_ref.shape[0], window_ref.shape[1]
    local_modes = probe_ref.shape[0]
    modes = local_modes * lax.axis_size("mode")
    width = probe_ref.shape[-1]
    tile_rows, columns = own_ref.shape[2:]
    per_slot = BLOCKS // slots
    slot_rows = width // per_slot
    per_layer = LINE_BLOCKS // layers
    per_part = per_layer // 2

    def stored(k):
        return (layers - 1 - k // per_layer) * per_layer + k % per_layer

    plane = lax.axis_index("mode")
    odd = lax.rem(plane, 2)
    partner = plane + 1 - 2 * odd
    near = lax.rem(me, 2)
    piece_rows = width // (2 * PIECES)

    def rows_of(half, piece):
        return pl.multiple_of((half * PIECES + piece) * piece_rows, 8)

    def region(layer, part, half, piece):
        return ext_ref.at[layer, part, pl.ds(tile_rows + rows_of(half, piece), piece_rows)]

    def halo(layer, part, half, piece):
        return pltpu.make_async_remote_copy(
            src_ref=own_ref.at[layer, part, pl.ds(rows_of(half, piece), piece_rows)],
            dst_ref=region(layer, part, half, piece),
            send_sem=halo_sems.at[0, layer, part, half, piece], recv_sem=halo_sems.at[1, layer, part, half, piece],
            device_id={"tile": me - 1}, device_id_type=MESH)

    def hand_over(layer, part, half, piece):
        return pltpu.make_async_remote_copy(
            src_ref=region(layer, part, half, piece), dst_ref=region(layer, part, half, piece),
            send_sem=halo_sems.at[2, layer, part, half, piece], recv_sem=halo_sems.at[1, layer, part, half, piece],
            device_id={"mode": partner}, device_id_type=MESH)

    def each_piece(layer, halves, action):
        for part in range(2):
            for piece in range(PIECES):
                for half in halves:
                    action(layer, part, half, piece)

    def start_halo():
        for layer in range(layers):
            @pl.when(has_last & (near == 1))
            def _():
                each_piece(layer, (0, 1), lambda *which: halo(*which).start())

            @pl.when(has_last & (near == 0))
            def _():
                each_piece(layer, (odd,), lambda *which: halo(*which).start())

    def pass_halo(layer):
        def one(*which):
            halo(*which).wait_recv()
            hand_over(*which).start()

        @pl.when(has_next & (near == 1))
        def _():
            each_piece(layer, (odd,), one)

    def take_halo(layer):
        @pl.when(has_next & (near == 0))
        def _():
            each_piece(layer, (0, 1), lambda *which: halo(*which).wait_recv())

        @pl.when(has_next & (near == 1))
        def _():
            each_piece(layer, (1 - odd,), lambda *which: halo(*which).wait_recv())

    def end_halo():
        for layer in range(layers):
            @pl.when(has_last & (near == 1))
            def _():
                each_piece(layer, (0, 1), lambda *which: halo(*which).wait_send())

            @pl.when(has_last & (near == 0))
            def _():
                each_piece(layer, (odd,), lambda *which: halo(*which).wait_send())

            @pl.when(has_next & (near == 1))
            def _():
                each_piece(layer, (odd,), lambda *which: hand_over(*which).wait_send())

    def finish_halo():
        for layer in range(1, layers):
            take_halo(layer)
            cut_window(0, layer)

    def rim_copy(k):
        return pltpu.make_async_remote_copy(
            src_ref=total_ref.at[k // per_part, per_part + k % per_part], dst_ref=rim_in_ref.at[k],
            send_sem=rim_sems.at[0, k], recv_sem=rim_sems.at[1, k],
            device_id={"tile": me + 1}, device_id_type=MESH)

    def other(step):
        bit = step and bits - step
        low = lax.rem(me // (1 << bit), 2)
        return me + (1 - 2 * low) * (1 << bit)

    side = lax.rem(me, 2)

    def probe_copy(step, source, target):
        return pltpu.make_async_remote_copy(
            src_ref=source, dst_ref=target,
            send_sem=probe_sems.at[0, step], recv_sem=probe_sems.at[1, step],
            device_id={"tile": other(0 if step == bits else step)}, device_id_type=MESH)

    def exchange(step):
        if step == 0:
            return probe_copy(0, probe_grad_ref.at[1 - side], got_ref.at[0])
        if step < bits:
            return probe_copy(step, part_ref.at[step - 1], got_ref.at[step])
        return probe_copy(step, part_ref.at[bits - 1], probe_out_ref.at[side])

    power_line = Line(lambda k: part_power_ref[k], power_ref, power_up_ref, power_down_ref, power_send_ref, power_sems)

    def own(k):
        return total_ref[k // per_part, k % per_part]

    line = Line(own, out_ref, up_ref, down_ref, send_ref, sems)

    def fetch(number):
        source, target = ((phase_in_ref, phase_ref), (measured_in_ref, measured_ref), (own_ref, ext_ref.at[:, :, pl.ds(0, tile_rows)]),
                          (left_in_ref, left_ref), (right_in_ref, right_ref), (probe_in_ref, probe_ref))[number]
        return pltpu.make_async_copy(source, target, fetch_sems.at[number])

    for number in range(6):
        fetch(number).start()
    barrier = pltpu.get_barrier_semaphore()
    count = line.greet(barrier)
    for bit in range(bits):
        pl.semaphore_signal(barrier, inc=1, device_id={"tile": other(bit)}, device_id_type=MESH)

    @pl.when(has_next)
    def _():
        pl.semaphore_signal(barrier, inc=1, device_id={"tile": me + 1}, device_id_type=MESH)

    @pl.when(has_last)
    def _():
        pl.semaphore_signal(barrier, inc=1, device_id={"tile": me - 1}, device_id_type=MESH)

    pl.semaphore_wait(barrier, count + bits + has_next.astype(jnp.int32) + has_last.astype(jnp.int32))

    start_halo()

    @pl.when(jnp.logical_not(has_next))
    def _():
        ext_ref[:, :, tile_rows:, :] = jnp.zeros((layers, 2, width, columns), F32)

    total_ref[...] = jnp.zeros_like(total_ref)
    probe_grad_ref[...] = jnp.zeros_like(probe_grad_ref)
    fetch(0).wait()
    phase = to_even_odd(phase_ref[...])
    prop_ref[0] = jnp.cos(phase)
    prop_ref[1] = jnp.sin(phase)
    fetch(1).wait()

    def order(slot, carry):
        target_ref[slot] = to_even_odd(measured_ref[slot])
        return carry
    lax.fori_loop(0, slots, order, 0)
    for number in range(2, 6):
        fetch(number).wait()

    def chosen(amount, bit, yes, no):
        return jnp.where(jnp.full(yes.shape, amount & bit, jnp.int32) > 0, yes, no)

    steps = [1 << level for level in reversed(range(3, (tile_rows - 1).bit_length()))]

    def cut_window(slot, layer):
        row = row_ref[slot]
        pick = shift_pick((columns, width), col_ref[slot], 1)
        for part in range(2):
            block = select(ext_ref[layer, part], pick, 2)
            for step in steps:
                size = block.shape[0] - step
                block = chosen(row, step, block[step:], block[:size])
            size = block.shape[0]
            for step in (4, 2, 1):
                block = chosen(row, step, pltpu.roll(block, size - step, 0), block)
            window_ref[slot, layer, part] = block[:width]

    def put_back(slot, layer):
        row = row_ref[slot]
        pick = shift_pick((width, columns), col_ref[slot], 0)
        for part in range(2):
            block = jnp.concatenate([select(piece_ref[part], pick, 2), jnp.zeros((8, columns), F32)], axis=0)
            for step in (1, 2, 4):
                block = chosen(row, step, pltpu.roll(block, step, 0), block)
            for step in reversed(steps):
                space = jnp.zeros((step, columns), F32)
                block = chosen(row, step, jnp.concatenate([space, block], axis=0), jnp.concatenate([block, space], axis=0))
            total_ref[layer * 2 + part] += block.reshape(total_ref.shape[1:])

    lag_gather, lag_middle, lag_outer = 6, 10, 12

    def within(k, blocks, action):
        if isinstance(k, int):
            if 0 <= k < blocks:
                action(k)
        else:
            @pl.when((k >= 0) & (k < blocks))
            def _():
                action(k)

    def power_hook(q):
        within(q - lag_gather, BLOCKS, power_line.gather_inner)
        within(q - lag_middle, BLOCKS, power_line.spread_middle)
        within(q - lag_outer, BLOCKS, power_line.spread_outer)

    pair = lambda ref, *place: (ref[(*place, 0)], ref[(*place, 1)])
    each = range(local_modes)
    prop = lambda: pair(prop_ref)

    def forward_slot(slot, carry):
        @pl.when(slot > 0)
        def _():
            for layer in range(layers):
                cut_window(slot, layer)

        waves = [times(pair(probe_ref, mode), pair(window_ref, slot, 0)) for mode in each]
        spectra = transform(waves, left_ref, right_ref, 0)

        @pl.when(slot == 0)
        def _():
            for layer in range(1, layers):
                pass_halo(layer)

        q = slot * per_slot
        for h in range(per_slot // 2):
            power_hook(q + h)
        moved = transform([times(prop(), field) for field in spectra], left_ref, right_ref, 1)
        for mode in each:
            for part in range(2):
                before_ref[slot, mode, part] = moved[mode][part]

        @pl.when(slot == 0)
        def _():
            finish_halo()

        for h in range(per_slot // 2, per_slot):
            power_hook(q + h)
        waves = [times(pair(before_ref, slot, mode), pair(window_ref, slot, 1)) for mode in each]
        far = transform(waves, left_ref, right_ref, 0)
        power = None
        for mode in each:
            for part in range(2):
                far_ref[slot, mode, part] = far[mode][part]
                here = far[mode][part] * far[mode][part]
                power = here if power is None else power + here
        for part in range(per_slot):
            part_power_ref[slot * per_slot + part] = power[part * slot_rows:(part + 1) * slot_rows]
        for part in range(per_slot):
            power_line.gather_outer(slot * per_slot + part)
        return carry

    pass_halo(0)
    take_halo(0)
    cut_window(0, 0)
    lax.fori_loop(0, slots, forward_slot, 0)
    hooks = [BLOCKS]

    def next_power_hook():
        power_hook(hooks[0])
        hooks[0] += 1

    def add_up(fields):
        for part in range(2):
            total = fields[0][part]
            for field in fields[1:]:
                total = total + field[part]
            piece_ref[part] = total

    def first_back(slot, hook):
        live = jnp.where(jnp.full((width, width), count_ref[0], jnp.int32) > slot, 1.0 / modes, 0.0)
        power = power_ref[slot * per_slot:(slot + 1) * per_slot].reshape(width, width)
        weight = (power - target_ref[slot]) * live
        waves = [(weight * far_ref[slot, mode, 0], weight * far_ref[slot, mode, 1]) for mode in each]
        back = transform(waves, left_ref, right_ref, 1)
        add_up([times_conj(pair(before_ref, slot, mode), back[mode]) for mode in each])
        for mode in each:
            for part in range(2):
                far_ref[slot, mode, part] = back[mode][part]
        for _ in range(per_slot // 2):
            hook()
        put_back(slot, 1)

    def second_back(slot, hook):
        waves = [times_conj(pair(window_ref, slot, 1), pair(far_ref, slot, mode)) for mode in each]
        inner = transform(waves, left_ref, right_ref, 0)
        for _ in range(per_slot - 1):
            hook()
        back = transform([times_conj(prop(), field) for field in inner], left_ref, right_ref, 1)
        add_up([times_conj(pair(probe_ref, mode), back[mode]) for mode in each])
        for mode in each:
            grad = times_conj(pair(window_ref, slot, 0), back[mode])
            for part in range(2):
                flat = mode * 2 + part
                first = flat % local_modes * width
                probe_grad_ref[flat // local_modes, first:first + width, :] += grad[part]
        for _ in range(per_slot - 1):
            hook()
        put_back(slot, 0)

    def ready(slot):
        while hooks[0] <= (slot + 1) * per_slot - 1 + lag_outer:
            next_power_hook()

    no_hook = lambda: None
    for slot in range(slots - 1):
        ready(slot)
        first_back(slot, no_hook)
    while hooks[0] < BLOCKS + lag_middle:
        next_power_hook()
    early = min(1, slots - 1)
    for slot in range(early):
        second_back(slot, no_hook)
    ready(slots - 1)
    first_back(slots - 1, no_hook)
    while hooks[0] < BLOCKS + lag_outer:
        next_power_hook()

    def send_rim(layer):
        @pl.when(has_next)
        def _():
            def one(k, carry):
                rim_copy(layer * per_layer + k).start()
                return carry
            lax.fori_loop(0, per_layer, one, 0)

    def add_rim(k):
        @pl.when(has_last)
        def _():
            rim_copy(k).wait_recv()
            total_ref[k // per_part, k % per_part] += rim_in_ref[k]

    def gather_outer(k):
        add_rim(stored(k))
        line.gather_outer(stored(k))

    line_lags = ((1, gather_outer), (9, lambda k: line.gather_inner(stored(k))),
                 (17, lambda k: line.spread_middle(stored(k))), (24, lambda k: line.spread_outer(stored(k))))
    end = LINE_BLOCKS + 24

    def line_hook(h):
        for lag, action in line_lags:
            within(h - lag, LINE_BLOCKS, action)

    hooks = [0]

    def next_line_hook():
        if hooks[0] < per_layer:
            line_hook(hooks[0])
            hooks[0] += 1

    def line_hooks(number):
        number = min(number, end - hooks[0])

        def one(i, carry):
            line_hook(i)
            return carry
        lax.fori_loop(hooks[0], hooks[0] + number, one, 0)
        hooks[0] += number

    def reduce_probe(bit):
        exchange(bit).wait_recv()
        part_ref[bit] = (probe_grad_ref[side] if bit == 0 else part_ref[bit - 1]) + got_ref[bit]
        exchange(bit + 1).start()

    for layer in range(layers - 1, 0, -1):
        send_rim(layer)
    for slot in range(early, slots):
        second_back(slot, next_line_hook)
    exchange(0).start()
    send_rim(0)
    line_hooks(2)
    reduce_probe(0)
    for bit in range(1, bits):
        line_hooks((end - 6 - hooks[0]) // (bits - bit))
        reduce_probe(bit)
    line_hooks(end)
    probe_out_ref[side] = part_ref[bits - 1]
    exchange(bits).wait_recv()
    for step in range(bits + 1):
        exchange(step).wait_send()
    power_line.drain()
    line.drain()

    @pl.when(has_next)
    def _():
        def sent(k, carry):
            rim_copy(k).wait_send()
            return carry
        lax.fori_loop(0, LINE_BLOCKS, sent, 0)

    end_halo()


def per_device(object_field, probe, measured, prop_phase, counts, row_offset, col_offset):
    layers, _, tile_rows, columns = object_field.shape
    width = probe.shape[-1]
    local_modes = probe.shape[0]
    slots = row_offset.shape[0]
    bits = lax.axis_size("tile").bit_length() - 1
    left, right = (jnp.asarray(table) for table in dft_constants(width))
    smem = pl.BlockSpec(memory_space=pltpu.SMEM)
    field = pltpu.VMEM((slots, local_modes, 2, width, width), F32)
    power = pltpu.VMEM((BLOCKS, slots * width // BLOCKS, width), F32)
    own_blocks = (LINE_BLOCKS, layers * 2 * tile_rows // LINE_BLOCKS, columns)
    block = pltpu.VMEM(own_blocks, F32)
    ext = pltpu.VMEM((layers, 2, tile_rows + width, columns), F32)
    halves = (2, local_modes * width, width)
    parts = pltpu.VMEM((bits, *halves[1:]), F32)
    dma = pltpu.SemaphoreType.DMA
    object_grad, probe_grad = pl.pallas_call(
        ptycho_kernel,
        out_shape=(jax.ShapeDtypeStruct(own_blocks, F32), jax.ShapeDtypeStruct(halves, F32)),
        in_specs=[smem] * 3 + [pl.BlockSpec(memory_space=pl.ANY)] * 6,
        out_specs=(VMEM_SPEC, VMEM_SPEC),
        scratch_shapes=[
            pltpu.VMEM(probe.shape, F32), pltpu.VMEM((width, width), F32), pltpu.VMEM(measured.shape, F32),
            pltpu.VMEM(left.shape, BF16), pltpu.VMEM(right.shape, BF16),
            ext, pltpu.VMEM((2, width, width), F32), pltpu.VMEM((slots, width, width), F32),
            pltpu.VMEM((slots, layers, 2, width, width), F32), field, field, power, power,
            power, power, power, pltpu.VMEM((2, width, width), F32),
            pltpu.VMEM((layers * 2, (tile_rows + width) // own_blocks[1], *own_blocks[1:]), F32), pltpu.VMEM(halves, F32),
            block, block, block, block, parts, parts,
            dma((6,)), dma((3, layers, 2, 2, PIECES)), dma((4, BLOCKS)), dma((4, LINE_BLOCKS)), dma((2, LINE_BLOCKS)), dma((2, bits + 1))],
        compiler_params=pltpu.CompilerParams(collective_id=0, has_side_effects=True, vmem_limit_bytes=62 << 20),
        name="ptycho",
    )(counts, row_offset, col_offset, object_field, probe, prop_phase, measured, left, right)
    return object_grad.reshape(object_field.shape), probe_grad.reshape(probe.shape)


def solution(mesh):
    placed = (
        P(None, None, "tile", None),
        P("mode", None, None, None),
        P("tile", None, None),
        P(),
        P("tile"),
        P("tile"),
        P("tile"),
    )
    return jax.shard_map(
        per_device,
        mesh=mesh,
        in_specs=placed,
        out_specs=(P(None, None, "tile", None), P("mode", None, None, None)),
        check_vma=False,
    )
```
